128 devices in a mesh: slide: 4 (over z_hi, core), space: 32 (over y, x, z_lo).
Axes of the slice: x: 4, y: 4, z: 4 (z_hi: 2, z_lo: 2; z = z_hi * 2 + z_lo), core: 2. Of those that a mesh axis runs over, the one named last changes fastest.
Arguments:
- features: bfloat16 [4, 32, 8, 256, 192], P('slide', 'space'), may hold values from -16 to 16
- dw_kernel: float32 [7, 7, 192], replicated, may hold values from -1.3 to 1.3
- dw_bias: float32 [192], replicated, may hold values from -4 to 4
- ln_gain: float32 [192], replicated, may hold values from 0.5 to 1.5
- ln_bias: float32 [192], replicated, may hold values from -3 to 3
- w_in: bfloat16 [192, 768], replicated, may hold values from -0.4375 to 0.4375
- b_in: float32 [768], replicated, may hold values from -3 to 3
- w_out: bfloat16 [768, 192], replicated, may hold values from -0.21875 to 0.21875
- b_out: float32 [192], replicated, may hold values from -3 to 3
- layer_scale: float32 [192], replicated, may hold values from 0.5 to 1.5
- cotangent: bfloat16 [4, 32, 8, 256, 192], P('slide', 'space'), may hold values from -6 to 6
Outputs:
- block_output: bfloat16 [4, 32, 8, 256, 192], P('slide', 'space')
- grad_input: bfloat16 [4, 32, 8, 256, 192], P('slide', 'space')
- grad_w_in: float32 [192, 768], replicated
- grad_w_out: float32 [768, 192], replicated
- grad_kernel: float32 [7, 7, 192], replicated
The draws below stay inside these ranges and needn't reach their ends.
All inputs are finite; a program needn't handle non-finite values.
Results may differ from the reference program's by a relative error of at most 0.0068.
Values may be sent and summed in bfloat16 or wider, within the bound.
A program may use at most 64 MiB of HBM per device.

```python
import math
import jax
import jax.numpy as jnp
from jax import lax

C = 192
F = 768
TH = 8
TW = 256
TILES = 32
SLIDES = 4
PIXELS = 262144


def draw_features(key, part):
    shape = (SLIDES, TILES, TH, TW, C)
    first, second = jax.random.split(jax.random.fold_in(key, 11), 2)
    pixel_scale = jnp.exp(jax.random.uniform(second, (SLIDES, TILES, TH, TW, 1), jnp.float32, math.log(0.4), math.log(4.0)))
    values = jax.random.truncated_normal(first, -4.0, 4.0, shape, jnp.float32)
    return (values * pixel_scale).astype(jnp.bfloat16)


def draw_dw_kernel(key, part):
    first, second = jax.random.split(jax.random.fold_in(key, 23), 2)
    channel_scale = jnp.exp(jax.random.uniform(second, (1, 1, C), jnp.float32, math.log(0.3), math.log(3.0)))
    values = jax.random.truncated_normal(first, -3.0, 3.0, (7, 7, C), jnp.float32)
    return values * channel_scale / 7.0


def levels(stream_key, extent, cuts, least, high):
    gain, own = 1.0, jax.random.fold_in(stream_key, 6)
    for axis_at, shards_of in cuts:
        heights = jnp.exp(jax.random.uniform(jax.random.fold_in(own, axis_at), (shards_of,), jnp.float32, least / len(cuts), high / len(cuts)))
        gain = gain * jnp.repeat(heights, extent[axis_at] // shards_of).reshape([-1 if axis == axis_at else 1 for axis in range(len(extent))])
    return gain


def scatter_about(rng, extent, spread, most, cuts=(), dtype=jnp.bfloat16):
    values = spread * jax.random.normal(rng, extent, jnp.float32)
    if cuts:
        values = values * levels(rng, extent, cuts, -0.22, 0.18)
    return jnp.clip(values, -most, most).astype(dtype)


def setup_inputs(seed: int = 0) -> dict:
    splits = jax.random.split(jax.random.key(seed), 12)
    features = draw_features(jax.random.fold_in(splits[11], 71), 0)
    dw_kernel = draw_dw_kernel(jax.random.fold_in(splits[11], 71), 0)
    dw_bias = scatter_about(splits[2], (C,), 1.0, 4.0, (), jnp.float32)
    ln_gain = jnp.clip(jax.random.uniform(splits[3], (C,), jnp.float32, 0.5, 1.5), 0.5, 1.5)
    ln_bias = scatter_about(splits[4], (C,), 0.5, 3.0, (), jnp.float32)
    w_in = scatter_about(splits[5], (C, F), C ** -0.5, 0.4375)
    b_in = scatter_about(splits[6], (F,), 0.5, 3.0, (), jnp.float32)
    w_out = scatter_about(splits[7], (F, C), F ** -0.5, 0.21875)
    b_out = scatter_about(splits[8], (C,), 0.5, 3.0, (), jnp.float32)
    layer_scale = jnp.clip(jax.random.uniform(splits[9], (C,), jnp.float32, 0.5, 1.5), 0.5, 1.5)
    cotangent = scatter_about(splits[10], (SLIDES, TILES, TH, TW, C), 1.0, 6.0, ((0, 4), (1, 32)))
    return dict(features=features, dw_kernel=dw_kernel, dw_bias=dw_bias, ln_gain=ln_gain, ln_bias=ln_bias, w_in=w_in, b_in=b_in, w_out=w_out, b_out=b_out, layer_scale=layer_scale, cotangent=cotangent)


EPSILON = 1e-06

def gelu_slope(hidden):
    return 0.5 * (1.0 + lax.erf(hidden * 0.7071067811865476)) + hidden * jnp.exp(-0.5 * hidden * hidden) * 0.3989422804014327

def reference(features, dw_kernel, dw_bias, ln_gain, ln_bias, w_in, b_in, w_out, b_out, layer_scale, cotangent):
    chans = features.shape[4]
    strips, strip_rows, strip_cols = (features.shape[1], features.shape[2], features.shape[3])

    def one_slide(pair):
        image = pair[0].reshape(strips * strip_rows, strip_cols, chans).astype(jnp.float32)
        upstream = pair[1].reshape(strips * strip_rows, strip_cols, chans).astype(jnp.float32)
        height, width = (image.shape[0], image.shape[1])
        padded = jnp.pad(image, ((3, 3), (3, 3), (0, 0)))
        mixed = jnp.zeros((height, width, chans), jnp.float32) + dw_bias
        for row_off in range(7):
            for col_off in range(7):
                mixed = mixed + dw_kernel[row_off, col_off] * padded[row_off:row_off + height, col_off:col_off + width]
        flat = mixed.reshape(height * width, chans)
        centre = flat - lax.optimization_barrier(jnp.mean(flat, axis=1, keepdims=True))
        inverse = lax.rsqrt(lax.optimization_barrier(jnp.mean(centre * centre, axis=1, keepdims=True)) + EPSILON)
        unit = centre * inverse
        normed = (unit * ln_gain + ln_bias).astype(jnp.bfloat16)
        hidden = jnp.dot(normed, w_in, preferred_element_type=jnp.float32) + b_in
        act = jax.nn.gelu(hidden, approximate=False).astype(jnp.bfloat16)
        branch = jnp.dot(act, w_out, preferred_element_type=jnp.float32) + b_out
        result = (image.reshape(height * width, chans) + layer_scale * branch).astype(jnp.bfloat16)
        up_flat = upstream.reshape(height * width, chans)
        gout = (layer_scale * up_flat).astype(jnp.bfloat16)
        grad_act = jnp.dot(gout, w_out.T, preferred_element_type=jnp.float32)
        grad_hidden = (grad_act * gelu_slope(hidden)).astype(jnp.bfloat16)
        grad_norm = jnp.dot(grad_hidden, w_in.T, preferred_element_type=jnp.float32) * ln_gain
        grad_mixed = inverse * (grad_norm - lax.optimization_barrier(jnp.mean(grad_norm, axis=1, keepdims=True)) - unit * lax.optimization_barrier(jnp.mean(grad_norm * unit, axis=1, keepdims=True)))
        grad_mixed = grad_mixed.astype(jnp.bfloat16).reshape(height, width, chans)
        grad_wide = jnp.pad(grad_mixed.astype(jnp.float32), ((3, 3), (3, 3), (0, 0)))
        grad_image = upstream
        kernel_terms = []
        for row_off in range(7):
            for col_off in range(7):
                grad_image = grad_image + dw_kernel[row_off, col_off] * grad_wide[6 - row_off:6 - row_off + height, 6 - col_off:6 - col_off + width]
                kernel_terms.append(lax.optimization_barrier(jnp.sum(grad_wide[3:3 + height, 3:3 + width] * padded[row_off:row_off + height, col_off:col_off + width], axis=(0, 1))))
        grad_k = jnp.stack(kernel_terms).reshape(7, 7, chans)
        grad_wi = jnp.dot(normed.T, grad_hidden, preferred_element_type=jnp.float32)
        grad_wo = jnp.dot(act.T, gout, preferred_element_type=jnp.float32)
        out_tiles = result.reshape(strips, strip_rows, strip_cols, chans)
        grad_tiles = grad_image.astype(jnp.bfloat16).reshape(strips, strip_rows, strip_cols, chans)
        return (out_tiles, grad_tiles, grad_wi, grad_wo, grad_k)
    results = lax.map(one_slide, (features, cotangent))
    scale = jnp.float32(float(PIXELS) ** (-0.5))
    return (results[0], results[1], lax.optimization_barrier(jnp.sum(results[2], axis=0)) * scale, lax.optimization_barrier(jnp.sum(results[3], axis=0)) * scale, lax.optimization_barrier(jnp.sum(results[4], axis=0)) * scale)
```

```python
import jax
import jax.numpy as jnp
from jax import lax
from jax.experimental import pallas as pl
from jax.experimental.pallas import tpu as pltpu
from jax.sharding import PartitionSpec as P

EPSILON = 1e-06
F32 = jnp.float32
BF16 = jnp.bfloat16
MESH = pl.DeviceIdType.MESH
PIXEL_SCALE = float(262144) ** (-0.5)
TILES = 160
NT = (((1,), (1,)), ((), ()))


def remote(src, dst, send, recv, slide, space):
    return pltpu.make_async_remote_copy(
        src_ref=src, dst_ref=dst, send_sem=send, recv_sem=recv,
        device_id={"slide": slide, "space": space}, device_id_type=MESH,
    )


def gelu_parts(h):
    cdf = 0.5 * (1.0 + lax.erf(h * 0.7071067811865476))
    slope = cdf + h * jnp.exp(-0.5 * h * h) * 0.3989422804014327
    return h * cdf, slope


def lay_out(row, wide, packed, value):
    wide[row, 8:264, :] = value[:, :128]
    tail = value[:, 128:192]
    none = jnp.zeros((8, 64), F32)
    packed[row, 8:136, :] = jnp.concatenate([tail[:128], tail[128:]], axis=1)
    packed[row, 0:8, :] = jnp.concatenate([none, tail[120:128]], axis=1)
    packed[row, 136:144, :] = jnp.concatenate([tail[128:136], none], axis=1)


def conv_block(src, taps, start, flip):
    sums = [jnp.zeros((16, 128), F32) for _ in range(8)]
    for b in range(7):
        held = [taps[(6 - a) * 7 + (6 - b) if flip else a * 7 + b] for a in range(7)]
        held = [jnp.concatenate([k, k], axis=0) for k in held]
        for r in range(14):
            v = src[r, pl.ds(start + 5 + b, 16), :]
            for a in range(7):
                if 0 <= r - a < 8:
                    sums[r - a] = sums[r - a] + v * held[a]
    return sums


def kernel(
    feat, cot, dwk, dwb, gain, lbias, w_in, b_in, w_out, b_out, lscale,
    out_block, out_gin, out_gwi, out_gwoT, out_gk,
    fx, ct, xa, xb, ka, kb, za, zc, gza, gzb, par, win, wout, gout, goutT,
    nb, unit, inv, hid, gact, act, gh, outs, gzs, gwi, gwoT, gka, gkb, gia, gib,
    pay, r0, s1, r1, s2, r2, s3, r3, full, halo,
    in_sem, out_sem, halo_send, halo_recv, core_sem, x_send, x_recv, y_send, y_recv, z_send, z_recv,
):
    s, t = lax.axis_index("slide"), lax.axis_index("space")
    z_hi, core = s // 2, s % 2
    z_lo, x, y = t % 2, (t // 2) % 4, t // 8
    z = z_hi * 2 + z_lo
    partner = z_hi * 2 + (1 - core)
    x_peers = [(s, (y * 4 + (x + d) % 4) * 2 + z_lo) for d in (1, 2, 3)]
    y_peers = [(s, (((y + d) % 4) * 4 + x) * 2 + z_lo) for d in (1, 2, 3)]
    z_peers = [(((z + d) % 4) // 2 * 2 + core, (y * 4 + x) * 2 + ((z + d) % 4) % 2) for d in (1, 2, 3)]
    has_up, has_down = t > 0, t < 31
    up, down = jnp.maximum(t - 1, 0), jnp.minimum(t + 1, 31)

    barrier = pltpu.get_barrier_semaphore()
    for ps, pt in [(partner, t)] + x_peers + y_peers + z_peers:
        pl.semaphore_signal(barrier, inc=1, device_id={"slide": ps, "space": pt}, device_id_type=MESH)

    @pl.when(has_up)
    def _():
        pl.semaphore_signal(barrier, inc=1, device_id={"slide": s, "space": up}, device_id_type=MESH)

    @pl.when(has_down)
    def _():
        pl.semaphore_signal(barrier, inc=1, device_id={"slide": s, "space": down}, device_id_type=MESH)

    own_in = pltpu.make_async_copy(feat.at[0, 0], fx.at[pl.ds(3, 8)], in_sem.at[0])
    own_in.start()
    cot_in = pltpu.make_async_copy(cot.at[0, 0], ct, in_sem.at[1])
    cot_in.start()

    pl.semaphore_wait(barrier, 10 + jnp.minimum(t, 1) + jnp.minimum(31 - t, 1))

    to_up = remote(feat.at[0, 0, pl.ds(0, 3)], fx.at[pl.ds(11, 3)], halo_send.at[0], halo_recv.at[0], s, up)
    to_down = remote(feat.at[0, 0, pl.ds(5, 3)], fx.at[pl.ds(0, 3)], halo_send.at[1], halo_recv.at[1], s, down)

    @pl.when(has_up)
    def _():
        to_up.start()

    @pl.when(has_down)
    def _():
        to_down.start()

    par[...] = jnp.zeros_like(par)
    for n, ref in enumerate((dwb, gain, lbias, b_out, lscale)):
        par[n : n + 1, 0:192] = ref[...]
    win[0:192, :] = w_in[...]
    win[192:256, :] = jnp.zeros((64, 768), BF16)
    wout[:, 0:192] = w_out[...]
    wout[:, 192:256] = jnp.zeros((768, 64), BF16)
    for a in range(7):
        for b in range(7):
            k = dwk[a, b : b + 1, :]
            ka[a * 7 + b] = jnp.broadcast_to(k[:, 0:128], (8, 128))
            tail = k[:, 128:192]
            kb[a * 7 + b] = jnp.broadcast_to(jnp.concatenate([tail, tail], axis=1), (8, 128))

    def clear(r, _):
        zeros = jnp.zeros((8, 128), F32)
        for ref in (xa, gza):
            ref[r, 0:8, :] = zeros
            ref[r, 264:272, :] = zeros
        return 0

    lax.fori_loop(0, 14, clear, 0)
    gwi[...] = jnp.zeros_like(gwi)
    gwoT[...] = jnp.zeros_like(gwoT)
    gka[...] = jnp.zeros_like(gka)
    gkb[...] = jnp.zeros_like(gkb)

    cot_in.wait()

    def scale_row(i, _):
        g = (par[4:5, 0:192] * ct[i].astype(F32)).astype(BF16)
        gout[i, :, 0:192] = g
        gout[i, :, 192:256] = jnp.zeros((256, 64), BF16)
        goutT[i] = g.T
        return 0

    lax.fori_loop(0, 8, scale_row, 0)
    own_in.wait()

    @pl.when(has_up)
    def _():
        to_down.wait_recv()

    @pl.when(t == 0)
    def _():
        fx[0:3] = jnp.zeros((3, 256, 192), BF16)

    @pl.when(has_down)
    def _():
        to_up.wait_recv()

    @pl.when(t == 31)
    def _():
        fx[11:14] = jnp.zeros((3, 256, 192), BF16)

    def lay_row(r, _):
        lay_out(r, xa, xb, fx[r].astype(F32))
        return 0

    lax.fori_loop(0, 14, lay_row, 0)

    def conv_a(n, _):
        start = pl.multiple_of(n * 16, 16)
        sums = conv_block(xa, ka, start, False)
        for i in range(8):
            za[i, pl.ds(start, 16), :] = sums[i] + par[0:1, 0:128]
        return 0

    lax.fori_loop(0, 16, conv_a, 0)

    def conv_b(n, _):
        start = pl.multiple_of(n * 16, 16)
        sums = conv_block(xb, kb, start, False)
        lower = lax.broadcasted_iota(jnp.int32, (16, 128), 1) < 64
        for i in range(8):
            zc[i, pl.ds(start, 16), :] = jnp.where(lower, sums[i] + par[0:1, 128:256], 0.0)
            zc[i, pl.ds(start + 128, 16), :] = jnp.where(lower, pltpu.roll(sums[i], 64, 1) + par[0:1, 128:256], 0.0)
        return 0

    lax.fori_loop(0, 8, conv_b, 0)

    def mlp_row(i, _):
        def norm(q, _):
            px = pl.ds(pl.multiple_of(q * 64, 64), 64)
            a, c = za[i, px, :], zc[i, px, :]
            lower = lax.broadcasted_iota(jnp.int32, (64, 128), 1) < 64
            mean = jnp.sum(a + c, axis=1, keepdims=True) * (1.0 / 192)
            a = a - mean
            c = jnp.where(lower, c - mean, 0.0)
            var = jnp.sum(a * a + c * c, axis=1, keepdims=True) * (1.0 / 192)
            r = lax.rsqrt(var + EPSILON)
            a, c = a * r, c * r
            unit[px, 0:128] = a
            unit[px, 128:256] = c
            inv[px, :] = jnp.broadcast_to(r, (64, 128))
            nb[px, 0:128] = (a * par[1:2, 0:128] + par[2:3, 0:128]).astype(BF16)
            nb[px, 128:256] = (c * par[1:2, 128:256] + par[2:3, 128:256]).astype(BF16)
            return 0

        lax.fori_loop(0, 4, norm, 0)
        hid[...] = jnp.dot(nb[...], win[...], preferred_element_type=F32)
        gact[...] = lax.dot_general(gout[i], wout[...], NT, preferred_element_type=F32)

        def gelu(n, _):
            px = pl.ds(pl.multiple_of((n // 2) * 16, 16), 16)
            ln = pl.ds(pl.multiple_of((n % 2) * 384, 384), 384)
            h = hid[px, ln] + b_in[0:1, ln]
            value, slope = gelu_parts(h)
            act[px, ln] = value.astype(BF16)
            gh[px, ln] = (gact[px, ln] * slope).astype(BF16)
            return 0

        lax.fori_loop(0, 32, gelu, 0)
        hid[:, 0:256] = jnp.dot(act[...], wout[...], preferred_element_type=F32)
        hid[:, 256:512] = lax.dot_general(gh[...], win[...], NT, preferred_element_type=F32)
        gwi[...] += jnp.dot(nb[:, 0:192].T, gh[...], preferred_element_type=F32)
        gwoT[...] += jnp.dot(goutT[i], act[...], preferred_element_type=F32)

        def finish(q, _):
            px = pl.ds(pl.multiple_of(q * 64, 64), 64)
            branch = (hid[px, 0:256] + par[3:4, :])[:, 0:192]
            outs[i, px, :] = (fx[i + 3, px, :].astype(F32) + par[4:5, 0:192] * branch).astype(BF16)
            gn = hid[px, 256:512] * par[1:2, :]
            u = unit[px, :]
            m1 = jnp.sum(gn[:, :128] + gn[:, 128:], axis=1, keepdims=True) * (1.0 / 192)
            gu = gn * u
            m2 = jnp.sum(gu[:, :128] + gu[:, 128:], axis=1, keepdims=True) * (1.0 / 192)
            r = inv[px, :]
            gz = (gn - m1 - u * m2) * jnp.concatenate([r, r], axis=1)
            gzs[i, px, :] = gz[:, 0:192].astype(BF16)
            return 0

        lax.fori_loop(0, 4, finish, 0)
        lay_out(i + 3, gza, gzb, gzs[i].astype(F32))
        return 0

    lax.fori_loop(0, 8, mlp_row, 0)
    block_out = pltpu.make_async_copy(outs, out_block.at[0, 0], out_sem.at[0])
    block_out.start()

    gz_up = remote(gzs.at[pl.ds(0, 3)], halo.at[1], halo_send.at[2], halo_recv.at[2], s, up)
    gz_down = remote(gzs.at[pl.ds(5, 3)], halo.at[0], halo_send.at[3], halo_recv.at[3], s, down)

    @pl.when(has_up)
    def _():
        gz_up.start()

    @pl.when(has_down)
    def _():
        gz_down.start()

    def taps_grad(src, grad, total):
        def step(n, _):
            start = pl.multiple_of(n * 16, 16)
            g = [grad[i + 3, pl.ds(start + 8, 16), :] for i in range(8)]
            for b in range(7):
                sums = [None] * 7
                for r in range(14):
                    v = src[r, pl.ds(start + 5 + b, 16), :]
                    for a in range(7):
                        if 0 <= r - a < 8:
                            p = g[r - a] * v
                            sums[a] = p if sums[a] is None else sums[a] + p
                for a in range(7):
                    total[a * 7 + b] += sums[a][0:8] + sums[a][8:16]
            return 0

        return step

    lax.fori_loop(0, 16, taps_grad(xa, gza, gka), 0)
    lax.fori_loop(0, 8, taps_grad(xb, gzb, gkb), 0)

    for m, ref in enumerate((gwi, gwoT)):
        for rt in range(12):
            for lt in range(6):
                pay[m * 72 + rt * 6 + lt] = ref[rt * 16 : rt * 16 + 16, lt * 128 : lt * 128 + 128].astype(BF16)
    sum_a = jnp.sum(gka[...], axis=1)
    sum_b = jnp.sum(gkb[...], axis=1)
    sum_b = sum_b + pltpu.roll(sum_b, 64, 1)
    for m in range(4):
        pay[144 + m] = sum_a[m * 16 : m * 16 + 16].astype(BF16)
        pay[148 + m] = sum_b[m * 16 : m * 16 + 16].astype(BF16)
    pay[152:160] = jnp.zeros((8, 16, 128), BF16)

    core_copy = remote(pay.at[pl.ds((1 - core) * 80, 80)], r0, core_sem.at[0], core_sem.at[1], partner, t)
    core_copy.start()

    @pl.when(has_up)
    def _():
        gz_down.wait_recv()

    @pl.when(t == 0)
    def _():
        halo[0] = jnp.zeros((3, 256, 192), BF16)

    @pl.when(has_down)
    def _():
        gz_up.wait_recv()

    @pl.when(t == 31)
    def _():
        halo[1] = jnp.zeros((3, 256, 192), BF16)

    def lay_halo(r, _):
        lay_out(r, gza, gzb, halo[0, r].astype(F32))
        lay_out(r + 11, gza, gzb, halo[1, r].astype(F32))
        return 0

    lax.fori_loop(0, 3, lay_halo, 0)

    def back_a(n, _):
        start = pl.multiple_of(n * 16, 16)
        sums = conv_block(gza, ka, start, True)
        for i in range(8):
            gia[i, pl.ds(start, 16), :] = sums[i]
        return 0

    def back_b(n, _):
        start = pl.multiple_of(n * 16, 16)
        sums = conv_block(gzb, kb, start, True)
        for i in range(8):
            gib[i, pl.ds(start, 16), :] = sums[i]
            gib[i, pl.ds(start + 128, 16), :] = pltpu.roll(sums[i], 64, 1)
        return 0

    def add_tiles(count, dst, first, firsts_at, others):
        def step(n, _):
            total = first[firsts_at + n].astype(F32)
            for ref in others:
                total = total + ref[n].astype(F32)
            dst[n] = total.astype(BF16)
            return 0

        lax.fori_loop(0, count, step, 0)

    core_copy.wait()
    add_tiles(80, s1, pay, core * 80, [r0])
    x_copies = [
        remote(s1.at[pl.ds(((x + d + 1) % 4) * 20, 20)], r1.at[d], x_send.at[d], x_recv.at[d], *x_peers[d]) for d in range(3)
    ]
    for c in x_copies:
        c.start()
    lax.fori_loop(0, 8, back_a, 0)
    for c in x_copies:
        c.wait()
    add_tiles(20, s2, s1, x * 20, [r1.at[d] for d in range(3)])
    y_copies = [
        remote(s2.at[pl.ds(((y + d + 1) % 4) * 5, 5)], r2.at[d], y_send.at[d], y_recv.at[d], *y_peers[d]) for d in range(3)
    ]
    for c in y_copies:
        c.start()
    lax.fori_loop(8, 13, back_a, 0)
    for c in y_copies:
        c.wait()
    add_tiles(5, s3, s2, y * 5, [r2.at[d] for d in range(3)])
    z_copies = [remote(s3, r3.at[z], z_send.at[d], z_recv.at[d], *z_peers[d]) for d in range(3)]
    for c in z_copies:
        c.start()
    r3[z] = s3[...]
    lax.fori_loop(13, 16, back_a, 0)
    for c in z_copies:
        c.wait()
    at_y = core * 80 + x * 20 + y * 5
    total = r3[0].astype(F32)
    for k in range(1, 4):
        total = total + r3[k].astype(F32)
    full[pl.ds(at_y, 5)] = total.astype(BF16)
    y_back = [
        remote(full.at[pl.ds(at_y, 5)], full.at[pl.ds(at_y, 5)], y_send.at[d + 3], y_recv.at[d + 3], *y_peers[d]) for d in range(3)
    ]
    for c in y_back:
        c.start()
    lax.fori_loop(0, 4, back_b, 0)
    for c in y_back:
        c.wait()
    at_x = core * 80 + x * 20
    x_back = [
        remote(full.at[pl.ds(at_x, 20)], full.at[pl.ds(at_x, 20)], x_send.at[d + 3], x_recv.at[d + 3], *x_peers[d]) for d in range(3)
    ]
    for c in x_back:
        c.start()
    lax.fori_loop(4, 8, back_b, 0)

    def back_out(i, _):
        g = ct[i].astype(F32)
        fx[i, :, 0:128] = (g[:, 0:128] + gia[i]).astype(BF16)
        fx[i, :, 128:192] = (g[:, 128:192] + gib[i][:, 0:64]).astype(BF16)
        return 0

    lax.fori_loop(0, 8, back_out, 0)
    gin_out = pltpu.make_async_copy(fx.at[pl.ds(0, 8)], out_gin.at[0, 0], out_sem.at[1])
    gin_out.start()
    for c in x_back:
        c.wait()
    mine = pl.ds(core * 80, 80)
    core_back = remote(full.at[mine], full.at[mine], core_sem.at[2], core_sem.at[3], partner, t)
    core_back.start()
    core_back.wait()

    for m, ref in enumerate((out_gwi, out_gwoT)):
        for rt in range(12):
            for lt in range(6):
                ref[rt * 16 : rt * 16 + 16, lt * 128 : lt * 128 + 128] = full[m * 72 + rt * 6 + lt].astype(F32) * PIXEL_SCALE
    for m in range(4):
        out_gk[m * 16 : m * 16 + 16, 0:128] = full[144 + m].astype(F32) * PIXEL_SCALE
        out_gk[m * 16 : m * 16 + 16, 128:256] = full[148 + m].astype(F32) * PIXEL_SCALE

    @pl.when(has_up)
    def _():
        to_up.wait_send()
        gz_up.wait_send()

    @pl.when(has_down)
    def _():
        to_down.wait_send()
        gz_down.wait_send()

    block_out.wait()
    gin_out.wait()


def on_device(features, dw_kernel, dw_bias, ln_gain, ln_bias, w_in, b_in, w_out, b_out, layer_scale, cotangent):
    row = lambda v: v.reshape(1, -1)
    any_, vmem = pl.BlockSpec(memory_space=pl.ANY), pl.BlockSpec(memory_space=pltpu.VMEM)
    V, DMA = pltpu.VMEM, pltpu.SemaphoreType.DMA
    scratch = [
        V((14, 256, 192), BF16), V((8, 256, 192), BF16),
        V((14, 272, 128), F32), V((14, 144, 128), F32), V((49, 8, 128), F32), V((49, 8, 128), F32),
        V((8, 256, 128), F32), V((8, 256, 128), F32), V((14, 272, 128), F32), V((14, 144, 128), F32),
        V((8, 256), F32), V((256, 768), BF16), V((768, 256), BF16), V((8, 256, 256), BF16), V((8, 192, 256), BF16),
        V((256, 256), BF16), V((256, 256), F32), V((256, 128), F32), V((256, 768), F32), V((256, 768), F32),
        V((256, 768), BF16), V((256, 768), BF16), V((8, 256, 192), BF16), V((8, 256, 192), BF16),
        V((192, 768), F32), V((192, 768), F32), V((64, 8, 128), F32), V((64, 8, 128), F32),
        V((8, 256, 128), F32), V((8, 256, 128), F32),
        V((TILES, 16, 128), BF16), V((80, 16, 128), BF16), V((80, 16, 128), BF16), V((3, 20, 16, 128), BF16),
        V((20, 16, 128), BF16), V((3, 5, 16, 128), BF16), V((5, 16, 128), BF16), V((4, 5, 16, 128), BF16),
        V((TILES, 16, 128), BF16), V((2, 3, 256, 192), BF16),
        DMA((2,)), DMA((2,)), DMA((4,)), DMA((4,)), DMA((4,)), DMA((6,)), DMA((6,)), DMA((6,)), DMA((6,)), DMA((3,)), DMA((3,)),
    ]
    block, gin, gwi, gwoT, gk = pl.pallas_call(
        kernel,
        out_shape=(
            jax.ShapeDtypeStruct((1, 1, 8, 256, 192), BF16), jax.ShapeDtypeStruct((1, 1, 8, 256, 192), BF16),
            jax.ShapeDtypeStruct((192, 768), F32), jax.ShapeDtypeStruct((192, 768), F32), jax.ShapeDtypeStruct((64, 256), F32),
        ),
        in_specs=[any_, any_] + [vmem] * 9,
        out_specs=(any_, any_, vmem, vmem, vmem),
        scratch_shapes=scratch,
        compiler_params=pltpu.CompilerParams(collective_id=0, has_side_effects=True, vmem_limit_bytes=60 << 20),
    )(
        features, cotangent, dw_kernel, row(dw_bias), row(ln_gain), row(ln_bias), w_in, row(b_in), w_out, row(b_out),
        row(layer_scale),
    )
    return block, gin, gwi, gwoT.T, gk[:49, :192].reshape(7, 7, 192)


def solution(mesh):
    split, whole = P("slide", "space", None, None, None), P()
    return jax.shard_map(
        on_device,
        mesh=mesh,
        in_specs=(split,) + (whole,) * 9 + (split,),
        out_specs=(split, split, whole, whole, whole),
        check_vma=False,
    )
```

```python
import jax
import jax.numpy as jnp
from jax import lax
from jax.experimental import pallas as pl
from jax.experimental.pallas import tpu as pltpu
from jax.sharding import PartitionSpec as P

EPSILON = 1e-06
F32 = jnp.float32
BF16 = jnp.bfloat16
MESH = pl.DeviceIdType.MESH
PIXEL_SCALE = float(262144) ** (-0.5)
TILES = 160
NT = (((1,), (1,)), ((), ()))


def remote(src, dst, send, recv, slide, space):
    return pltpu.make_async_remote_copy(
        src_ref=src, dst_ref=dst, send_sem=send, recv_sem=recv,
        device_id={"slide": slide, "space": space}, device_id_type=MESH,
    )


def gelu_parts(h):
    cdf = 0.5 * (1.0 + lax.erf(h * 0.7071067811865476))
    slope = cdf + h * jnp.exp(-0.5 * h * h) * 0.3989422804014327
    return h * cdf, slope


def spread(value, row, group, dst):
    column = lax.broadcasted_iota(jnp.int32, (16, 256), 1)
    wide = value.astype(F32)
    for b in range(7):
        moved = wide
        if b != 3:
            moved = pltpu.roll(wide, (3 - b) % 256, 1)
            inside = column >= 3 - b if b < 3 else column < 259 - b
            moved = jnp.where(inside, moved, 0.0)
        dst[group, pl.ds(pl.multiple_of((b * 16 + row) * 16, 16), 16), :] = moved.astype(BF16)


def build_taps(dwk, flat, taps, flip):
    lane8 = lax.broadcasted_iota(jnp.int32, (8, 128), 1)
    for a in range(7):
        flat[a, 0:7, 0:192] = jnp.concatenate(
            [dwk[6 - a if flip else a, (6 - b if flip else b) : (6 - b if flip else b) + 1, :] for b in range(7)], axis=0
        )
    for g in range(12):
        base = jnp.zeros((8, 128), F32)
        tile, at = g // 8 * 128, g % 8 * 16
        for a in range(7):
            v = flat[a, :, tile : tile + 128]
            v = pltpu.roll(v, (a * 16 - at) % 128, 1)
            base = jnp.where((lane8 >= a * 16) & (lane8 < a * 16 + 16), v, base)
        flat[7 + g, :, 0:128] = base
    same = (
        lax.broadcasted_iota(jnp.int32, (16, 128), 1) % 16 == lax.broadcasted_iota(jnp.int32, (16, 128), 0)
    )

    def group(g, _):
        base = flat[7 + g, :, 0:128]
        for i in range(8):
            moved = pltpu.roll(base, i * 16, 1) if i else base
            first = jnp.where(lane8 >= i * 16, moved, 0.0)
            second = jnp.where(lane8 < i * 16, moved, 0.0)
            for b in range(7):
                for half, v in enumerate((first, second)):
                    row = jnp.broadcast_to(v[b : b + 1, :], (16, 128))
                    taps[g, i * 16 : i * 16 + 16, b * 256 + half * 128 : b * 256 + half * 128 + 128] = jnp.where(
                        same, row, 0.0
                    ).astype(BF16)
        return 0

    lax.fori_loop(0, 12, group, 0)


def kernel(
    feat, cot, dwk, dwb, gain, lbias, w_in, b_in, woutT, b_out, lscale,
    out_block, out_gin, out_gwi, out_gwoT, out_gk,
    fx, ct, xs, gs, taps, back, flat, zf, par, bias, winT, wout, gout,
    nb, unit, hid, gact, act, gh, outs, gzs, gwi, gwoT, gkr,
    pay, r0, s1, r1, s2, r2, s3, r3, full, halo,
    in_sem, out_sem, halo_send, halo_recv, core_sem, x_send, x_recv, y_send, y_recv, z_send, z_recv,
):
    s, t = lax.axis_index("slide"), lax.axis_index("space")
    z_hi, core = s // 2, s % 2
    z_lo, x, y = t % 2, (t // 2) % 4, t // 8
    z = z_hi * 2 + z_lo
    partner = z_hi * 2 + (1 - core)
    x_peers = [(s, (y * 4 + (x + d) % 4) * 2 + z_lo) for d in (1, 2, 3)]
    y_peers = [(s, (((y + d) % 4) * 4 + x) * 2 + z_lo) for d in (1, 2, 3)]
    z_peers = [(((z + d) % 4) // 2 * 2 + core, (y * 4 + x) * 2 + ((z + d) % 4) % 2) for d in (1, 2, 3)]
    has_up, has_down = t > 0, t < 31
    up, down = jnp.maximum(t - 1, 0), jnp.minimum(t + 1, 31)

    barrier = pltpu.get_barrier_semaphore()
    for ps, pt in [(partner, t)] + x_peers + y_peers + z_peers:
        pl.semaphore_signal(barrier, inc=1, device_id={"slide": ps, "space": pt}, device_id_type=MESH)

    @pl.when(has_up)
    def _():
        pl.semaphore_signal(barrier, inc=1, device_id={"slide": s, "space": up}, device_id_type=MESH)

    @pl.when(has_down)
    def _():
        pl.semaphore_signal(barrier, inc=1, device_id={"slide": s, "space": down}, device_id_type=MESH)

    own_in = pltpu.make_async_copy(feat.at[0, 0], fx.at[pl.ds(3, 8)], in_sem.at[0])
    own_in.start()
    cot_in = pltpu.make_async_copy(cot.at[0, 0], ct, in_sem.at[1])
    cot_in.start()

    pl.semaphore_wait(barrier, 10 + jnp.minimum(t, 1) + jnp.minimum(31 - t, 1))

    to_up = remote(feat.at[0, 0, pl.ds(0, 3)], fx.at[pl.ds(11, 3)], halo_send.at[0], halo_recv.at[0], s, up)
    to_down = remote(feat.at[0, 0, pl.ds(5, 3)], fx.at[pl.ds(0, 3)], halo_send.at[1], halo_recv.at[1], s, down)

    @pl.when(has_up)
    def _():
        to_up.start()

    @pl.when(has_down)
    def _():
        to_down.start()

    for n, ref in enumerate((dwb, gain, lbias, b_out, lscale)):
        par[n, 0:128, :] = jnp.broadcast_to(ref[:, 0:128], (128, 128)).T
        tail = jnp.concatenate([ref[:, 128:192], ref[:, 128:192]], axis=1)
        par[n, 128:256, :] = jnp.broadcast_to(tail, (128, 128)).T
    for n in range(6):
        bias[n * 128 : n * 128 + 128, :] = jnp.broadcast_to(b_in[:, n * 128 : n * 128 + 128], (128, 128)).T
    winT[...] = w_in[...].T
    wout[...] = woutT[...].T
    gwi[...] = jnp.zeros_like(gwi)
    gwoT[...] = jnp.zeros_like(gwoT)

    def clear(g, _):
        none = jnp.zeros((32, 256), BF16)
        for b in range(7):
            xs[g, b * 256 + 224 : b * 256 + 256, :] = none
            gs[g, b * 256 + 224 : b * 256 + 256, :] = none
        return 0

    lax.fori_loop(0, 12, clear, 0)
    build_taps(dwk, flat, taps, False)
    build_taps(dwk, flat, back, True)

    cot_in.wait()

    def both(v):
        return jnp.concatenate([v, v], axis=1)

    def scale_row(i, _):
        gout[i] = (both(par[4, 0:192, :]) * ct[i].astype(F32)).astype(BF16)
        return 0

    lax.fori_loop(0, 8, scale_row, 0)
    own_in.wait()

    @pl.when(has_up)
    def _():
        to_down.wait_recv()

    @pl.when(t == 0)
    def _():
        fx[0:3] = jnp.zeros((3, 192, 256), BF16)

    @pl.when(has_down)
    def _():
        to_up.wait_recv()

    @pl.when(t == 31)
    def _():
        fx[11:14] = jnp.zeros((3, 192, 256), BF16)

    def group_rows(g):
        return pl.ds(pl.multiple_of(g * 16, 16), 16)

    def spread_x(n, _):
        r, g = n // 12, n % 12
        spread(fx[r, group_rows(g), :], r, g, xs)
        return 0

    lax.fori_loop(0, 14 * 12, spread_x, 0)

    def conv(g, _):
        z = jnp.dot(taps[g], xs[g], preferred_element_type=F32)
        for i in range(8):
            zf[i, group_rows(g), :] = z[i * 16 : i * 16 + 16, :] + both(par[0, group_rows(g), :])
        return 0

    lax.fori_loop(0, 12, conv, 0)

    def mlp_row(i, _):
        def norm(q, _):
            ln = pl.ds(pl.multiple_of(q * 128, 128), 128)
            v = zf[i, :, ln]
            v = v - jnp.sum(v, axis=0, keepdims=True) * (1.0 / 192)
            var = jnp.sum(v * v, axis=0, keepdims=True) * (1.0 / 192)
            r = lax.rsqrt(var + EPSILON)
            v = v * r
            zf[i, :, ln] = v
            unit[0:8, ln] = jnp.broadcast_to(r, (8, 128))
            nb[:, ln] = (v * par[1, 0:192, :] + par[2, 0:192, :]).astype(BF16)
            return 0

        lax.fori_loop(0, 2, norm, 0)
        hid[...] = jnp.dot(winT[...], nb[...], preferred_element_type=F32)
        gact[...] = jnp.dot(wout[...], gout[i], preferred_element_type=F32)

        def gelu(n, _):
            px = pl.ds(pl.multiple_of(n * 16, 16), 16)
            value, slope = gelu_parts(hid[px, :] + both(bias[px, :]))
            act[px, :] = value.astype(BF16)
            gh[px, :] = (gact[px, :] * slope).astype(BF16)
            return 0

        lax.fori_loop(0, 48, gelu, 0)
        hid[0:192, :] = jnp.dot(woutT[...], act[...], preferred_element_type=F32)
        hid[192:384, :] = jnp.dot(w_in[...], gh[...], preferred_element_type=F32)
        gwi[...] += lax.dot_general(nb[...], gh[...], NT, preferred_element_type=F32)
        gwoT[...] += lax.dot_general(gout[i], act[...], NT, preferred_element_type=F32)

        def finish(q, _):
            ln = pl.ds(pl.multiple_of(q * 128, 128), 128)
            branch = hid[0:192, ln] + par[3, 0:192, :]
            outs[i, :, ln] = (fx[i + 3, :, ln].astype(F32) + par[4, 0:192, :] * branch).astype(BF16)
            gn = hid[192:384, ln] * par[1, 0:192, :]
            u = zf[i, :, ln]
            m1 = jnp.sum(gn, axis=0, keepdims=True) * (1.0 / 192)
            m2 = jnp.sum(gn * u, axis=0, keepdims=True) * (1.0 / 192)
            gzs[i, :, ln] = (unit[0:1, ln] * (gn - m1 - u * m2)).astype(BF16)
            return 0

        lax.fori_loop(0, 2, finish, 0)

        def spread_gz(g, _):
            spread(gzs[i, group_rows(g), :], i + 3, g, gs)
            return 0

        lax.fori_loop(0, 12, spread_gz, 0)
        return 0

    lax.fori_loop(0, 8, mlp_row, 0)
    block_out = pltpu.make_async_copy(outs, out_block.at[0, 0], out_sem.at[0])
    block_out.start()

    gz_up = remote(gzs.at[pl.ds(0, 3)], halo.at[1], halo_send.at[2], halo_recv.at[2], s, up)
    gz_down = remote(gzs.at[pl.ds(5, 3)], halo.at[0], halo_send.at[3], halo_recv.at[3], s, down)

    @pl.when(has_up)
    def _():
        gz_up.start()

    @pl.when(has_down)
    def _():
        gz_down.start()

    same = lax.broadcasted_iota(jnp.int32, (16, 256), 1) % 16 == lax.broadcasted_iota(jnp.int32, (16, 256), 0)
    lane8 = lax.broadcasted_iota(jnp.int32, (8, 128), 1)

    def taps_grad(g, _):
        own = gs[g, 3 * 256 + 48 : 3 * 256 + 48 + 128, :]
        for b in range(7):
            pairs = lax.dot_general(own, xs[g, b * 256 : b * 256 + 256, :], NT, preferred_element_type=F32)
            total = jnp.zeros((8, 128), F32)
            for i in range(8):
                v = jnp.where(same, pairs[i * 16 : i * 16 + 16, :], 0.0)
                v = v[0:8] + v[8:16]
                if i == 0:
                    total = total + v[:, 0:128]
                else:
                    v = pltpu.roll(jnp.where(lane8 >= i * 16, v[:, 0:128], v[:, 128:256]), 128 - i * 16, 1)
                    total = total + v
            gkr[g, b : b + 1, :] = jnp.sum(total, axis=0, keepdims=True)
        gkr[g, 7:8, :] = jnp.zeros((1, 128), F32)
        return 0

    lax.fori_loop(0, 12, taps_grad, 0)

    for m, ref in enumerate((gwi, gwoT)):
        for rt in range(12):
            for lt in range(6):
                pay[m * 72 + rt * 6 + lt] = ref[rt * 16 : rt * 16 + 16, lt * 128 : lt * 128 + 128].astype(BF16)
    for m in range(6):
        pay[144 + m] = jnp.concatenate([gkr[2 * m], gkr[2 * m + 1]], axis=0).astype(BF16)
    pay[150:160] = jnp.zeros((10, 16, 128), BF16)

    core_copy = remote(pay.at[pl.ds((1 - core) * 80, 80)], r0, core_sem.at[0], core_sem.at[1], partner, t)
    core_copy.start()

    @pl.when(has_up)
    def _():
        gz_down.wait_recv()

    @pl.when(t == 0)
    def _():
        halo[0] = jnp.zeros((3, 192, 256), BF16)

    @pl.when(has_down)
    def _():
        gz_up.wait_recv()

    @pl.when(t == 31)
    def _():
        halo[1] = jnp.zeros((3, 192, 256), BF16)

    def spread_halo(n, _):
        r, g = n // 12, n % 12
        spread(halo[0, r, group_rows(g), :], r, g, gs)
        spread(halo[1, r, group_rows(g), :], r + 11, g, gs)
        return 0

    lax.fori_loop(0, 36, spread_halo, 0)

    def back_conv(g, _):
        v = jnp.dot(back[g], gs[g], preferred_element_type=F32)
        for i in range(8):
            fx[i, group_rows(g), :] = (ct[i, group_rows(g), :].astype(F32) + v[i * 16 : i * 16 + 16, :]).astype(BF16)
        return 0

    def add_tiles(count, dst, first, firsts_at, others):
        def step(n, _):
            total = first[firsts_at + n].astype(F32)
            for ref in others:
                total = total + ref[n].astype(F32)
            dst[n] = total.astype(BF16)
            return 0

        lax.fori_loop(0, count, step, 0)

    core_copy.wait()
    add_tiles(80, s1, pay, core * 80, [r0])
    x_copies = [
        remote(s1.at[pl.ds(((x + d + 1) % 4) * 20, 20)], r1.at[d], x_send.at[d], x_recv.at[d], *x_peers[d]) for d in range(3)
    ]
    for c in x_copies:
        c.start()
    lax.fori_loop(0, 4, back_conv, 0)
    for c in x_copies:
        c.wait()
    add_tiles(20, s2, s1, x * 20, [r1.at[d] for d in range(3)])
    y_copies = [
        remote(s2.at[pl.ds(((y + d + 1) % 4) * 5, 5)], r2.at[d], y_send.at[d], y_recv.at[d], *y_peers[d]) for d in range(3)
    ]
    for c in y_copies:
        c.start()
    lax.fori_loop(4, 6, back_conv, 0)
    for c in y_copies:
        c.wait()
    add_tiles(5, s3, s2, y * 5, [r2.at[d] for d in range(3)])
    z_copies = [remote(s3, r3.at[z], z_send.at[d], z_recv.at[d], *z_peers[d]) for d in range(3)]
    for c in z_copies:
        c.start()
    r3[z] = s3[...]
    lax.fori_loop(6, 8, back_conv, 0)
    for c in z_copies:
        c.wait()
    at_y = core * 80 + x * 20 + y * 5
    total = r3[0].astype(F32)
    for k in range(1, 4):
        total = total + r3[k].astype(F32)
    full[pl.ds(at_y, 5)] = total.astype(BF16)
    y_back = [
        remote(full.at[pl.ds(at_y, 5)], full.at[pl.ds(at_y, 5)], y_send.at[d + 3], y_recv.at[d + 3], *y_peers[d]) for d in range(3)
    ]
    for c in y_back:
        c.start()
    lax.fori_loop(8, 10, back_conv, 0)
    for c in y_back:
        c.wait()
    at_x = core * 80 + x * 20
    x_back = [
        remote(full.at[pl.ds(at_x, 20)], full.at[pl.ds(at_x, 20)], x_send.at[d + 3], x_recv.at[d + 3], *x_peers[d]) for d in range(3)
    ]
    for c in x_back:
        c.start()
    lax.fori_loop(10, 12, back_conv, 0)
    gin_out = pltpu.make_async_copy(fx.at[pl.ds(0, 8)], out_gin.at[0, 0], out_sem.at[1])
    gin_out.start()
    for c in x_back:
        c.wait()
    mine = pl.ds(core * 80, 80)
    core_back = remote(full.at[mine], full.at[mine], core_sem.at[2], core_sem.at[3], partner, t)
    core_back.start()
    core_back.wait()

    for m, ref in enumerate((out_gwi, out_gwoT)):
        for rt in range(12):
            for lt in range(6):
                ref[rt * 16 : rt * 16 + 16, lt * 128 : lt * 128 + 128] = full[m * 72 + rt * 6 + lt].astype(F32) * PIXEL_SCALE
    for m in range(6):
        out_gk[m * 16 : m * 16 + 16, :] = full[144 + m].astype(F32) * PIXEL_SCALE

    @pl.when(has_up)
    def _():
        to_up.wait_send()
        gz_up.wait_send()

    @pl.when(has_down)
    def _():
        to_down.wait_send()
        gz_down.wait_send()

    block_out.wait()
    gin_out.wait()


def on_device(features, dw_kernel, dw_bias, ln_gain, ln_bias, w_in, b_in, w_out, b_out, layer_scale, cotangent):
    row = lambda v: v.reshape(1, -1)
    turn = lambda v: jnp.swapaxes(v, 3, 4)
    any_, vmem = pl.BlockSpec(memory_space=pl.ANY), pl.BlockSpec(memory_space=pltpu.VMEM)
    V, DMA = pltpu.VMEM, pltpu.SemaphoreType.DMA
    scratch = [
        V((14, 192, 256), BF16), V((8, 192, 256), BF16), V((12, 1792, 256), BF16), V((12, 1792, 256), BF16),
        V((12, 128, 1792), BF16), V((12, 128, 1792), BF16), V((19, 8, 256), F32), V((8, 192, 256), F32),
        V((5, 256, 128), F32), V((768, 128), F32), V((768, 192), BF16), V((768, 192), BF16), V((8, 192, 256), BF16),
        V((192, 256), BF16), V((8, 256), F32), V((768, 256), F32), V((768, 256), F32), V((768, 256), BF16),
        V((768, 256), BF16), V((8, 192, 256), BF16), V((8, 192, 256), BF16),
        V((192, 768), F32), V((192, 768), F32), V((12, 8, 128), F32),
        V((TILES, 16, 128), BF16), V((80, 16, 128), BF16), V((80, 16, 128), BF16), V((3, 20, 16, 128), BF16),
        V((20, 16, 128), BF16), V((3, 5, 16, 128), BF16), V((5, 16, 128), BF16), V((4, 5, 16, 128), BF16),
        V((TILES, 16, 128), BF16), V((2, 3, 192, 256), BF16),
        DMA((2,)), DMA((2,)), DMA((4,)), DMA((4,)), DMA((4,)), DMA((6,)), DMA((6,)), DMA((6,)), DMA((6,)), DMA((3,)), DMA((3,)),
    ]
    block, gin, gwi, gwoT, gk = pl.pallas_call(
        kernel,
        out_shape=(
            jax.ShapeDtypeStruct((1, 1, 8, 192, 256), BF16), jax.ShapeDtypeStruct((1, 1, 8, 192, 256), BF16),
            jax.ShapeDtypeStruct((192, 768), F32), jax.ShapeDtypeStruct((192, 768), F32), jax.ShapeDtypeStruct((96, 128), F32),
        ),
        in_specs=[any_, any_] + [vmem] * 9,
        out_specs=(any_, any_, vmem, vmem, vmem),
        scratch_shapes=scratch,
        compiler_params=pltpu.CompilerParams(collective_id=0, has_side_effects=True, vmem_limit_bytes=60 << 20),
    )(
        turn(features), turn(cotangent), dw_kernel, row(dw_bias), row(ln_gain), row(ln_bias), w_in, row(b_in), w_out.T, row(b_out),
        row(layer_scale),
    )
    gk = gk.reshape(12, 8, 8, 16)[:, :7, :7].transpose(2, 1, 0, 3).reshape(7, 7, 192)
    return turn(block), turn(gin), gwi, gwoT.T, gk


def solution(mesh):
    split, whole = P("slide", "space", None, None, None), P()
    return jax.shard_map(
        on_device,
        mesh=mesh,
        in_specs=(split,) + (whole,) * 9 + (split,),
        out_specs=(split, split, whole, whole, whole),
        check_vma=False,
    )
```

```python
import jax
import jax.numpy as jnp
from jax import lax
from jax.experimental import pallas as pl
from jax.experimental.pallas import tpu as pltpu
from jax.sharding import PartitionSpec as P

EPSILON = 1e-06
F32 = jnp.float32
BF16 = jnp.bfloat16
MESH = pl.DeviceIdType.MESH
PIXEL_SCALE = float(262144) ** (-0.5)
NT = (((1,), (1,)), ((), ()))


def remote(src, dst, send, recv, slide, space):
    return pltpu.make_async_remote_copy(
        src_ref=src, dst_ref=dst, send_sem=send, recv_sem=recv,
        device_id={"slide": slide, "space": space}, device_id_type=MESH,
    )


def gelu_parts(h):
    cdf = 0.5 * (1.0 + lax.erf(h * 0.7071067811865476))
    slope = cdf + h * jnp.exp(-0.5 * h * h) * 0.3989422804014327
    return h * cdf, slope


def spread(value, slot, group, dst):
    lane = lax.broadcasted_iota(jnp.int32, (16, 128), 1)
    left, right = value[:, 0:128], value[:, 128:256]
    none = jnp.zeros_like(left)
    for b in range(7):
        d = b - 3
        first, second = left, right
        if d:
            first, second = pltpu.roll(left, -d % 128, 1), pltpu.roll(right, -d % 128, 1)
            if d > 0:
                first, second = jnp.where(lane < 128 - d, first, second), jnp.where(lane < 128 - d, second, none)
            else:
                first, second = jnp.where(lane < -d, none, first), jnp.where(lane < -d, first, second)
        at = b * 128 + slot * 16
        dst[group, at : at + 16, 0:128] = first
        dst[group, at : at + 16, 128:256] = second


def valid(i, lane):
    slot = lane // 16
    own = (slot >= i - 3) & (slot <= i + 3)
    halo = jnp.zeros_like(own)
    if i < 3:
        halo = slot >= i + 5
    if i >= 5:
        halo = slot <= i - 5
    return own, halo


def build_taps(dwk, flat, own, halo, flip):
    lane8 = lax.broadcasted_iota(jnp.int32, (8, 128), 1)
    for a in range(7):
        flat[a, 0:7, 0:192] = jnp.concatenate(
            [dwk[6 - a if flip else a, (6 - b if flip else b) : (6 - b if flip else b) + 1, :] for b in range(7)], axis=0
        )
    for g in range(12):
        base = jnp.zeros((8, 128), F32)
        tile, at = g // 8 * 128, g % 8 * 16
        for a in range(7):
            v = flat[a, :, tile : tile + 128]
            v = pltpu.roll(v, (a * 16 - at) % 128, 1)
            base = jnp.where((lane8 >= a * 16) & (lane8 < a * 16 + 16), v, base)
        flat[7 + g, :, 0:128] = base
    lane = lax.broadcasted_iota(jnp.int32, (16, 128), 1)
    same = lane % 16 == lax.broadcasted_iota(jnp.int32, (16, 128), 0)

    def group(g, _):
        base = flat[7 + g, :, 0:128]
        for i in range(8):
            moved = pltpu.roll(base, (i - 3) * 16 % 128, 1)
            for keep, dst in zip(valid(i, lane8), (own, halo)):
                if dst is halo and 3 <= i < 5:
                    dst[g, i * 16 : i * 16 + 16, :] = jnp.zeros((16, 896), BF16)
                    continue
                v = jnp.where(keep, moved, 0.0)
                for b in range(7):
                    row = jnp.broadcast_to(v[b : b + 1, :], (16, 128))
                    dst[g, i * 16 : i * 16 + 16, b * 128 : b * 128 + 128] = jnp.where(same, row, 0.0).astype(BF16)
        return 0

    lax.fori_loop(0, 12, group, 0)


def both(v):
    return jnp.concatenate([v, v], axis=1)


def rows16(g):
    return pl.ds(pl.multiple_of(g * 16, 16), 16)


HALO_SLOTS = ((0, 5), (1, 6), (2, 7), (11, 0), (12, 1), (13, 2))


def kernel(
    feat, cot, dwk, dwb, gain, lbias, w_in, b_in, woutT, b_out, lscale,
    out_block, out_gin, out_gwi, out_gwoT, out_gk,
    fx, ct, xs, xh, gs, gh_, taps, taps_h, back, back_h, flat, zf, par, bias, winT, wout, gout,
    nb, rinv, osum, nsum, outs, gzs, gw, gkr, halo,
    pay, r0, s1f, s1b, r1, ry, rz, full, k0, kx, ky, kz, kfull,
    in_sem, out_sem, halo_send, halo_recv, ar_send, ar_recv, k_send, k_recv,
):
    s, t = lax.axis_index("slide"), lax.axis_index("space")
    z_hi, core = s // 2, s % 2
    z_lo, x, y = t % 2, (t // 2) % 4, t // 8
    z = z_hi * 2 + z_lo
    partner = z_hi * 2 + (1 - core)
    x_peers = [(s, (y * 4 + (x + d) % 4) * 2 + z_lo) for d in (1, 2, 3)]
    y_peers = [(s, (((y + d) % 4) * 4 + x) * 2 + z_lo) for d in (1, 2, 3)]
    z_peers = [(((z + d) % 4) // 2 * 2 + core, (y * 4 + x) * 2 + ((z + d) % 4) % 2) for d in (1, 2, 3)]
    has_up, has_down = t > 0, t < 31
    up, down = jnp.maximum(t - 1, 0), jnp.minimum(t + 1, 31)

    own_in = pltpu.make_async_copy(feat.at[0, 0], fx.at[pl.ds(3, 8)], in_sem.at[0])
    own_in.start()
    cot_in = pltpu.make_async_copy(cot.at[0, 0], ct, in_sem.at[1])
    cot_in.start()

    barrier = pltpu.get_barrier_semaphore()
    for ps, pt in [(partner, t)] + x_peers + y_peers + z_peers:
        pl.semaphore_signal(barrier, inc=1, device_id={"slide": ps, "space": pt}, device_id_type=MESH)

    @pl.when(has_up)
    def _():
        pl.semaphore_signal(barrier, inc=1, device_id={"slide": s, "space": up}, device_id_type=MESH)

    @pl.when(has_down)
    def _():
        pl.semaphore_signal(barrier, inc=1, device_id={"slide": s, "space": down}, device_id_type=MESH)

    pl.semaphore_wait(barrier, 10 + jnp.minimum(t, 1) + jnp.minimum(31 - t, 1))

    to_up = remote(feat.at[0, 0, pl.ds(0, 3)], fx.at[pl.ds(11, 3)], halo_send.at[0], halo_recv.at[0], s, up)
    to_down = remote(feat.at[0, 0, pl.ds(5, 3)], fx.at[pl.ds(0, 3)], halo_send.at[1], halo_recv.at[1], s, down)

    @pl.when(has_up)
    def _():
        to_up.start()

    @pl.when(has_down)
    def _():
        to_down.start()

    for n, ref in enumerate((dwb, gain, lbias, b_out, lscale)):
        par[n, 0:128, :] = jnp.broadcast_to(ref[:, 0:128], (128, 128)).T
        par[n, 128:256, :] = jnp.broadcast_to(both(ref[:, 128:192]), (128, 128)).T
    for n in range(6):
        bias[n * 128 : n * 128 + 128, :] = jnp.broadcast_to(b_in[:, n * 128 : n * 128 + 128], (128, 128)).T
    winT[...] = w_in[...].T
    wout[...] = woutT[...].T
    build_taps(dwk, flat, taps, taps_h, False)

    def clear(g, _):
        none = jnp.zeros((32, 256), BF16)
        for b in range(7):
            xh[g, b * 128 + 48 : b * 128 + 80, :] = none
            gh_[g, b * 128 + 48 : b * 128 + 80, :] = none
        return 0

    lax.fori_loop(0, 12, clear, 0)
    own_in.wait()

    def conv_own(g, _):
        for i in range(8):
            spread(fx[i + 3, rows16(g), :], i, g, xs)
        v = jnp.dot(taps[g], xs[g], preferred_element_type=F32)
        for i in range(8):
            zf[i, rows16(g), :] = v[i * 16 : i * 16 + 16, :] + both(par[0, rows16(g), :])
        return 0

    lax.fori_loop(0, 12, conv_own, 0)
    build_taps(dwk, flat, back, back_h, True)
    cot_in.wait()

    def scale_row(i, _):
        gout[i] = (both(par[4, 0:192, :]) * ct[i].astype(F32)).astype(BF16)
        return 0

    lax.fori_loop(0, 8, scale_row, 0)

    @pl.when(has_up)
    def _():
        to_down.wait_recv()

    @pl.when(t == 0)
    def _():
        fx[0:3] = jnp.zeros((3, 192, 256), BF16)

    @pl.when(has_down)
    def _():
        to_up.wait_recv()

    @pl.when(t == 31)
    def _():
        fx[11:14] = jnp.zeros((3, 192, 256), BF16)

    def conv_halo(g, _):
        for r, slot in HALO_SLOTS:
            spread(fx[r, rows16(g), :], slot, g, xh)
        v = jnp.dot(taps_h[g], xh[g], preferred_element_type=F32)
        for i in (0, 1, 2, 5, 6, 7):
            zf[i, rows16(g), :] += v[i * 16 : i * 16 + 16, :]
        return 0

    lax.fori_loop(0, 12, conv_halo, 0)

    def norm(n, _):
        i = n // 2
        ln = pl.ds(pl.multiple_of(n % 2 * 128, 128), 128)
        v = zf[i, :, ln]
        v = v - jnp.sum(v, axis=0, keepdims=True) * (1.0 / 192)
        var = jnp.sum(v * v, axis=0, keepdims=True) * (1.0 / 192)
        r = lax.rsqrt(var + EPSILON)
        v = v * r
        zf[i, :, ln] = v
        rinv[i, :, ln] = jnp.broadcast_to(r, (8, 128))
        nb[i, :, ln] = (v * par[1, 0:192, :] + par[2, 0:192, :]).astype(BF16)
        return 0

    lax.fori_loop(0, 16, norm, 0)

    def stage0(f):
        pay[f] = gw[1 - core, f].astype(BF16)
        core_copy(f).start()

    def core_copy(f):
        return remote(pay.at[f], r0.at[f], ar_send.at[f, 0], ar_recv.at[f, 0], partner, t)

    def x_copies(f):
        return [
            remote(s1b.at[f, pl.ds(((x + d + 1) % 4) * 48, 48)], r1.at[f, d], ar_send.at[f, 1 + d], ar_recv.at[f, 1 + d], *x_peers[d])
            for d in range(3)
        ]

    def y_copies(f):
        return [remote(ry.at[f, y], ry.at[f, y], ar_send.at[f, 4 + d], ar_recv.at[f, 4 + d], *y_peers[d]) for d in range(3)]

    def z_copies(f):
        return [remote(rz.at[f, z], rz.at[f, z], ar_send.at[f, 7 + d], ar_recv.at[f, 7 + d], *z_peers[d]) for d in range(3)]

    def x_back(f):
        mine = full.at[core, f, pl.ds(x * 48, 48)]
        return [remote(mine, mine, ar_send.at[f, 10 + d], ar_recv.at[f, 10 + d], *x_peers[d]) for d in range(3)]

    def core_back(f):
        return remote(full.at[core, f], full.at[core, f], ar_send.at[f, 13], ar_recv.at[f, 13], partner, t)

    def stage1(f):
        core_copy(f).wait()
        total = gw[core, f] + r0[f].astype(F32)
        s1f[f] = total
        s1b[f] = total.astype(BF16)
        for c in x_copies(f):
            c.start()

    def stage2(f):
        for c in x_copies(f):
            c.wait()
        total = s1f[f, pl.ds(x * 48, 48), :]
        for d in range(3):
            total = total + r1[f, d].astype(F32)
        ry[f, y] = total
        for c in y_copies(f):
            c.start()

    def stage3(f):
        for c in y_copies(f):
            c.wait()
        rz[f, z] = (ry[f, 0] + ry[f, 1]) + (ry[f, 2] + ry[f, 3])
        for c in z_copies(f):
            c.start()

    def stage4(f):
        for c in z_copies(f):
            c.wait()
        full[core, f, pl.ds(x * 48, 48), :] = ((rz[f, 0] + rz[f, 1]) + (rz[f, 2] + rz[f, 3])).astype(BF16)
        for c in x_back(f):
            c.start()

    def stage5(f):
        for c in x_back(f):
            c.wait()
        core_back(f).start()

    def stage6(f):
        core_back(f).wait()
        out_gwi[:, f * 256 : f * 256 + 256] = full[0, f].astype(F32) * PIXEL_SCALE
        out_gwoT[:, f * 256 : f * 256 + 256] = full[1, f].astype(F32) * PIXEL_SCALE

    gw[...] = jnp.zeros_like(gw)
    osum[...] = jnp.zeros_like(osum)
    nsum[...] = jnp.zeros_like(nsum)
    after = {
        3: [(stage0, 0)], 4: [(stage1, 0)], 7: [(stage2, 0), (stage0, 1)], 8: [(stage1, 1)], 10: [(stage3, 0)],
        11: [(stage2, 1), (stage0, 2)],
    }

    def mlp(k, _):
        f = k // 4
        units = pl.ds(pl.multiple_of(f * 256, 256), 256)
        for m in range(2):
            i = k % 4 * 2 + m
            hidden = jnp.dot(winT[units, :], nb[i], preferred_element_type=F32) + both(bias[units, :])
            value, slope = gelu_parts(hidden)
            act = value.astype(BF16)
            gh = (jnp.dot(wout[units, :], gout[i], preferred_element_type=F32) * slope).astype(BF16)
            osum[i] += jnp.dot(woutT[:, units], act, preferred_element_type=F32)
            nsum[i] += jnp.dot(w_in[:, units], gh, preferred_element_type=F32)
            gw[0, f] += lax.dot_general(nb[i], gh, NT, preferred_element_type=F32)
            gw[1, f] += lax.dot_general(gout[i], act, NT, preferred_element_type=F32)
        for at, steps in after.items():

            @pl.when(k == at)
            def _():
                for step, chunk in steps:
                    step(chunk)

        return 0

    lax.fori_loop(0, 12, mlp, 0)

    def finish(n, _):
        i = n // 2
        ln = pl.ds(pl.multiple_of(n % 2 * 128, 128), 128)
        gn = nsum[i, :, ln] * par[1, 0:192, :]
        u = zf[i, :, ln]
        m1 = jnp.sum(gn, axis=0, keepdims=True) * (1.0 / 192)
        m2 = jnp.sum(gn * u, axis=0, keepdims=True) * (1.0 / 192)
        gzs[i, :, ln] = (rinv[i, 0:1, ln] * (gn - m1 - u * m2)).astype(BF16)
        branch = osum[i, :, ln] + par[3, 0:192, :]
        outs[i, :, ln] = (fx[i + 3, :, ln].astype(F32) + par[4, 0:192, :] * branch).astype(BF16)
        return 0

    lax.fori_loop(0, 16, finish, 0)

    gz_up = remote(gzs.at[pl.ds(0, 3)], halo.at[1], halo_send.at[2], halo_recv.at[2], s, up)
    gz_down = remote(gzs.at[pl.ds(5, 3)], halo.at[0], halo_send.at[3], halo_recv.at[3], s, down)

    @pl.when(has_up)
    def _():
        gz_up.start()

    @pl.when(has_down)
    def _():
        gz_down.start()

    block_out = pltpu.make_async_copy(outs, out_block.at[0, 0], out_sem.at[0])
    block_out.start()
    stage4(0)
    stage1(2)

    lane = lax.broadcasted_iota(jnp.int32, (8, 128), 1)
    sub = lax.broadcasted_iota(jnp.int32, (8, 128), 0)

    def taps_grad(g, _):
        for i in range(8):
            spread(gzs[i, rows16(g), :], i, g, gs)
        mine = gs[g, 3 * 128 : 3 * 128 + 128, :]
        for b in range(7):
            at_own = lax.dot_general(mine, xs[g, b * 128 : b * 128 + 128, :], NT, preferred_element_type=F32)
            at_halo = lax.dot_general(mine, xh[g, b * 128 : b * 128 + 128, :], NT, preferred_element_type=F32)
            total = jnp.zeros((8, 128), F32)
            for i in range(8):
                use_own, use_halo = valid(i, lane)
                v = jnp.zeros((8, 128), F32)
                for h in range(2):
                    at = i * 16 + h * 8
                    same = lane % 16 == sub + h * 8
                    v = jnp.where(same & use_own, at_own[at : at + 8], v)
                    if not 3 <= i < 5:
                        v = jnp.where(same & use_halo, at_halo[at : at + 8], v)
                total = total + (pltpu.roll(v, (3 - i) * 16 % 128, 1) if i != 3 else v)
            gkr[pl.ds(g * 8 + b, 1), :] = jnp.sum(total, axis=0, keepdims=True)
        return 0

    gkr[...] = jnp.zeros_like(gkr)
    lax.fori_loop(0, 6, taps_grad, 0)
    stage5(0)
    stage3(1)
    stage2(2)
    lax.fori_loop(6, 12, taps_grad, 0)

    other = pl.ds((1 - core) * 48, 48)
    own_half = pl.ds(core * 48, 48)
    k_core = remote(gkr.at[other], k0, k_send.at[0], k_recv.at[0], partner, t)
    k_core.start()
    stage6(0)

    def back_own(g, _):
        v = jnp.dot(back[g], gs[g], preferred_element_type=F32)
        for i in range(8):
            zf[i, rows16(g), :] = ct[i, rows16(g), :].astype(F32) + v[i * 16 : i * 16 + 16, :]
        return 0

    lax.fori_loop(0, 6, back_own, 0)
    k_core.wait()
    kx[x] = gkr[own_half, :] + k0[...]
    kx_copies = [remote(kx.at[x], kx.at[x], k_send.at[1 + d], k_recv.at[1 + d], *x_peers[d]) for d in range(3)]
    for c in kx_copies:
        c.start()
    stage4(1)
    stage3(2)
    lax.fori_loop(6, 12, back_own, 0)

    @pl.when(has_up)
    def _():
        gz_down.wait_recv()

    @pl.when(t == 0)
    def _():
        halo[0] = jnp.zeros((3, 192, 256), BF16)

    @pl.when(has_down)
    def _():
        gz_up.wait_recv()

    @pl.when(t == 31)
    def _():
        halo[1] = jnp.zeros((3, 192, 256), BF16)

    def back_halo(g, _):
        for r, slot in HALO_SLOTS:
            spread(halo[r // 8, r % 11, rows16(g), :], slot, g, gh_)
        v = jnp.dot(back_h[g], gh_[g], preferred_element_type=F32)
        for i in range(8):
            fx[i, rows16(g), :] = (zf[i, rows16(g), :] + v[i * 16 : i * 16 + 16, :]).astype(BF16)
        return 0

    for c in kx_copies:
        c.wait()
    ky[y] = (kx[0] + kx[1]) + (kx[2] + kx[3])
    ky_copies = [remote(ky.at[y], ky.at[y], k_send.at[4 + d], k_recv.at[4 + d], *y_peers[d]) for d in range(3)]
    for c in ky_copies:
        c.start()
    stage5(1)
    lax.fori_loop(0, 6, back_halo, 0)
    stage4(2)
    for c in ky_copies:
        c.wait()
    kz[z] = (ky[0] + ky[1]) + (ky[2] + ky[3])
    kz_copies = [remote(kz.at[z], kz.at[z], k_send.at[7 + d], k_recv.at[7 + d], *z_peers[d]) for d in range(3)]
    for c in kz_copies:
        c.start()
    stage6(1)
    lax.fori_loop(6, 12, back_halo, 0)
    gin_out = pltpu.make_async_copy(fx.at[pl.ds(0, 8)], out_gin.at[0, 0], out_sem.at[1])
    gin_out.start()
    stage5(2)
    for c in kz_copies:
        c.wait()
    kfull[own_half, :] = (kz[0] + kz[1]) + (kz[2] + kz[3])
    k_back = remote(kfull.at[own_half], kfull.at[own_half], k_send.at[10], k_recv.at[10], partner, t)
    k_back.start()
    stage6(2)
    k_back.wait()
    out_gk[...] = kfull[...] * PIXEL_SCALE

    @pl.when(has_up)
    def _():
        to_up.wait_send()
        gz_up.wait_send()

    @pl.when(has_down)
    def _():
        to_down.wait_send()
        gz_down.wait_send()

    block_out.wait()
    gin_out.wait()


def on_device(features, dw_kernel, dw_bias, ln_gain, ln_bias, w_in, b_in, w_out, b_out, layer_scale, cotangent):
    row = lambda v: v.reshape(1, -1)
    turn = lambda v: jnp.swapaxes(v, 3, 4)
    any_, vmem = pl.BlockSpec(memory_space=pl.ANY), pl.BlockSpec(memory_space=pltpu.VMEM)
    V, DMA = pltpu.VMEM, pltpu.SemaphoreType.DMA
    groups = V((12, 896, 256), BF16)
    tables = V((12, 128, 896), BF16)
    scratch = [
        V((14, 192, 256), BF16), V((8, 192, 256), BF16), groups, groups, groups, groups, tables, tables, tables, tables,
        V((19, 8, 256), F32), V((8, 192, 256), F32), V((5, 256, 128), F32), V((768, 128), F32), V((768, 192), BF16),
        V((768, 192), BF16), V((8, 192, 256), BF16),
        V((8, 192, 256), BF16), V((8, 8, 256), F32), V((8, 192, 256), F32), V((8, 192, 256), F32), V((8, 192, 256), BF16),
        V((8, 192, 256), BF16), V((2, 3, 192, 256), F32), V((96, 128), F32), V((2, 3, 192, 256), BF16),
        V((3, 192, 256), BF16), V((3, 192, 256), BF16), V((3, 192, 256), F32), V((3, 192, 256), BF16), V((3, 3, 48, 256), BF16),
        V((3, 4, 48, 256), F32), V((3, 4, 48, 256), F32), V((2, 3, 192, 256), BF16),
        V((48, 128), F32), V((4, 48, 128), F32), V((4, 48, 128), F32), V((4, 48, 128), F32), V((96, 128), F32),
        DMA((2,)), DMA((2,)), DMA((4,)), DMA((4,)), DMA((3, 14)), DMA((3, 14)), DMA((11,)), DMA((11,)),
    ]
    block, gin, gwi, gwoT, gk = pl.pallas_call(
        kernel,
        out_shape=(
            jax.ShapeDtypeStruct((1, 1, 8, 192, 256), BF16), jax.ShapeDtypeStruct((1, 1, 8, 192, 256), BF16),
            jax.ShapeDtypeStruct((192, 768), F32), jax.ShapeDtypeStruct((192, 768), F32), jax.ShapeDtypeStruct((96, 128), F32),
        ),
        in_specs=[any_, any_] + [vmem] * 9,
        out_specs=(any_, any_, vmem, vmem, vmem),
        scratch_shapes=scratch,
        compiler_params=pltpu.CompilerParams(collective_id=0, has_side_effects=True, vmem_limit_bytes=60 << 20),
    )(
        turn(features), turn(cotangent), dw_kernel, row(dw_bias), row(ln_gain), row(ln_bias), w_in, row(b_in), w_out.T, row(b_out),
        row(layer_scale),
    )
    gk = gk.reshape(12, 8, 8, 16)[:, :7, :7].transpose(2, 1, 0, 3).reshape(7, 7, 192)
    return turn(block), turn(gin), gwi, gwoT.T, gk


def solution(mesh):
    split, whole = P("slide", "space", None, None, None), P()
    return jax.shard_map(
        on_device,
        mesh=mesh,
        in_specs=(split,) + (whole,) * 9 + (split,),
        out_specs=(split, split, whole, whole, whole),
        check_vma=False,
    )
```

```python
import jax
import jax.numpy as jnp
from jax import lax
from jax.experimental import pallas as pl
from jax.experimental.pallas import tpu as pltpu
from jax.sharding import PartitionSpec as P

EPSILON = 1e-06
F32 = jnp.float32
BF16 = jnp.bfloat16
MESH = pl.DeviceIdType.MESH
PIXEL_SCALE = float(262144) ** (-0.5)
NT = (((1,), (1,)), ((), ()))


def remote(src, dst, send, recv, slide, space):
    return pltpu.make_async_remote_copy(
        src_ref=src, dst_ref=dst, send_sem=send, recv_sem=recv,
        device_id={"slide": slide, "space": space}, device_id_type=MESH,
    )


def gelu_parts(h):
    r = h * 0.7071067811865476
    cdf = 0.5 + 0.5 * lax.erf(r)
    density = jnp.exp2(r * r * -1.4426950408889634)
    return h * cdf, cdf + (h * 0.3989422804014327) * density


def spread(value, slot, group, dst):
    lane = lax.broadcasted_iota(jnp.int32, (16, 128), 1)
    left, right = value[:, 0:128], value[:, 128:256]
    none = jnp.zeros_like(left)
    for b in range(7):
        d = b - 3
        first, second = left, right
        if d:
            first, second = pltpu.roll(left, -d % 128, 1), pltpu.roll(right, -d % 128, 1)
            if d > 0:
                first, second = jnp.where(lane < 128 - d, first, second), jnp.where(lane < 128 - d, second, none)
            else:
                first, second = jnp.where(lane < -d, none, first), jnp.where(lane < -d, first, second)
        at = b * 128 + slot * 16
        dst[group, at : at + 16, 0:128] = first
        dst[group, at : at + 16, 128:256] = second


def valid(i, lane):
    slot = lane // 16
    own = (slot >= i - 3) & (slot <= i + 3)
    halo = jnp.zeros_like(own)
    if i < 3:
        halo = slot >= i + 5
    if i >= 5:
        halo = slot <= i - 5
    return own, halo


def build_taps(dwk, flat, own, halo, flip):
    lane8 = lax.broadcasted_iota(jnp.int32, (8, 128), 1)
    for a in range(7):
        flat[a, 0:7, 0:192] = jnp.concatenate(
            [dwk[6 - a if flip else a, (6 - b if flip else b) : (6 - b if flip else b) + 1, :] for b in range(7)], axis=0
        )
    for g in range(12):
        base = jnp.zeros((8, 128), F32)
        tile, at = g // 8 * 128, g % 8 * 16
        for a in range(7):
            v = flat[a, :, tile : tile + 128]
            v = pltpu.roll(v, (a * 16 - at) % 128, 1)
            base = jnp.where((lane8 >= a * 16) & (lane8 < a * 16 + 16), v, base)
        flat[7 + g, :, 0:128] = base
    lane = lax.broadcasted_iota(jnp.int32, (16, 128), 1)
    same = lane % 16 == lax.broadcasted_iota(jnp.int32, (16, 128), 0)

    def group(g, _):
        base = flat[7 + g, :, 0:128]
        for i in range(8):
            moved = pltpu.roll(base, (i - 3) * 16 % 128, 1)
            for keep, dst in zip(valid(i, lane8), (own, halo)):
                if dst is halo and 3 <= i < 5:
                    dst[g, i * 16 : i * 16 + 16, :] = jnp.zeros((16, 896), BF16)
                    continue
                v = jnp.where(keep, moved, 0.0)
                for b in range(7):
                    row = jnp.broadcast_to(v[b : b + 1, :], (16, 128))
                    dst[g, i * 16 : i * 16 + 16, b * 128 : b * 128 + 128] = jnp.where(same, row, 0.0).astype(BF16)
        return 0

    lax.fori_loop(0, 12, group, 0)


def both(v):
    return jnp.concatenate([v, v], axis=1)


def rows16(g):
    return pl.ds(pl.multiple_of(g * 16, 16), 16)


HALO_SLOTS = ((0, 5), (1, 6), (2, 7), (11, 0), (12, 1), (13, 2))


def kernel(
    feat, cot, dwk, dwb, gain, lbias, w_in, b_in, woutT, b_out, lscale,
    out_block, out_gin, out_gwi, out_gwoT, out_gk,
    fx, ct, xs, xh, gs, gh_, taps, taps_h, back, back_h, flat, zf, par, bias, winT, wout, gout,
    nb, rinv, osum, nsum, outs, gzs, gw, gkr, halo,
    pay, r0, s1f, s1b, r1, ry, rz, full, k0, kx, ky, kz, kfull,
    in_sem, out_sem, halo_send, halo_recv, ar_send, ar_recv, k_send, k_recv,
):
    s, t = lax.axis_index("slide"), lax.axis_index("space")
    z_hi, core = s // 2, s % 2
    z_lo, x, y = t % 2, (t // 2) % 4, t // 8
    z = z_hi * 2 + z_lo
    partner = z_hi * 2 + (1 - core)
    x_peers = [(s, (y * 4 + (x + d) % 4) * 2 + z_lo) for d in (1, 2, 3)]
    y_peers = [(s, (((y + d) % 4) * 4 + x) * 2 + z_lo) for d in (1, 2, 3)]
    z_peers = [(((z + d) % 4) // 2 * 2 + core, (y * 4 + x) * 2 + ((z + d) % 4) % 2) for d in (1, 2, 3)]
    has_up, has_down = t > 0, t < 31
    up, down = jnp.maximum(t - 1, 0), jnp.minimum(t + 1, 31)

    own_in = pltpu.make_async_copy(feat.at[0, 0], fx.at[pl.ds(3, 8)], in_sem.at[0])
    own_in.start()
    cot_in = pltpu.make_async_copy(cot.at[0, 0], ct, in_sem.at[1])
    cot_in.start()

    barrier = pltpu.get_barrier_semaphore()
    for ps, pt in [(partner, t)] + x_peers + y_peers + z_peers:
        pl.semaphore_signal(barrier, inc=1, device_id={"slide": ps, "space": pt}, device_id_type=MESH)

    @pl.when(has_up)
    def _():
        pl.semaphore_signal(barrier, inc=1, device_id={"slide": s, "space": up}, device_id_type=MESH)

    @pl.when(has_down)
    def _():
        pl.semaphore_signal(barrier, inc=1, device_id={"slide": s, "space": down}, device_id_type=MESH)

    pl.semaphore_wait(barrier, 10 + jnp.minimum(t, 1) + jnp.minimum(31 - t, 1))

    to_up = remote(feat.at[0, 0, pl.ds(0, 3)], fx.at[pl.ds(11, 3)], halo_send.at[0], halo_recv.at[0], s, up)
    to_down = remote(feat.at[0, 0, pl.ds(5, 3)], fx.at[pl.ds(0, 3)], halo_send.at[1], halo_recv.at[1], s, down)

    @pl.when(has_up)
    def _():
        to_up.start()

    @pl.when(has_down)
    def _():
        to_down.start()

    for n, ref in enumerate((dwb, gain, lbias, b_out, lscale)):
        par[n, 0:128, :] = jnp.broadcast_to(ref[:, 0:128], (128, 128)).T
        par[n, 128:256, :] = jnp.broadcast_to(both(ref[:, 128:192]), (128, 128)).T
    for n in range(6):
        bias[n * 128 : n * 128 + 128, :] = jnp.broadcast_to(b_in[n * 128 : n * 128 + 128].reshape(1, 128), (128, 128)).T
    winT[...] = w_in[...].T
    wout[...] = woutT[...].T
    build_taps(dwk, flat, taps, taps_h, False)

    def clear(g, _):
        none = jnp.zeros((32, 256), BF16)
        for b in range(7):
            xh[g, b * 128 + 48 : b * 128 + 80, :] = none
            gh_[g, b * 128 + 48 : b * 128 + 80, :] = none
        return 0

    lax.fori_loop(0, 12, clear, 0)
    own_in.wait()

    def conv_own(g, _):
        for i in range(8):
            spread(fx[i + 3, rows16(g), :], i, g, xs)
        v = jnp.dot(taps[g], xs[g], preferred_element_type=F32)
        for i in range(8):
            zf[i, rows16(g), :] = v[i * 16 : i * 16 + 16, :] + both(par[0, rows16(g), :])
        return 0

    lax.fori_loop(0, 12, conv_own, 0)
    cot_in.wait()

    def scale_row(i, _):
        gout[i] = (both(par[4, 0:192, :]) * ct[i].astype(F32)).astype(BF16)
        return 0

    lax.fori_loop(0, 8, scale_row, 0)

    def norm(n, _):
        i = n // 2
        ln = pl.ds(pl.multiple_of(n % 2 * 128, 128), 128)
        v = zf[i, :, ln]
        v = v - jnp.sum(v, axis=0, keepdims=True) * (1.0 / 192)
        var = jnp.sum(v * v, axis=0, keepdims=True) * (1.0 / 192)
        r = lax.rsqrt(var + EPSILON)
        v = v * r
        zf[i, :, ln] = v
        rinv[i, :, ln] = jnp.broadcast_to(r, (8, 128))
        nb[i, :, ln] = (v * par[1, 0:192, :] + par[2, 0:192, :]).astype(BF16)
        return 0

    lax.fori_loop(6, 10, norm, 0)

    gw[...] = jnp.zeros_like(gw)
    osum[...] = jnp.zeros_like(osum)
    nsum[...] = jnp.zeros_like(nsum)

    def mlp_pair(f, p):
        units = pl.ds(pl.multiple_of(f * 256, 256), 256)
        q = 7 - p
        normed = jnp.concatenate([nb[p], nb[q]], axis=1)
        upper = jnp.concatenate([gout[p], gout[q]], axis=1)
        hidden = jnp.dot(winT[units, :], normed, preferred_element_type=F32) + both(both(bias[units, :]))
        value, slope = gelu_parts(hidden)
        act = value.astype(BF16)
        gh = (jnp.dot(wout[units, :], upper, preferred_element_type=F32) * slope).astype(BF16)
        out = jnp.dot(woutT[:, units], act, preferred_element_type=F32)
        osum[p] += out[:, 0:256]
        osum[q] += out[:, 256:512]
        out = jnp.dot(w_in[:, units], gh, preferred_element_type=F32)
        nsum[p] += out[:, 0:256]
        nsum[q] += out[:, 256:512]
        gw[0, f] += lax.dot_general(normed, gh, NT, preferred_element_type=F32)
        gw[1, f] += lax.dot_general(upper, act, NT, preferred_element_type=F32)

    def mlp_inner(k, _):
        mlp_pair(k, 3)
        return 0

    lax.fori_loop(0, 3, mlp_inner, 0)

    @pl.when(has_up)
    def _():
        to_down.wait_recv()

    @pl.when(t == 0)
    def _():
        fx[0:3] = jnp.zeros((3, 192, 256), BF16)

    @pl.when(has_down)
    def _():
        to_up.wait_recv()

    @pl.when(t == 31)
    def _():
        fx[11:14] = jnp.zeros((3, 192, 256), BF16)

    def conv_halo(g, _):
        for r, slot in HALO_SLOTS:
            spread(fx[r, rows16(g), :], slot, g, xh)
        v = jnp.dot(taps_h[g], xh[g], preferred_element_type=F32)
        for i in (0, 1, 2, 5, 6, 7):
            zf[i, rows16(g), :] += v[i * 16 : i * 16 + 16, :]
        return 0

    lax.fori_loop(0, 12, conv_halo, 0)

    lax.fori_loop(0, 6, norm, 0)
    lax.fori_loop(10, 16, norm, 0)

    def stage0(f):
        pay[f] = gw[1 - core, f].astype(BF16)
        core_copy(f).start()

    def core_copy(f):
        return remote(pay.at[f], r0.at[f], ar_send.at[f, 0], ar_recv.at[f, 0], partner, t)

    def x_copies(f):
        return [
            remote(s1b.at[f, pl.ds(((x + d + 1) % 4) * 48, 48)], r1.at[f, d], ar_send.at[f, 1 + d], ar_recv.at[f, 1 + d], *x_peers[d])
            for d in range(3)
        ]

    def y_copies(f):
        return [remote(ry.at[f, y], ry.at[f, y], ar_send.at[f, 4 + d], ar_recv.at[f, 4 + d], *y_peers[d]) for d in range(3)]

    def z_copies(f):
        return [remote(rz.at[f, z], rz.at[f, z], ar_send.at[f, 7 + d], ar_recv.at[f, 7 + d], *z_peers[d]) for d in range(3)]

    def x_back(f):
        mine = full.at[core, f, pl.ds(x * 48, 48)]
        return [remote(mine, mine, ar_send.at[f, 10 + d], ar_recv.at[f, 10 + d], *x_peers[d]) for d in range(3)]

    def core_back(f):
        return remote(full.at[core, f], full.at[core, f], ar_send.at[f, 13], ar_recv.at[f, 13], partner, t)

    def stage1(f):
        core_copy(f).wait()
        total = gw[core, f] + r0[f].astype(F32)
        s1f[f] = total
        s1b[f] = total.astype(BF16)
        for c in x_copies(f):
            c.start()

    def stage2(f):
        for c in x_copies(f):
            c.wait()
        total = s1f[f, pl.ds(x * 48, 48), :]
        for d in range(3):
            total = total + r1[f, d].astype(F32)
        ry[f, y] = total
        for c in y_copies(f):
            c.start()

    def stage3(f):
        for c in y_copies(f):
            c.wait()
        rz[f, z] = (ry[f, 0] + ry[f, 1]) + (ry[f, 2] + ry[f, 3])
        for c in z_copies(f):
            c.start()

    def stage4(f):
        for c in z_copies(f):
            c.wait()
        full[core, f, pl.ds(x * 48, 48), :] = ((rz[f, 0] + rz[f, 1]) + (rz[f, 2] + rz[f, 3])).astype(BF16)
        for c in x_back(f):
            c.start()

    def stage5(f):
        for c in x_back(f):
            c.wait()
        core_back(f).start()

    def stage6(f):
        core_back(f).wait()
        out_gwi[:, f * 256 : f * 256 + 256] = full[0, f].astype(F32) * PIXEL_SCALE
        out_gwoT[:, f * 256 : f * 256 + 256] = full[1, f].astype(F32) * PIXEL_SCALE

    after = {
        2: [(stage0, 0)], 4: [(stage1, 0)], 5: [(stage0, 1)], 7: [(stage2, 0), (stage1, 1)], 8: [(stage0, 2)],
    }

    def mlp(k, _):
        mlp_pair(k // 3, k % 3)
        for at, steps in after.items():

            @pl.when(k == at)
            def _():
                for step, chunk in steps:
                    step(chunk)

        return 0

    lax.fori_loop(0, 9, mlp, 0)

    def finish(n, _):
        i = n // 2
        ln = pl.ds(pl.multiple_of(n % 2 * 128, 128), 128)
        gn = nsum[i, :, ln] * par[1, 0:192, :]
        u = zf[i, :, ln]
        m1 = jnp.sum(gn, axis=0, keepdims=True) * (1.0 / 192)
        m2 = jnp.sum(gn * u, axis=0, keepdims=True) * (1.0 / 192)
        gzs[i, :, ln] = (rinv[i, 0:1, ln] * (gn - m1 - u * m2)).astype(BF16)
        return 0

    def finish_out(n, _):
        i = n // 2
        ln = pl.ds(pl.multiple_of(n % 2 * 128, 128), 128)
        branch = osum[i, :, ln] + par[3, 0:192, :]
        outs[i, :, ln] = (fx[i + 3, :, ln].astype(F32) + par[4, 0:192, :] * branch).astype(BF16)
        return 0

    lax.fori_loop(0, 16, finish, 0)

    gz_up = remote(gzs.at[pl.ds(0, 3)], halo.at[1], halo_send.at[2], halo_recv.at[2], s, up)
    gz_down = remote(gzs.at[pl.ds(5, 3)], halo.at[0], halo_send.at[3], halo_recv.at[3], s, down)

    @pl.when(has_up)
    def _():
        gz_up.start()

    @pl.when(has_down)
    def _():
        gz_down.start()

    stage1(2)
    stage2(1)
    stage3(0)

    lane = lax.broadcasted_iota(jnp.int32, (8, 128), 1)
    sub = lax.broadcasted_iota(jnp.int32, (8, 128), 0)

    def taps_grad(g, _):
        for i in range(8):
            spread(gzs[i, rows16(g), :], i, g, gs)
        mine = gs[g, 3 * 128 : 3 * 128 + 128, :]
        for b in range(7):
            at_own = lax.dot_general(mine, xs[g, b * 128 : b * 128 + 128, :], NT, preferred_element_type=F32)
            at_halo = lax.dot_general(mine, xh[g, b * 128 : b * 128 + 128, :], NT, preferred_element_type=F32)
            total = jnp.zeros((8, 128), F32)
            for i in range(8):
                use_own, use_halo = valid(i, lane)
                v = jnp.zeros((8, 128), F32)
                for h in range(2):
                    at = i * 16 + h * 8
                    same = lane % 16 == sub + h * 8
                    v = jnp.where(same & use_own, at_own[at : at + 8], v)
                    if not 3 <= i < 5:
                        v = jnp.where(same & use_halo, at_halo[at : at + 8], v)
                total = total + (pltpu.roll(v, (3 - i) * 16 % 128, 1) if i != 3 else v)
            gkr[pl.ds(g * 8 + b, 1), :] = jnp.sum(total, axis=0, keepdims=True)
        return 0

    gkr[...] = jnp.zeros_like(gkr)
    lax.fori_loop(0, 6, taps_grad, 0)
    stage2(2)
    stage3(1)
    stage4(0)
    lax.fori_loop(6, 12, taps_grad, 0)

    other = pl.ds((1 - core) * 48, 48)
    own_half = pl.ds(core * 48, 48)
    k_core = remote(gkr.at[other], k0, k_send.at[0], k_recv.at[0], partner, t)
    k_core.start()
    stage3(2)
    stage4(1)
    stage5(0)
    lax.fori_loop(0, 16, finish_out, 0)
    block_out = pltpu.make_async_copy(outs, out_block.at[0, 0], out_sem.at[0])
    block_out.start()

    def back_own(g, _):
        v = jnp.dot(back[g], gs[g], preferred_element_type=F32)
        for i in range(8):
            zf[i, rows16(g), :] = ct[i, rows16(g), :].astype(F32) + v[i * 16 : i * 16 + 16, :]
        return 0

    k_core.wait()
    kx[x] = gkr[own_half, :] + k0[...]
    kx_copies = [remote(kx.at[x], kx.at[x], k_send.at[1 + d], k_recv.at[1 + d], *x_peers[d]) for d in range(3)]
    for c in kx_copies:
        c.start()
    build_taps(dwk, flat, back, back_h, True)
    stage4(2)
    stage6(0)
    lax.fori_loop(0, 12, back_own, 0)
    for c in kx_copies:
        c.wait()
    ky[y] = (kx[0] + kx[1]) + (kx[2] + kx[3])
    ky_copies = [remote(ky.at[y], ky.at[y], k_send.at[4 + d], k_recv.at[4 + d], *y_peers[d]) for d in range(3)]
    for c in ky_copies:
        c.start()
    stage5(1)
    stage5(2)
    for c in ky_copies:
        c.wait()
    kz[z] = (ky[0] + ky[1]) + (ky[2] + ky[3])
    kz_copies = [remote(kz.at[z], kz.at[z], k_send.at[7 + d], k_recv.at[7 + d], *z_peers[d]) for d in range(3)]
    for c in kz_copies:
        c.start()
    stage6(1)
    stage6(2)

    @pl.when(has_up)
    def _():
        gz_down.wait_recv()

    @pl.when(t == 0)
    def _():
        halo[0] = jnp.zeros((3, 192, 256), BF16)

    @pl.when(has_down)
    def _():
        gz_up.wait_recv()

    @pl.when(t == 31)
    def _():
        halo[1] = jnp.zeros((3, 192, 256), BF16)

    def back_halo(g, _):
        for r, slot in HALO_SLOTS:
            spread(halo[r // 8, r % 11, rows16(g), :], slot, g, gh_)
        v = jnp.dot(back_h[g], gh_[g], preferred_element_type=F32)
        for i in range(8):
            fx[i, rows16(g), :] = (zf[i, rows16(g), :] + v[i * 16 : i * 16 + 16, :]).astype(BF16)
        return 0

    lax.fori_loop(0, 6, back_halo, 0)
    for c in kz_copies:
        c.wait()
    kfull[own_half, :] = (kz[0] + kz[1]) + (kz[2] + kz[3])
    k_back = remote(kfull.at[own_half], kfull.at[own_half], k_send.at[10], k_recv.at[10], partner, t)
    k_back.start()
    lax.fori_loop(6, 12, back_halo, 0)
    gin_out = pltpu.make_async_copy(fx.at[pl.ds(0, 8)], out_gin.at[0, 0], out_sem.at[1])
    gin_out.start()
    k_back.wait()
    for a in range(7):
        for tile, width in ((0, 128), (128, 64)):
            base = jnp.zeros((8, 128), F32)
            for g in range(tile // 16, (tile + width) // 16):
                at = g % 8 * 16
                v = pltpu.roll(kfull[g * 8 : g * 8 + 8, :], (at - a * 16) % 128, 1)
                base = jnp.where((lane >= at) & (lane < at + 16), v, base)
            out_gk[a, :, tile : tile + width] = base[0:7, 0:width] * PIXEL_SCALE

    @pl.when(has_up)
    def _():
        to_up.wait_send()
        gz_up.wait_send()

    @pl.when(has_down)
    def _():
        to_down.wait_send()
        gz_down.wait_send()

    block_out.wait()
    gin_out.wait()


def hand_over_kernel(*refs):
    ins, outs, held, sems = refs[:5], refs[5:10], refs[10:15], refs[15]
    loads = [pltpu.make_async_copy(i, h, sems.at[0, n]) for n, (i, h) in enumerate(zip(ins, held))]
    stores = [pltpu.make_async_copy(h, o, sems.at[1, n]) for n, (h, o) in enumerate(zip(held, outs))]
    for c in loads:
        c.start()
    for load, store in zip(loads, stores):
        load.wait()
        store.start()
    for c in stores:
        c.wait()


def hand_over(*values):
    shapes = tuple(jax.ShapeDtypeStruct(v.shape, v.dtype) for v in values)
    return pl.pallas_call(
        hand_over_kernel,
        out_shape=shapes,
        in_specs=[pl.BlockSpec(memory_space=pl.ANY)] * 5,
        out_specs=(pl.BlockSpec(memory_space=pl.ANY),) * 5,
        scratch_shapes=[pltpu.VMEM(v.shape, v.dtype) for v in values] + [pltpu.SemaphoreType.DMA((2, 5))],
    )(*values)


def on_device(features, dw_kernel, dw_bias, ln_gain, ln_bias, w_in, b_in, w_out, b_out, layer_scale, cotangent):
    row = lambda v: v.reshape(1, -1)
    turn = lambda v: jnp.swapaxes(v, 3, 4)
    any_, vmem = pl.BlockSpec(memory_space=pl.ANY), pl.BlockSpec(memory_space=pltpu.VMEM)
    V, DMA = pltpu.VMEM, pltpu.SemaphoreType.DMA
    groups = V((12, 896, 256), BF16)
    tables = V((12, 128, 896), BF16)
    scratch = [
        V((14, 192, 256), BF16), V((8, 192, 256), BF16), groups, groups, groups, groups, tables, tables, tables, tables,
        V((19, 8, 256), F32), V((8, 192, 256), F32), V((5, 256, 128), F32), V((768, 128), F32), V((768, 192), BF16),
        V((768, 192), BF16), V((8, 192, 256), BF16),
        V((8, 192, 256), BF16), V((8, 8, 256), F32), V((8, 192, 256), F32), V((8, 192, 256), F32), V((8, 192, 256), BF16),
        V((8, 192, 256), BF16), V((2, 3, 192, 256), F32), V((96, 128), F32), V((2, 3, 192, 256), BF16),
        V((3, 192, 256), BF16), V((3, 192, 256), BF16), V((3, 192, 256), F32), V((3, 192, 256), BF16), V((3, 3, 48, 256), BF16),
        V((3, 4, 48, 256), F32), V((3, 4, 48, 256), F32), V((2, 3, 192, 256), BF16),
        V((48, 128), F32), V((4, 48, 128), F32), V((4, 48, 128), F32), V((4, 48, 128), F32), V((96, 128), F32),
        DMA((2,)), DMA((2,)), DMA((4,)), DMA((4,)), DMA((3, 14)), DMA((3, 14)), DMA((11,)), DMA((11,)),
    ]
    block, gin, gwi, gwoT, gk = pl.pallas_call(
        kernel,
        out_shape=(
            jax.ShapeDtypeStruct((1, 1, 8, 192, 256), BF16), jax.ShapeDtypeStruct((1, 1, 8, 192, 256), BF16),
            jax.ShapeDtypeStruct((192, 768), F32), jax.ShapeDtypeStruct((192, 768), F32), jax.ShapeDtypeStruct((7, 7, 192), F32),
        ),
        in_specs=[any_, any_] + [vmem] * 9,
        out_specs=(any_, any_, vmem, vmem, vmem),
        scratch_shapes=scratch,
        compiler_params=pltpu.CompilerParams(collective_id=0, has_side_effects=True, vmem_limit_bytes=60 << 20),
    )(
        turn(features), turn(cotangent), dw_kernel, row(dw_bias), row(ln_gain), row(ln_bias), w_in, b_in, w_out.T, row(b_out),
        row(layer_scale),
    )
    block, gin, gwi, gwoT, gk = hand_over(block, gin, gwi, gwoT, gk)
    return turn(block), turn(gin), gwi, gwoT.T, gk


def solution(mesh):
    split, whole = P("slide", "space", None, None, None), P()
    return jax.shard_map(
        on_device,
        mesh=mesh,
        in_specs=(split,) + (whole,) * 9 + (split,),
        out_specs=(split, split, whole, whole, whole),
        check_vma=False,
    )
```

```python
import jax
import jax.numpy as jnp
from jax import lax
from jax.experimental import pallas as pl
from jax.experimental.pallas import tpu as pltpu
from jax.sharding import PartitionSpec as P

EPSILON = 1e-06
F32 = jnp.float32
BF16 = jnp.bfloat16
MESH = pl.DeviceIdType.MESH
PIXEL_SCALE = float(262144) ** (-0.5)
NT = (((1,), (1,)), ((), ()))


def remote(src, dst, send, recv, slide, space):
    return pltpu.make_async_remote_copy(
        src_ref=src, dst_ref=dst, send_sem=send, recv_sem=recv,
        device_id={"slide": slide, "space": space}, device_id_type=MESH,
    )


def gelu_parts(h):
    r = h * 0.7071067811865476
    cdf = 0.5 + 0.5 * lax.erf(r)
    density = jnp.exp2(r * r * -1.4426950408889634)
    return h * cdf, cdf + (h * 0.3989422804014327) * density


def spread(value, slot, group, dst):
    lane = lax.broadcasted_iota(jnp.int32, (16, 128), 1)
    left, right = value[:, 0:128], value[:, 128:256]
    none = jnp.zeros_like(left)
    for b in range(7):
        d = b - 3
        first, second = left, right
        if d:
            first, second = pltpu.roll(left, -d % 128, 1), pltpu.roll(right, -d % 128, 1)
            if d > 0:
                first, second = jnp.where(lane < 128 - d, first, second), jnp.where(lane < 128 - d, second, none)
            else:
                first, second = jnp.where(lane < -d, none, first), jnp.where(lane < -d, first, second)
        at = b * 128 + slot * 16
        dst[group, at : at + 16, 0:128] = first
        dst[group, at : at + 16, 128:256] = second


def valid(i, lane):
    slot = lane // 16
    own = (slot >= i - 3) & (slot <= i + 3)
    halo = jnp.zeros_like(own)
    if i < 3:
        halo = slot >= i + 5
    if i >= 5:
        halo = slot <= i - 5
    return own, halo


def build_taps(dwk, flat, own, halo, flip):
    lane8 = lax.broadcasted_iota(jnp.int32, (8, 128), 1)
    for a in range(7):
        flat[a, 0:7, 0:192] = jnp.concatenate(
            [dwk[6 - a if flip else a, (6 - b if flip else b) : (6 - b if flip else b) + 1, :] for b in range(7)], axis=0
        )
    for g in range(12):
        base = jnp.zeros((8, 128), F32)
        tile, at = g // 8 * 128, g % 8 * 16
        for a in range(7):
            v = flat[a, :, tile : tile + 128]
            v = pltpu.roll(v, (a * 16 - at) % 128, 1)
            base = jnp.where((lane8 >= a * 16) & (lane8 < a * 16 + 16), v, base)
        flat[7 + g, :, 0:128] = base
    lane = lax.broadcasted_iota(jnp.int32, (16, 128), 1)
    same = lane % 16 == lax.broadcasted_iota(jnp.int32, (16, 128), 0)

    def group(g, _):
        base = flat[7 + g, :, 0:128]
        for i in range(8):
            moved = pltpu.roll(base, (i - 3) * 16 % 128, 1)
            for keep, dst in zip(valid(i, lane8), (own, halo)):
                if dst is halo and 3 <= i < 5:
                    dst[g, i * 16 : i * 16 + 16, :] = jnp.zeros((16, 896), BF16)
                    continue
                v = jnp.where(keep, moved, 0.0)
                for b in range(7):
                    row = jnp.broadcast_to(v[b : b + 1, :], (16, 128))
                    dst[g, i * 16 : i * 16 + 16, b * 128 : b * 128 + 128] = jnp.where(same, row, 0.0).astype(BF16)
        return 0

    lax.fori_loop(0, 12, group, 0)


def both(v):
    return jnp.concatenate([v, v], axis=1)


def rows16(g):
    return pl.ds(pl.multiple_of(g * 16, 16), 16)


HALO_SLOTS = ((0, 5), (1, 6), (2, 7), (11, 0), (12, 1), (13, 2))


def kernel(
    feat, cot, dwk, dwb, gain, lbias, w_in, b_in, woutT, b_out, lscale,
    out_block, out_gin, out_gwi, out_gwoT, out_gk,
    fx, ct, xs, xh, gs, gh_, taps, taps_h, back, back_h, flat, zf, par, bias, winT, wout, gout,
    nb, rinv, osum, nsum, outs, gzs, gw, gkr, halo,
    pay, r0, s1f, s1b, r1, s2, r2, rz, fa, full, k0, kx, ky, kz, kfull,
    in_sem, out_sem, halo_send, halo_recv, ar_send, ar_recv, k_send, k_recv,
):
    s, t = lax.axis_index("slide"), lax.axis_index("space")
    z_hi, core = s // 2, s % 2
    z_lo, x, y = t % 2, (t // 2) % 4, t // 8
    z = z_hi * 2 + z_lo
    partner = z_hi * 2 + (1 - core)
    x_peers = [(s, (y * 4 + (x + d) % 4) * 2 + z_lo) for d in (1, 2, 3)]
    y_peers = [(s, (((y + d) % 4) * 4 + x) * 2 + z_lo) for d in (1, 2, 3)]
    z_peers = [(((z + d) % 4) // 2 * 2 + core, (y * 4 + x) * 2 + ((z + d) % 4) % 2) for d in (1, 2, 3)]
    has_up, has_down = t > 0, t < 31
    up, down = jnp.maximum(t - 1, 0), jnp.minimum(t + 1, 31)

    own_in = pltpu.make_async_copy(feat.at[0, 0], fx.at[pl.ds(3, 8)], in_sem.at[0])
    own_in.start()
    cot_in = pltpu.make_async_copy(cot.at[0, 0], ct, in_sem.at[1])
    cot_in.start()

    barrier = pltpu.get_barrier_semaphore()
    for ps, pt in [(partner, t)] + x_peers + y_peers + z_peers:
        pl.semaphore_signal(barrier, inc=1, device_id={"slide": ps, "space": pt}, device_id_type=MESH)

    @pl.when(has_up)
    def _():
        pl.semaphore_signal(barrier, inc=1, device_id={"slide": s, "space": up}, device_id_type=MESH)

    @pl.when(has_down)
    def _():
        pl.semaphore_signal(barrier, inc=1, device_id={"slide": s, "space": down}, device_id_type=MESH)

    pl.semaphore_wait(barrier, 10 + jnp.minimum(t, 1) + jnp.minimum(31 - t, 1))

    to_up = remote(feat.at[0, 0, pl.ds(0, 3)], fx.at[pl.ds(11, 3)], halo_send.at[0], halo_recv.at[0], s, up)
    to_down = remote(feat.at[0, 0, pl.ds(5, 3)], fx.at[pl.ds(0, 3)], halo_send.at[1], halo_recv.at[1], s, down)

    @pl.when(has_up)
    def _():
        to_up.start()

    @pl.when(has_down)
    def _():
        to_down.start()

    for n, ref in enumerate((dwb, gain, lbias, b_out, lscale)):
        par[n, 0:128, :] = jnp.broadcast_to(ref[:, 0:128], (128, 128)).T
        par[n, 128:256, :] = jnp.broadcast_to(both(ref[:, 128:192]), (128, 128)).T
    for n in range(6):
        bias[n * 128 : n * 128 + 128, :] = jnp.broadcast_to(b_in[n * 128 : n * 128 + 128].reshape(1, 128), (128, 128)).T
    winT[...] = w_in[...].T
    wout[...] = woutT[...].T
    build_taps(dwk, flat, taps, taps_h, False)

    def clear(g, _):
        none = jnp.zeros((32, 256), BF16)
        for b in range(7):
            xh[g, b * 128 + 48 : b * 128 + 80, :] = none
            gh_[g, b * 128 + 48 : b * 128 + 80, :] = none
        return 0

    lax.fori_loop(0, 12, clear, 0)
    own_in.wait()

    def conv_own(g, _):
        for i in range(8):
            spread(fx[i + 3, rows16(g), :], i, g, xs)
        v = jnp.dot(taps[g], xs[g], preferred_element_type=F32)
        for i in range(8):
            zf[i, rows16(g), :] = v[i * 16 : i * 16 + 16, :] + both(par[0, rows16(g), :])
        return 0

    lax.fori_loop(0, 12, conv_own, 0)
    cot_in.wait()

    def scale_row(i, _):
        gout[i] = (both(par[4, 0:192, :]) * ct[i].astype(F32)).astype(BF16)
        return 0

    lax.fori_loop(0, 8, scale_row, 0)

    def norm(n, _):
        i = n // 2
        ln = pl.ds(pl.multiple_of(n % 2 * 128, 128), 128)
        v = zf[i, :, ln]
        v = v - jnp.sum(v, axis=0, keepdims=True) * (1.0 / 192)
        var = jnp.sum(v * v, axis=0, keepdims=True) * (1.0 / 192)
        r = lax.rsqrt(var + EPSILON)
        v = v * r
        zf[i, :, ln] = v
        rinv[i, :, ln] = jnp.broadcast_to(r, (8, 128))
        nb[i, :, ln] = (v * par[1, 0:192, :] + par[2, 0:192, :]).astype(BF16)
        return 0

    lax.fori_loop(6, 10, norm, 0)

    gw[...] = jnp.zeros_like(gw)
    osum[...] = jnp.zeros_like(osum)
    nsum[...] = jnp.zeros_like(nsum)

    def mlp_pair(f, p):
        units = pl.ds(pl.multiple_of(f * 256, 256), 256)
        q = 7 - p
        normed = jnp.concatenate([nb[p], nb[q]], axis=1)
        upper = jnp.concatenate([gout[p], gout[q]], axis=1)
        hidden = jnp.dot(winT[units, :], normed, preferred_element_type=F32) + both(both(bias[units, :]))
        value, slope = gelu_parts(hidden)
        act = value.astype(BF16)
        gh = (jnp.dot(wout[units, :], upper, preferred_element_type=F32) * slope).astype(BF16)
        out = jnp.dot(woutT[:, units], act, preferred_element_type=F32)
        osum[p] += out[:, 0:256]
        osum[q] += out[:, 256:512]
        out = jnp.dot(w_in[:, units], gh, preferred_element_type=F32)
        nsum[p] += out[:, 0:256]
        nsum[q] += out[:, 256:512]
        gw[0, f] += lax.dot_general(normed, gh, NT, preferred_element_type=F32)
        gw[1, f] += lax.dot_general(upper, act, NT, preferred_element_type=F32)

    def mlp_inner(k, _):
        mlp_pair(k, 3)
        return 0

    lax.fori_loop(0, 3, mlp_inner, 0)

    @pl.when(has_up)
    def _():
        to_down.wait_recv()

    @pl.when(t == 0)
    def _():
        fx[0:3] = jnp.zeros((3, 192, 256), BF16)

    @pl.when(has_down)
    def _():
        to_up.wait_recv()

    @pl.when(t == 31)
    def _():
        fx[11:14] = jnp.zeros((3, 192, 256), BF16)

    def conv_halo(g, _):
        for r, slot in HALO_SLOTS:
            spread(fx[r, rows16(g), :], slot, g, xh)
        v = jnp.dot(taps_h[g], xh[g], preferred_element_type=F32)
        for i in (0, 1, 2, 5, 6, 7):
            zf[i, rows16(g), :] += v[i * 16 : i * 16 + 16, :]
        return 0

    lax.fori_loop(0, 12, conv_halo, 0)

    lax.fori_loop(0, 6, norm, 0)
    lax.fori_loop(10, 16, norm, 0)

    def stage0(f):
        pay[f] = gw[1 - core, f].astype(BF16)
        core_copy(f).start()

    def core_copy(f):
        return remote(pay.at[f], r0.at[f], ar_send.at[f, 0], ar_recv.at[f, 0], partner, t)

    def y_copies(f):
        return [
            remote(s1b.at[f, pl.ds(((y + d + 1) % 4) * 48, 48)], r1.at[f, d], ar_send.at[f, 1 + d], ar_recv.at[f, 1 + d], *y_peers[d])
            for d in range(3)
        ]

    def x_copies(f):
        return [
            remote(s2.at[f, (x + d + 1) % 4], r2.at[f, d], ar_send.at[f, 4 + d], ar_recv.at[f, 4 + d], *x_peers[d]) for d in range(3)
        ]

    def z_copies(f):
        return [remote(rz.at[f, z], rz.at[f, z], ar_send.at[f, 7 + d], ar_recv.at[f, 7 + d], *z_peers[d]) for d in range(3)]

    def x_back(f):
        return [remote(fa.at[f, x], fa.at[f, x], ar_send.at[f, 10 + d], ar_recv.at[f, 10 + d], *x_peers[d]) for d in range(3)]

    def y_back(f):
        mine = full.at[core, f, pl.ds(y * 48, 48)]
        return [remote(mine, mine, ar_send.at[f, 13 + d], ar_recv.at[f, 13 + d], *y_peers[d]) for d in range(3)]

    def core_back(f):
        return remote(full.at[core, f], full.at[core, f], ar_send.at[f, 16], ar_recv.at[f, 16], partner, t)

    def stage1(f):
        core_copy(f).wait()
        total = gw[core, f] + r0[f].astype(F32)
        s1f[f] = total
        s1b[f] = total.astype(BF16)
        for c in y_copies(f):
            c.start()

    def stage2(f):
        for c in y_copies(f):
            c.wait()
        total = s1f[f, pl.ds(y * 48, 48), :]
        for d in range(3):
            total = total + r1[f, d].astype(F32)
        for part in range(4):
            at, ln = part % 2 * 24, part // 2 * 128
            s2[f, part] = total[at : at + 24, ln : ln + 128]
        for c in x_copies(f):
            c.start()

    def stage3(f):
        for c in x_copies(f):
            c.wait()
        rz[f, z] = (s2[f, x] + r2[f, 0]) + (r2[f, 1] + r2[f, 2])
        for c in z_copies(f):
            c.start()

    def stage4(f):
        for c in z_copies(f):
            c.wait()
        fa[f, x] = (rz[f, 0] + rz[f, 1]) + (rz[f, 2] + rz[f, 3])
        for c in x_back(f):
            c.start()

    def stage5(f):
        for c in x_back(f):
            c.wait()
        rows = [jnp.concatenate([fa[f, part], fa[f, part + 2]], axis=1) for part in range(2)]
        full[core, f, pl.ds(pl.multiple_of(y * 48, 16), 48), :] = jnp.concatenate(rows, axis=0).astype(BF16)
        for c in y_back(f):
            c.start()

    def stage6(f):
        for c in y_back(f):
            c.wait()
        core_back(f).start()

    def stage7(f):
        core_back(f).wait()
        out_gwi[:, f * 256 : f * 256 + 256] = full[0, f].astype(F32) * PIXEL_SCALE
        out_gwoT[:, f * 256 : f * 256 + 256] = full[1, f].astype(F32) * PIXEL_SCALE

    after = {
        2: [(stage0, 0)], 4: [(stage1, 0)], 5: [(stage0, 1)], 7: [(stage2, 0), (stage1, 1)], 8: [(stage0, 2)],
    }

    def mlp(k, _):
        mlp_pair(k // 3, k % 3)
        for at, steps in after.items():

            @pl.when(k == at)
            def _():
                for step, chunk in steps:
                    step(chunk)

        return 0

    lax.fori_loop(0, 9, mlp, 0)

    def finish(n, _):
        i = n // 2
        ln = pl.ds(pl.multiple_of(n % 2 * 128, 128), 128)
        gn = nsum[i, :, ln] * par[1, 0:192, :]
        u = zf[i, :, ln]
        m1 = jnp.sum(gn, axis=0, keepdims=True) * (1.0 / 192)
        m2 = jnp.sum(gn * u, axis=0, keepdims=True) * (1.0 / 192)
        gzs[i, :, ln] = (rinv[i, 0:1, ln] * (gn - m1 - u * m2)).astype(BF16)
        return 0

    def finish_out(n, _):
        i = n // 2
        ln = pl.ds(pl.multiple_of(n % 2 * 128, 128), 128)
        branch = osum[i, :, ln] + par[3, 0:192, :]
        outs[i, :, ln] = (fx[i + 3, :, ln].astype(F32) + par[4, 0:192, :] * branch).astype(BF16)
        return 0

    lax.fori_loop(0, 16, finish, 0)

    gz_up = [remote(gzs.at[n], halo.at[1, n], halo_send.at[2 + n], halo_recv.at[2 + n], s, up) for n in range(3)]
    gz_down = [remote(gzs.at[7 - n], halo.at[0, 2 - n], halo_send.at[5 + n], halo_recv.at[5 + n], s, down) for n in range(3)]

    def send_row(n):
        @pl.when(has_up)
        def _():
            gz_up[n].start()

        @pl.when(has_down)
        def _():
            gz_down[n].start()

    send_row(0)
    stage1(2)
    stage2(1)
    stage3(0)

    lane = lax.broadcasted_iota(jnp.int32, (8, 128), 1)
    sub = lax.broadcasted_iota(jnp.int32, (8, 128), 0)

    def taps_grad(g, _):
        for i in range(8):
            spread(gzs[i, rows16(g), :], i, g, gs)
        mine = gs[g, 3 * 128 : 3 * 128 + 128, :]
        for b in range(7):
            at_own = lax.dot_general(mine, xs[g, b * 128 : b * 128 + 128, :], NT, preferred_element_type=F32)
            at_halo = lax.dot_general(mine, xh[g, b * 128 : b * 128 + 128, :], NT, preferred_element_type=F32)
            total = jnp.zeros((8, 128), F32)
            for i in range(8):
                use_own, use_halo = valid(i, lane)
                v = jnp.zeros((8, 128), F32)
                for h in range(2):
                    at = i * 16 + h * 8
                    same = lane % 16 == sub + h * 8
                    v = jnp.where(same & use_own, at_own[at : at + 8], v)
                    if not 3 <= i < 5:
                        v = jnp.where(same & use_halo, at_halo[at : at + 8], v)
                total = total + (pltpu.roll(v, (3 - i) * 16 % 128, 1) if i != 3 else v)
            gkr[pl.ds(g * 8 + b, 1), :] = jnp.sum(total, axis=0, keepdims=True)
        return 0

    gkr[...] = jnp.zeros_like(gkr)
    def taps_step(g, _):
        taps_grad(g, 0)

        @pl.when(g == 3)
        def _():
            send_row(1)
            stage2(2)
            stage3(1)
            stage4(0)

        @pl.when(g == 8)
        def _():
            send_row(2)
            stage3(2)
            stage4(1)
            stage5(0)

        return 0

    lax.fori_loop(0, 12, taps_step, 0)

    other = pl.ds((1 - core) * 48, 48)
    own_half = pl.ds(core * 48, 48)
    k_core = remote(gkr.at[other], k0, k_send.at[0], k_recv.at[0], partner, t)
    k_core.start()
    lax.fori_loop(0, 16, finish_out, 0)
    block_out = pltpu.make_async_copy(outs, out_block.at[0, 0], out_sem.at[0])
    block_out.start()

    def back_own(g, _):
        v = jnp.dot(back[g], gs[g], preferred_element_type=F32)
        for i in range(8):
            zf[i, rows16(g), :] = ct[i, rows16(g), :].astype(F32) + v[i * 16 : i * 16 + 16, :]
        return 0

    k_core.wait()
    ky[y] = gkr[own_half, :] + k0[...]
    ky_copies = [remote(ky.at[y], ky.at[y], k_send.at[1 + d], k_recv.at[1 + d], *y_peers[d]) for d in range(3)]
    for c in ky_copies:
        c.start()
    stage4(2)
    stage5(1)
    stage6(0)
    build_taps(dwk, flat, back, back_h, True)
    for c in ky_copies:
        c.wait()
    kx[x] = (ky[0] + ky[1]) + (ky[2] + ky[3])
    kx_copies = [remote(kx.at[x], kx.at[x], k_send.at[4 + d], k_recv.at[4 + d], *x_peers[d]) for d in range(3)]
    for c in kx_copies:
        c.start()
    stage5(2)
    stage6(1)
    stage7(0)
    lax.fori_loop(0, 12, back_own, 0)
    for c in kx_copies:
        c.wait()
    kz[z] = (kx[0] + kx[1]) + (kx[2] + kx[3])
    kz_copies = [remote(kz.at[z], kz.at[z], k_send.at[7 + d], k_recv.at[7 + d], *z_peers[d]) for d in range(3)]
    for c in kz_copies:
        c.start()
    stage6(2)
    stage7(1)
    stage7(2)

    @pl.when(has_up)
    def _():
        for c in gz_down:
            c.wait_recv()

    @pl.when(t == 0)
    def _():
        halo[0] = jnp.zeros((3, 192, 256), BF16)

    @pl.when(has_down)
    def _():
        for c in gz_up:
            c.wait_recv()

    @pl.when(t == 31)
    def _():
        halo[1] = jnp.zeros((3, 192, 256), BF16)

    def back_halo(g, _):
        for r, slot in HALO_SLOTS:
            spread(halo[r // 8, r % 11, rows16(g), :], slot, g, gh_)
        v = jnp.dot(back_h[g], gh_[g], preferred_element_type=F32)
        for i in range(8):
            fx[i, rows16(g), :] = (zf[i, rows16(g), :] + v[i * 16 : i * 16 + 16, :]).astype(BF16)
        return 0

    lax.fori_loop(0, 6, back_halo, 0)
    for c in kz_copies:
        c.wait()
    kfull[own_half, :] = (kz[0] + kz[1]) + (kz[2] + kz[3])
    k_back = remote(kfull.at[own_half], kfull.at[own_half], k_send.at[10], k_recv.at[10], partner, t)
    k_back.start()
    lax.fori_loop(6, 12, back_halo, 0)
    gin_out = pltpu.make_async_copy(fx.at[pl.ds(0, 8)], out_gin.at[0, 0], out_sem.at[1])
    gin_out.start()
    k_back.wait()
    for a in range(7):
        for tile, width in ((0, 128), (128, 64)):
            base = jnp.zeros((8, 128), F32)
            for g in range(tile // 16, (tile + width) // 16):
                at = g % 8 * 16
                v = pltpu.roll(kfull[g * 8 : g * 8 + 8, :], (at - a * 16) % 128, 1)
                base = jnp.where((lane >= at) & (lane < at + 16), v, base)
            out_gk[a, :, tile : tile + width] = base[0:7, 0:width] * PIXEL_SCALE

    @pl.when(has_up)
    def _():
        to_up.wait_send()
        for c in gz_up:
            c.wait_send()

    @pl.when(has_down)
    def _():
        to_down.wait_send()
        for c in gz_down:
            c.wait_send()

    block_out.wait()
    gin_out.wait()


def hand_over_kernel(*refs):
    ins, outs, held, sems = refs[:5], refs[5:10], refs[10:15], refs[15]
    loads = [pltpu.make_async_copy(i, h, sems.at[0, n]) for n, (i, h) in enumerate(zip(ins, held))]
    stores = [pltpu.make_async_copy(h, o, sems.at[1, n]) for n, (h, o) in enumerate(zip(held, outs))]
    for c in loads:
        c.start()
    for load, store in zip(loads, stores):
        load.wait()
        store.start()
    for c in stores:
        c.wait()


def hand_over(*values):
    shapes = tuple(jax.ShapeDtypeStruct(v.shape, v.dtype) for v in values)
    return pl.pallas_call(
        hand_over_kernel,
        out_shape=shapes,
        in_specs=[pl.BlockSpec(memory_space=pl.ANY)] * 5,
        out_specs=(pl.BlockSpec(memory_space=pl.ANY),) * 5,
        scratch_shapes=[pltpu.VMEM(v.shape, v.dtype) for v in values] + [pltpu.SemaphoreType.DMA((2, 5))],
    )(*values)


def on_device(features, dw_kernel, dw_bias, ln_gain, ln_bias, w_in, b_in, w_out, b_out, layer_scale, cotangent):
    row = lambda v: v.reshape(1, -1)
    turn = lambda v: jnp.swapaxes(v, 3, 4)
    any_, vmem = pl.BlockSpec(memory_space=pl.ANY), pl.BlockSpec(memory_space=pltpu.VMEM)
    V, DMA = pltpu.VMEM, pltpu.SemaphoreType.DMA
    groups = V((12, 896, 256), BF16)
    tables = V((12, 128, 896), BF16)
    scratch = [
        V((14, 192, 256), BF16), V((8, 192, 256), BF16), groups, groups, groups, groups, tables, tables, tables, tables,
        V((19, 8, 256), F32), V((8, 192, 256), F32), V((5, 256, 128), F32), V((768, 128), F32), V((768, 192), BF16),
        V((768, 192), BF16), V((8, 192, 256), BF16),
        V((8, 192, 256), BF16), V((8, 8, 256), F32), V((8, 192, 256), F32), V((8, 192, 256), F32), V((8, 192, 256), BF16),
        V((8, 192, 256), BF16), V((2, 3, 192, 256), F32), V((96, 128), F32), V((2, 3, 192, 256), BF16),
        V((3, 192, 256), BF16), V((3, 192, 256), BF16), V((3, 192, 256), F32), V((3, 192, 256), BF16), V((3, 3, 48, 256), BF16),
        V((3, 4, 24, 128), F32), V((3, 3, 24, 128), F32), V((3, 4, 24, 128), F32), V((3, 4, 24, 128), F32), V((2, 3, 192, 256), BF16),
        V((48, 128), F32), V((4, 48, 128), F32), V((4, 48, 128), F32), V((4, 48, 128), F32), V((96, 128), F32),
        DMA((2,)), DMA((2,)), DMA((8,)), DMA((8,)), DMA((3, 17)), DMA((3, 17)), DMA((11,)), DMA((11,)),
    ]
    block, gin, gwi, gwoT, gk = pl.pallas_call(
        kernel,
        out_shape=(
            jax.ShapeDtypeStruct((1, 1, 8, 192, 256), BF16), jax.ShapeDtypeStruct((1, 1, 8, 192, 256), BF16),
            jax.ShapeDtypeStruct((192, 768), F32), jax.ShapeDtypeStruct((192, 768), F32), jax.ShapeDtypeStruct((7, 7, 192), F32),
        ),
        in_specs=[any_, any_] + [vmem] * 9,
        out_specs=(any_, any_, vmem, vmem, vmem),
        scratch_shapes=scratch,
        compiler_params=pltpu.CompilerParams(collective_id=0, has_side_effects=True, vmem_limit_bytes=60 << 20),
    )(
        turn(features), turn(cotangent), dw_kernel, row(dw_bias), row(ln_gain), row(ln_bias), w_in, b_in, w_out.T, row(b_out),
        row(layer_scale),
    )
    block, gin, gwi, gwoT, gk = hand_over(block, gin, gwi, gwoT, gk)
    return turn(block), turn(gin), gwi, gwoT.T, gk


def solution(mesh):
    split, whole = P("slide", "space", None, None, None), P()
    return jax.shard_map(
        on_device,
        mesh=mesh,
        in_specs=(split,) + (whole,) * 9 + (split,),
        out_specs=(split, split, whole, whole, whole),
        check_vma=False,
    )
```

```python
import jax
import jax.numpy as jnp
from jax import lax
from jax.experimental import pallas as pl
from jax.experimental.pallas import tpu as pltpu
from jax.sharding import PartitionSpec as P

EPSILON = 1e-06
F32 = jnp.float32
BF16 = jnp.bfloat16
MESH = pl.DeviceIdType.MESH
PIXEL_SCALE = float(262144) ** (-0.5)
NT = (((1,), (1,)), ((), ()))


def remote(src, dst, send, recv, slide, space):
    return pltpu.make_async_remote_copy(
        src_ref=src, dst_ref=dst, send_sem=send, recv_sem=recv,
        device_id={"slide": slide, "space": space}, device_id_type=MESH,
    )


def gelu_parts(h):
    r = h * 0.7071067811865476
    cdf = 0.5 + 0.5 * lax.erf(r)
    density = jnp.exp2(r * r * -1.4426950408889634)
    return h * cdf, cdf + (h * 0.3989422804014327) * density


def spread(value, slot, group, dst):
    lane = lax.broadcasted_iota(jnp.int32, (16, 128), 1)
    left, right = value[:, 0:128], value[:, 128:256]
    none = jnp.zeros_like(left)
    for b in range(7):
        d = b - 3
        first, second = left, right
        if d:
            first, second = pltpu.roll(left, -d % 128, 1), pltpu.roll(right, -d % 128, 1)
            if d > 0:
                first, second = jnp.where(lane < 128 - d, first, second), jnp.where(lane < 128 - d, second, none)
            else:
                first, second = jnp.where(lane < -d, none, first), jnp.where(lane < -d, first, second)
        at = b * 128 + slot * 16
        dst[group, at : at + 16, 0:128] = first
        dst[group, at : at + 16, 128:256] = second


def valid(i, lane):
    slot = lane // 16
    own = (slot >= i - 3) & (slot <= i + 3)
    halo = jnp.zeros_like(own)
    if i < 3:
        halo = slot >= i + 5
    if i >= 5:
        halo = slot <= i - 5
    return own, halo


def build_taps(dwk, flat, own, halo, flip):
    lane8 = lax.broadcasted_iota(jnp.int32, (8, 128), 1)
    for a in range(7):
        flat[a, 0:7, 0:192] = jnp.concatenate(
            [dwk[6 - a if flip else a, (6 - b if flip else b) : (6 - b if flip else b) + 1, :] for b in range(7)], axis=0
        )
    for g in range(12):
        base = jnp.zeros((8, 128), F32)
        tile, at = g // 8 * 128, g % 8 * 16
        for a in range(7):
            v = flat[a, :, tile : tile + 128]
            v = pltpu.roll(v, (a * 16 - at) % 128, 1)
            base = jnp.where((lane8 >= a * 16) & (lane8 < a * 16 + 16), v, base)
        flat[7 + g, :, 0:128] = base
    lane = lax.broadcasted_iota(jnp.int32, (16, 128), 1)
    same = lane % 16 == lax.broadcasted_iota(jnp.int32, (16, 128), 0)

    def group(g, _):
        base = flat[7 + g, :, 0:128]
        for i in range(8):
            moved = pltpu.roll(base, (i - 3) * 16 % 128, 1)
            for keep, dst in zip(valid(i, lane8), (own, halo)):
                if dst is halo and 3 <= i < 5:
                    dst[g, i * 16 : i * 16 + 16, :] = jnp.zeros((16, 896), BF16)
                    continue
                v = jnp.where(keep, moved, 0.0)
                for b in range(7):
                    row = jnp.broadcast_to(v[b : b + 1, :], (16, 128))
                    dst[g, i * 16 : i * 16 + 16, b * 128 : b * 128 + 128] = jnp.where(same, row, 0.0).astype(BF16)
        return 0

    lax.fori_loop(0, 12, group, 0)


def both(v):
    return jnp.concatenate([v, v], axis=1)


def rows16(g):
    return pl.ds(pl.multiple_of(g * 16, 16), 16)


HALO_SLOTS = ((0, 5), (1, 6), (2, 7), (11, 0), (12, 1), (13, 2))


def kernel(
    feat, cot, dwk, dwb, gain, lbias, w_in, b_in, woutT, b_out, lscale,
    out_block, out_gin, out_full, out_gk,
    fx, ct, xs, xh, gs, gh_, taps, taps_h, back, back_h, flat, zf, par, bias, winT, wout, gout,
    nb, rinv, osum, nsum, outs, gzs, gw, gkr, halo,
    pay, r0, s1f, s1b, r1, s2, r2, rz, fa, full, k0, kx, ky, kz, kfull,
    in_sem, out_sem, halo_send, halo_recv, ar_send, ar_recv, k_send, k_recv,
):
    s, t = lax.axis_index("slide"), lax.axis_index("space")
    z_hi, core = s // 2, s % 2
    z_lo, x, y = t % 2, (t // 2) % 4, t // 8
    z = z_hi * 2 + z_lo
    partner = z_hi * 2 + (1 - core)
    x_peers = [(s, (y * 4 + (x + d) % 4) * 2 + z_lo) for d in (1, 2, 3)]
    y_peers = [(s, (((y + d) % 4) * 4 + x) * 2 + z_lo) for d in (1, 2, 3)]
    z_peers = [(((z + d) % 4) // 2 * 2 + core, (y * 4 + x) * 2 + ((z + d) % 4) % 2) for d in (1, 2, 3)]
    has_up, has_down = t > 0, t < 31
    up, down = jnp.maximum(t - 1, 0), jnp.minimum(t + 1, 31)

    own_in = pltpu.make_async_copy(feat.at[0, 0], fx.at[pl.ds(3, 8)], in_sem.at[0])
    own_in.start()
    cot_in = pltpu.make_async_copy(cot.at[0, 0], ct, in_sem.at[1])
    cot_in.start()

    barrier = pltpu.get_barrier_semaphore()
    for ps, pt in [(partner, t)] + x_peers + y_peers + z_peers:
        pl.semaphore_signal(barrier, inc=1, device_id={"slide": ps, "space": pt}, device_id_type=MESH)

    @pl.when(has_up)
    def _():
        pl.semaphore_signal(barrier, inc=1, device_id={"slide": s, "space": up}, device_id_type=MESH)

    @pl.when(has_down)
    def _():
        pl.semaphore_signal(barrier, inc=1, device_id={"slide": s, "space": down}, device_id_type=MESH)

    pl.semaphore_wait(barrier, 10 + jnp.minimum(t, 1) + jnp.minimum(31 - t, 1))

    to_up = remote(feat.at[0, 0, pl.ds(0, 3)], fx.at[pl.ds(11, 3)], halo_send.at[0], halo_recv.at[0], s, up)
    to_down = remote(feat.at[0, 0, pl.ds(5, 3)], fx.at[pl.ds(0, 3)], halo_send.at[1], halo_recv.at[1], s, down)

    @pl.when(has_up)
    def _():
        to_up.start()

    @pl.when(has_down)
    def _():
        to_down.start()

    for n, ref in enumerate((dwb, gain, lbias, b_out, lscale)):
        par[n, 0:128, :] = jnp.broadcast_to(ref[:, 0:128], (128, 128)).T
        par[n, 128:256, :] = jnp.broadcast_to(both(ref[:, 128:192]), (128, 128)).T
    for n in range(6):
        bias[n * 128 : n * 128 + 128, :] = jnp.broadcast_to(b_in[n * 128 : n * 128 + 128].reshape(1, 128), (128, 128)).T
    winT[...] = w_in[...].T
    wout[...] = woutT[...].T
    build_taps(dwk, flat, taps, taps_h, False)

    def clear(g, _):
        none = jnp.zeros((32, 256), BF16)
        for b in range(7):
            xh[g, b * 128 + 48 : b * 128 + 80, :] = none
            gh_[g, b * 128 + 48 : b * 128 + 80, :] = none
        return 0

    lax.fori_loop(0, 12, clear, 0)
    own_in.wait()

    def conv_own(g, _):
        for i in range(8):
            spread(fx[i + 3, rows16(g), :], i, g, xs)
        v = jnp.dot(taps[g], xs[g], preferred_element_type=F32)
        for i in range(8):
            zf[i, rows16(g), :] = v[i * 16 : i * 16 + 16, :] + both(par[0, rows16(g), :])
        return 0

    lax.fori_loop(0, 12, conv_own, 0)
    cot_in.wait()

    def scale_row(i, _):
        gout[i] = (both(par[4, 0:192, :]) * ct[i].astype(F32)).astype(BF16)
        return 0

    lax.fori_loop(0, 8, scale_row, 0)

    def norm(n, _):
        i = n // 2
        ln = pl.ds(pl.multiple_of(n % 2 * 128, 128), 128)
        v = zf[i, :, ln]
        v = v - jnp.sum(v, axis=0, keepdims=True) * (1.0 / 192)
        var = jnp.sum(v * v, axis=0, keepdims=True) * (1.0 / 192)
        r = lax.rsqrt(var + EPSILON)
        v = v * r
        zf[i, :, ln] = v
        rinv[i, :, ln] = jnp.broadcast_to(r, (8, 128))
        nb[i, :, ln] = (v * par[1, 0:192, :] + par[2, 0:192, :]).astype(BF16)
        return 0

    lax.fori_loop(6, 10, norm, 0)

    gw[...] = jnp.zeros_like(gw)
    osum[...] = jnp.zeros_like(osum)
    nsum[...] = jnp.zeros_like(nsum)

    def mlp_pair(f, p):
        units = pl.ds(pl.multiple_of(f * 256, 256), 256)
        q = 7 - p
        normed = jnp.concatenate([nb[p], nb[q]], axis=1)
        upper = jnp.concatenate([gout[p], gout[q]], axis=1)
        hidden = jnp.dot(winT[units, :], normed, preferred_element_type=F32) + both(both(bias[units, :]))
        value, slope = gelu_parts(hidden)
        act = value.astype(BF16)
        gh = (jnp.dot(wout[units, :], upper, preferred_element_type=F32) * slope).astype(BF16)
        out = jnp.dot(woutT[:, units], act, preferred_element_type=F32)
        osum[p] += out[:, 0:256]
        osum[q] += out[:, 256:512]
        out = jnp.dot(w_in[:, units], gh, preferred_element_type=F32)
        nsum[p] += out[:, 0:256]
        nsum[q] += out[:, 256:512]
        gw[0, f] += lax.dot_general(normed, gh, NT, preferred_element_type=F32)
        gw[1, f] += lax.dot_general(upper, act, NT, preferred_element_type=F32)

    def mlp_inner(k, _):
        mlp_pair(k, 3)
        return 0

    lax.fori_loop(0, 3, mlp_inner, 0)

    @pl.when(has_up)
    def _():
        to_down.wait_recv()

    @pl.when(t == 0)
    def _():
        fx[0:3] = jnp.zeros((3, 192, 256), BF16)

    @pl.when(has_down)
    def _():
        to_up.wait_recv()

    @pl.when(t == 31)
    def _():
        fx[11:14] = jnp.zeros((3, 192, 256), BF16)

    def conv_halo(g, _):
        for r, slot in HALO_SLOTS:
            spread(fx[r, rows16(g), :], slot, g, xh)
        v = jnp.dot(taps_h[g], xh[g], preferred_element_type=F32)
        for i in (0, 1, 2, 5, 6, 7):
            zf[i, rows16(g), :] += v[i * 16 : i * 16 + 16, :]
        return 0

    lax.fori_loop(0, 12, conv_halo, 0)

    lax.fori_loop(0, 6, norm, 0)
    lax.fori_loop(10, 16, norm, 0)

    def stage0(f):
        pay[f] = gw[1 - core, f].astype(BF16)
        core_copy(f).start()

    def core_copy(f):
        return remote(pay.at[f], r0.at[f], ar_send.at[f, 0], ar_recv.at[f, 0], partner, t)

    def y_copies(f):
        return [
            remote(s1b.at[f, pl.ds(((y + d + 1) % 4) * 48, 48)], r1.at[f, d], ar_send.at[f, 1 + d], ar_recv.at[f, 1 + d], *y_peers[d])
            for d in range(3)
        ]

    def x_copies(f):
        return [
            remote(s2.at[f, (x + d + 1) % 4], r2.at[f, d], ar_send.at[f, 4 + d], ar_recv.at[f, 4 + d], *x_peers[d]) for d in range(3)
        ]

    def z_copies(f):
        return [remote(rz.at[f, z], rz.at[f, z], ar_send.at[f, 7 + d], ar_recv.at[f, 7 + d], *z_peers[d]) for d in range(3)]

    def x_back(f):
        return [remote(fa.at[f, x], fa.at[f, x], ar_send.at[f, 10 + d], ar_recv.at[f, 10 + d], *x_peers[d]) for d in range(3)]

    def y_back(f):
        mine = full.at[f, core, pl.ds(y * 48, 48)]
        return [remote(mine, mine, ar_send.at[f, 13 + d], ar_recv.at[f, 13 + d], *y_peers[d]) for d in range(3)]

    def core_back(f):
        return remote(full.at[f, core], full.at[f, core], ar_send.at[f, 16], ar_recv.at[f, 16], partner, t)

    def stage1(f):
        core_copy(f).wait()
        total = gw[core, f] + r0[f].astype(F32)
        s1f[f] = total
        s1b[f] = total.astype(BF16)
        for c in y_copies(f):
            c.start()

    def stage2(f):
        for c in y_copies(f):
            c.wait()
        total = s1f[f, pl.ds(y * 48, 48), :]
        for d in range(3):
            total = total + r1[f, d].astype(F32)
        for part in range(4):
            at, ln = part % 2 * 24, part // 2 * 128
            s2[f, part] = total[at : at + 24, ln : ln + 128]
        for c in x_copies(f):
            c.start()

    def stage3(f):
        for c in x_copies(f):
            c.wait()
        rz[f, z] = (s2[f, x] + r2[f, 0]) + (r2[f, 1] + r2[f, 2])
        for c in z_copies(f):
            c.start()

    def stage4(f):
        for c in z_copies(f):
            c.wait()
        fa[f, x] = (rz[f, 0] + rz[f, 1]) + (rz[f, 2] + rz[f, 3])
        for c in x_back(f):
            c.start()

    def stage5(f):
        for c in x_back(f):
            c.wait()
        rows = [jnp.concatenate([fa[f, part], fa[f, part + 2]], axis=1) for part in range(2)]
        full[f, core, pl.ds(pl.multiple_of(y * 48, 16), 48), :] = jnp.concatenate(rows, axis=0).astype(BF16)
        for c in y_back(f):
            c.start()

    def stage6(f):
        for c in y_back(f):
            c.wait()
        core_back(f).start()

    def stage7(f):
        core_back(f).wait()
        full_out(f).start()

    def full_out(f):
        return pltpu.make_async_copy(full.at[f], out_full.at[f], out_sem.at[2 + f])

    after = {
        2: [(stage0, 0)], 4: [(stage1, 0)], 5: [(stage0, 1)], 7: [(stage2, 0), (stage1, 1)], 8: [(stage0, 2)],
    }

    def mlp(k, _):
        mlp_pair(k // 3, k % 3)
        for at, steps in after.items():

            @pl.when(k == at)
            def _():
                for step, chunk in steps:
                    step(chunk)

        return 0

    lax.fori_loop(0, 9, mlp, 0)

    def finish(n, _):
        i = n // 2
        ln = pl.ds(pl.multiple_of(n % 2 * 128, 128), 128)
        gn = nsum[i, :, ln] * par[1, 0:192, :]
        u = zf[i, :, ln]
        m1 = jnp.sum(gn, axis=0, keepdims=True) * (1.0 / 192)
        m2 = jnp.sum(gn * u, axis=0, keepdims=True) * (1.0 / 192)
        gzs[i, :, ln] = (rinv[i, 0:1, ln] * (gn - m1 - u * m2)).astype(BF16)
        return 0

    def finish_out(n, _):
        i = n // 2
        ln = pl.ds(pl.multiple_of(n % 2 * 128, 128), 128)
        branch = osum[i, :, ln] + par[3, 0:192, :]
        outs[i, :, ln] = (fx[i + 3, :, ln].astype(F32) + par[4, 0:192, :] * branch).astype(BF16)
        return 0

    lax.fori_loop(0, 16, finish, 0)

    gz_up = [remote(gzs.at[n], halo.at[1, n], halo_send.at[2 + n], halo_recv.at[2 + n], s, up) for n in range(3)]
    gz_down = [remote(gzs.at[7 - n], halo.at[0, 2 - n], halo_send.at[5 + n], halo_recv.at[5 + n], s, down) for n in range(3)]

    def send_row(n):
        @pl.when(has_up)
        def _():
            gz_up[n].start()

        @pl.when(has_down)
        def _():
            gz_down[n].start()

    stage1(2)
    send_row(0)
    stage2(1)
    stage3(0)

    lane = lax.broadcasted_iota(jnp.int32, (8, 128), 1)
    sub = lax.broadcasted_iota(jnp.int32, (8, 128), 0)

    def taps_grad(g, _):
        mine = jnp.concatenate([gzs[i, rows16(g), :] for i in range(8)], axis=0)
        for b in range(7):
            rows = pl.ds(b * 128, 128)
            pairs = lax.dot_general(mine, jnp.concatenate([xs[g, rows, :], xh[g, rows, :]], axis=0), NT, preferred_element_type=F32)
            at_own, at_halo = pairs[:, 0:128], pairs[:, 128:256]
            total = jnp.zeros((8, 128), F32)
            for i in range(8):
                use_own, use_halo = valid(i, lane)
                v = jnp.zeros((8, 128), F32)
                for h in range(2):
                    at = i * 16 + h * 8
                    same = lane % 16 == sub + h * 8
                    v = jnp.where(same & use_own, at_own[at : at + 8], v)
                    if not 3 <= i < 5:
                        v = jnp.where(same & use_halo, at_halo[at : at + 8], v)
                total = total + (pltpu.roll(v, (3 - i) * 16 % 128, 1) if i != 3 else v)
            gkr[pl.ds(g * 8 + b, 1), :] = jnp.sum(total, axis=0, keepdims=True)
        return 0

    gkr[...] = jnp.zeros_like(gkr)
    def taps_step(g, _):
        taps_grad(g, 0)

        @pl.when(g == 5)
        def _():
            stage2(2)
            send_row(1)
            stage3(1)
            stage4(0)

        return 0

    lax.fori_loop(0, 12, taps_step, 0)

    other = pl.ds((1 - core) * 48, 48)
    own_half = pl.ds(core * 48, 48)
    k_core = remote(gkr.at[other], k0, k_send.at[0], k_recv.at[0], partner, t)
    k_core.start()
    stage3(2)
    send_row(2)
    stage4(1)
    stage5(0)
    lax.fori_loop(0, 16, finish_out, 0)
    block_out = pltpu.make_async_copy(outs, out_block.at[0, 0], out_sem.at[0])
    block_out.start()

    def back_own(g, _):
        for i in range(8):
            spread(gzs[i, rows16(g), :], i, g, gs)
        v = jnp.dot(back[g], gs[g], preferred_element_type=F32)
        for i in range(8):
            zf[i, rows16(g), :] = ct[i, rows16(g), :].astype(F32) + v[i * 16 : i * 16 + 16, :]
        return 0

    k_core.wait()
    ky[y] = gkr[own_half, :] + k0[...]
    ky_copies = [remote(ky.at[y], ky.at[y], k_send.at[1 + d], k_recv.at[1 + d], *y_peers[d]) for d in range(3)]
    for c in ky_copies:
        c.start()
    build_taps(dwk, flat, back, back_h, True)
    stage4(2)
    stage5(1)
    stage6(0)
    lax.fori_loop(0, 4, back_own, 0)
    for c in ky_copies:
        c.wait()
    kx[x] = (ky[0] + ky[1]) + (ky[2] + ky[3])
    kx_copies = [remote(kx.at[x], kx.at[x], k_send.at[4 + d], k_recv.at[4 + d], *x_peers[d]) for d in range(3)]
    for c in kx_copies:
        c.start()
    stage5(2)
    stage6(1)
    lax.fori_loop(4, 12, back_own, 0)
    for c in kx_copies:
        c.wait()
    kz[z] = (kx[0] + kx[1]) + (kx[2] + kx[3])
    kz_copies = [remote(kz.at[z], kz.at[z], k_send.at[7 + d], k_recv.at[7 + d], *z_peers[d]) for d in range(3)]
    for c in kz_copies:
        c.start()
    stage6(2)
    stage7(0)
    stage7(1)

    @pl.when(has_up)
    def _():
        for c in gz_down:
            c.wait_recv()

    @pl.when(t == 0)
    def _():
        halo[0] = jnp.zeros((3, 192, 256), BF16)

    @pl.when(has_down)
    def _():
        for c in gz_up:
            c.wait_recv()

    @pl.when(t == 31)
    def _():
        halo[1] = jnp.zeros((3, 192, 256), BF16)

    def back_halo(g, _):
        for r, slot in HALO_SLOTS:
            spread(halo[r // 8, r % 11, rows16(g), :], slot, g, gh_)
        v = jnp.dot(back_h[g], gh_[g], preferred_element_type=F32)
        for i in range(8):
            fx[i, rows16(g), :] = (zf[i, rows16(g), :] + v[i * 16 : i * 16 + 16, :]).astype(BF16)
        return 0

    def back_step(g, _):
        back_halo(g, 0)

        @pl.when(g == 5)
        def _():
            for c in kz_copies:
                c.wait()
            kfull[own_half, :] = (kz[0] + kz[1]) + (kz[2] + kz[3])
            k_back.start()

        return 0

    k_back = remote(kfull.at[own_half], kfull.at[own_half], k_send.at[10], k_recv.at[10], partner, t)
    lax.fori_loop(0, 12, back_step, 0)
    gin_out = pltpu.make_async_copy(fx.at[pl.ds(0, 8)], out_gin.at[0, 0], out_sem.at[1])
    gin_out.start()
    stage7(2)
    k_back.wait()
    for a in range(7):
        for tile, width in ((0, 128), (128, 64)):
            base = jnp.zeros((8, 128), F32)
            for g in range(tile // 16, (tile + width) // 16):
                at = g % 8 * 16
                v = pltpu.roll(kfull[g * 8 : g * 8 + 8, :], (at - a * 16) % 128, 1)
                base = jnp.where((lane >= at) & (lane < at + 16), v, base)
            out_gk[a, :, tile : tile + width] = base[0:7, 0:width] * PIXEL_SCALE

    @pl.when(has_up)
    def _():
        to_up.wait_send()
        for c in gz_up:
            c.wait_send()

    @pl.when(has_down)
    def _():
        to_down.wait_send()
        for c in gz_down:
            c.wait_send()

    block_out.wait()
    gin_out.wait()
    for f in range(3):
        full_out(f).wait()


def hand_over_kernel(
    block, gin, full, gk, out_block, out_gin, out_gk, out_gwi, out_gwoT, h_block, h_gin, h_gk, h_full, h_gwi, h_gwoT, sems
):
    plain = ((block, h_block, out_block), (gin, h_gin, out_gin), (gk, h_gk, out_gk))
    load = pltpu.make_async_copy(full, h_full, sems.at[0, 3])
    load.start()
    loads = [pltpu.make_async_copy(i, h, sems.at[0, n]) for n, (i, h, o) in enumerate(plain)]
    stores = [pltpu.make_async_copy(h, o, sems.at[1, n]) for n, (i, h, o) in enumerate(plain)]
    for c in loads:
        c.start()
    load.wait()
    for m, (held, out) in enumerate(((h_gwi, out_gwi), (h_gwoT, out_gwoT))):
        for f in range(3):
            held[:, f * 256 : f * 256 + 256] = h_full[f, m].astype(F32) * PIXEL_SCALE
        stores.append(pltpu.make_async_copy(held, out, sems.at[1, 3 + m]))
        stores[-1].start()
    for c, store in zip(loads, stores):
        c.wait()
        store.start()
    for c in stores:
        c.wait()


def hand_over(block, gin, full, gk):
    like = lambda v: jax.ShapeDtypeStruct(v.shape, v.dtype)
    weights = jax.ShapeDtypeStruct((192, 768), F32)
    shapes = (like(block), like(gin), like(gk), weights, weights)
    return pl.pallas_call(
        hand_over_kernel,
        out_shape=shapes,
        in_specs=[pl.BlockSpec(memory_space=pl.ANY)] * 4,
        out_specs=(pl.BlockSpec(memory_space=pl.ANY),) * 5,
        scratch_shapes=[pltpu.VMEM(v.shape, v.dtype) for v in (block, gin, gk, full, weights, weights)]
        + [pltpu.SemaphoreType.DMA((2, 5))],
    )(block, gin, full, gk)


def on_device(features, dw_kernel, dw_bias, ln_gain, ln_bias, w_in, b_in, w_out, b_out, layer_scale, cotangent):
    row = lambda v: v.reshape(1, -1)
    turn = lambda v: jnp.swapaxes(v, 3, 4)
    any_, vmem = pl.BlockSpec(memory_space=pl.ANY), pl.BlockSpec(memory_space=pltpu.VMEM)
    V, DMA = pltpu.VMEM, pltpu.SemaphoreType.DMA
    groups = V((12, 896, 256), BF16)
    tables = V((12, 128, 896), BF16)
    scratch = [
        V((14, 192, 256), BF16), V((8, 192, 256), BF16), groups, groups, groups, groups, tables, tables, tables, tables,
        V((19, 8, 256), F32), V((8, 192, 256), F32), V((5, 256, 128), F32), V((768, 128), F32), V((768, 192), BF16),
        V((768, 192), BF16), V((8, 192, 256), BF16),
        V((8, 192, 256), BF16), V((8, 8, 256), F32), V((8, 192, 256), F32), V((8, 192, 256), F32), V((8, 192, 256), BF16),
        V((8, 192, 256), BF16), V((2, 3, 192, 256), F32), V((96, 128), F32), V((2, 3, 192, 256), BF16),
        V((3, 192, 256), BF16), V((3, 192, 256), BF16), V((3, 192, 256), F32), V((3, 192, 256), BF16), V((3, 3, 48, 256), BF16),
        V((3, 4, 24, 128), F32), V((3, 3, 24, 128), F32), V((3, 4, 24, 128), F32), V((3, 4, 24, 128), F32), V((3, 2, 192, 256), BF16),
        V((48, 128), F32), V((4, 48, 128), F32), V((4, 48, 128), F32), V((4, 48, 128), F32), V((96, 128), F32),
        DMA((2,)), DMA((5,)), DMA((8,)), DMA((8,)), DMA((3, 17)), DMA((3, 17)), DMA((11,)), DMA((11,)),
    ]
    values = pl.pallas_call(
        kernel,
        out_shape=(
            jax.ShapeDtypeStruct((1, 1, 8, 192, 256), BF16), jax.ShapeDtypeStruct((1, 1, 8, 192, 256), BF16),
            jax.ShapeDtypeStruct((3, 2, 192, 256), BF16), jax.ShapeDtypeStruct((7, 7, 192), F32),
        ),
        in_specs=[any_, any_] + [vmem] * 9,
        out_specs=(any_, any_, any_, vmem),
        scratch_shapes=scratch,
        compiler_params=pltpu.CompilerParams(collective_id=0, has_side_effects=True, vmem_limit_bytes=60 << 20),
    )(
        turn(features), turn(cotangent), dw_kernel, row(dw_bias), row(ln_gain), row(ln_bias), w_in, b_in, w_out.T, row(b_out),
        row(layer_scale),
    )
    block, gin, gk, gwi, gwoT = hand_over(*values)
    return turn(block), turn(gin), gwi, gwoT.T, gk


def solution(mesh):
    split, whole = P("slide", "space", None, None, None), P()
    return jax.shard_map(
        on_device,
        mesh=mesh,
        in_specs=(split,) + (whole,) * 9 + (split,),
        out_specs=(split, split, whole, whole, whole),
        check_vma=False,
    )
```

```python
import jax
import jax.numpy as jnp
from jax import lax
from jax.experimental import pallas as pl
from jax.experimental.pallas import tpu as pltpu
from jax.sharding import PartitionSpec as P

EPSILON = 1e-06
F32 = jnp.float32
BF16 = jnp.bfloat16
MESH = pl.DeviceIdType.MESH
PIXEL_SCALE = float(262144) ** (-0.5)
NT = (((1,), (1,)), ((), ()))


def remote(src, dst, send, recv, slide, space):
    return pltpu.make_async_remote_copy(
        src_ref=src, dst_ref=dst, send_sem=send, recv_sem=recv,
        device_id={"slide": slide, "space": space}, device_id_type=MESH,
    )


def gelu_parts(h):
    r = h * 0.7071067811865476
    cdf = 0.5 + 0.5 * lax.erf(r)
    density = jnp.exp2(r * r * -1.4426950408889634)
    return h * cdf, cdf + (h * 0.3989422804014327) * density


def spread(value, slot, group, dst):
    lane = lax.broadcasted_iota(jnp.int32, (16, 128), 1)
    left, right = value[:, 0:128], value[:, 128:256]
    none = jnp.zeros_like(left)
    for b in range(7):
        d = b - 3
        first, second = left, right
        if d:
            first, second = pltpu.roll(left, -d % 128, 1), pltpu.roll(right, -d % 128, 1)
            if d > 0:
                first, second = jnp.where(lane < 128 - d, first, second), jnp.where(lane < 128 - d, second, none)
            else:
                first, second = jnp.where(lane < -d, none, first), jnp.where(lane < -d, first, second)
        at = b * 128 + slot * 16
        dst[group, at : at + 16, 0:128] = first
        dst[group, at : at + 16, 128:256] = second


def valid(i, lane):
    slot = lane // 16
    own = (slot >= i - 3) & (slot <= i + 3)
    halo = jnp.zeros_like(own)
    if i < 3:
        halo = slot >= i + 5
    if i >= 5:
        halo = slot <= i - 5
    return own, halo


def build_taps(dwk, flat, own, halo, flip):
    lane8 = lax.broadcasted_iota(jnp.int32, (8, 128), 1)
    for a in range(7):
        flat[a, 0:7, 0:192] = jnp.concatenate(
            [dwk[6 - a if flip else a, (6 - b if flip else b) : (6 - b if flip else b) + 1, :] for b in range(7)], axis=0
        )
    for g in range(12):
        base = jnp.zeros((8, 128), F32)
        tile, at = g // 8 * 128, g % 8 * 16
        for a in range(7):
            v = flat[a, :, tile : tile + 128]
            v = pltpu.roll(v, (a * 16 - at) % 128, 1)
            base = jnp.where((lane8 >= a * 16) & (lane8 < a * 16 + 16), v, base)
        flat[7 + g, :, 0:128] = base
    lane = lax.broadcasted_iota(jnp.int32, (16, 128), 1)
    same = lane % 16 == lax.broadcasted_iota(jnp.int32, (16, 128), 0)

    def group(g, _):
        base = flat[7 + g, :, 0:128]
        for i in range(8):
            moved = pltpu.roll(base, (i - 3) * 16 % 128, 1)
            for keep, dst in zip(valid(i, lane8), (own, halo)):
                if dst is halo and 3 <= i < 5:
                    dst[g, i * 16 : i * 16 + 16, :] = jnp.zeros((16, 896), BF16)
                    continue
                v = jnp.where(keep, moved, 0.0)
                for b in range(7):
                    row = jnp.broadcast_to(v[b : b + 1, :], (16, 128))
                    dst[g, i * 16 : i * 16 + 16, b * 128 : b * 128 + 128] = jnp.where(same, row, 0.0).astype(BF16)
        return 0

    lax.fori_loop(0, 12, group, 0)


def both(v):
    return jnp.concatenate([v, v], axis=1)


def rows16(g):
    return pl.ds(pl.multiple_of(g * 16, 16), 16)


HALO_SLOTS = ((0, 5), (1, 6), (2, 7), (11, 0), (12, 1), (13, 2))


def kernel(
    feat, cot, dwk, dwb, gain, lbias, w_in, b_in, woutT, b_out, lscale,
    out_block, out_gin, out_full, out_gk,
    fx, ct, xs, xh, gs, gh_, taps, taps_h, back, back_h, flat, zf, par, bias, winT, wout, gout,
    nb, rinv, osum, nsum, outs, gzs, gw, gkr, halo,
    pa, ra, rb, fc, rk, rk2, fk,
    in_sem, out_sem, halo_send, halo_recv, ar_send, ar_recv,
):
    s, t = lax.axis_index("slide"), lax.axis_index("space")
    z_hi, core = s // 2, s % 2
    z_lo = t % 2
    z = z_hi * 2 + z_lo
    plane, pillar = t // 2, z * 2 + core
    plane_peers = [((plane + e) % 16) for e in range(1, 16)]
    pillar_peers = [((pillar + e) % 8) for e in range(1, 8)]

    def in_plane(p):
        return s, p * 2 + z_lo

    def in_pillar(q):
        return q // 4 * 2 + q % 2, plane * 2 + q // 2 % 2

    has_up, has_down = t > 0, t < 31
    up, down = jnp.maximum(t - 1, 0), jnp.minimum(t + 1, 31)

    own_in = pltpu.make_async_copy(feat.at[0, 0], fx.at[pl.ds(3, 8)], in_sem.at[0])
    own_in.start()
    cot_in = pltpu.make_async_copy(cot.at[0, 0], ct, in_sem.at[1])
    cot_in.start()

    barrier = pltpu.get_barrier_semaphore()
    for ps, pt in [in_plane(p) for p in plane_peers] + [in_pillar(q) for q in pillar_peers]:
        pl.semaphore_signal(barrier, inc=1, device_id={"slide": ps, "space": pt}, device_id_type=MESH)

    @pl.when(has_up)
    def _():
        pl.semaphore_signal(barrier, inc=1, device_id={"slide": s, "space": up}, device_id_type=MESH)

    @pl.when(has_down)
    def _():
        pl.semaphore_signal(barrier, inc=1, device_id={"slide": s, "space": down}, device_id_type=MESH)

    pl.semaphore_wait(barrier, 22 + jnp.minimum(t, 1) + jnp.minimum(31 - t, 1))

    to_up = remote(feat.at[0, 0, pl.ds(0, 3)], fx.at[pl.ds(11, 3)], halo_send.at[0], halo_recv.at[0], s, up)
    to_down = remote(feat.at[0, 0, pl.ds(5, 3)], fx.at[pl.ds(0, 3)], halo_send.at[1], halo_recv.at[1], s, down)

    @pl.when(has_up)
    def _():
        to_up.start()

    @pl.when(has_down)
    def _():
        to_down.start()

    for n, ref in enumerate((dwb, gain, lbias, b_out, lscale)):
        par[n, 0:128, :] = jnp.broadcast_to(ref[:, 0:128], (128, 128)).T
        par[n, 128:256, :] = jnp.broadcast_to(both(ref[:, 128:192]), (128, 128)).T
    for n in range(6):
        bias[n * 128 : n * 128 + 128, :] = jnp.broadcast_to(b_in[n * 128 : n * 128 + 128].reshape(1, 128), (128, 128)).T
    winT[...] = w_in[...].T
    wout[...] = woutT[...].T
    build_taps(dwk, flat, taps, taps_h, False)

    def clear(g, _):
        none = jnp.zeros((32, 256), BF16)
        for b in range(7):
            xh[g, b * 128 + 48 : b * 128 + 80, :] = none
            gh_[g, b * 128 + 48 : b * 128 + 80, :] = none
        return 0

    lax.fori_loop(0, 12, clear, 0)
    own_in.wait()

    def conv_own(g, _):
        for i in range(8):
            spread(fx[i + 3, rows16(g), :], i, g, xs)
        v = jnp.dot(taps[g], xs[g], preferred_element_type=F32)
        for i in range(8):
            zf[i, rows16(g), :] = v[i * 16 : i * 16 + 16, :] + both(par[0, rows16(g), :])
        return 0

    lax.fori_loop(0, 12, conv_own, 0)
    cot_in.wait()

    def scale_row(i, _):
        gout[i] = (both(par[4, 0:192, :]) * ct[i].astype(F32)).astype(BF16)
        return 0

    lax.fori_loop(0, 8, scale_row, 0)

    def norm(n, _):
        i = n // 2
        ln = pl.ds(pl.multiple_of(n % 2 * 128, 128), 128)
        v = zf[i, :, ln]
        v = v - jnp.sum(v, axis=0, keepdims=True) * (1.0 / 192)
        var = jnp.sum(v * v, axis=0, keepdims=True) * (1.0 / 192)
        r = lax.rsqrt(var + EPSILON)
        v = v * r
        zf[i, :, ln] = v
        rinv[i, :, ln] = jnp.broadcast_to(r, (8, 128))
        nb[i, :, ln] = (v * par[1, 0:192, :] + par[2, 0:192, :]).astype(BF16)
        return 0

    lax.fori_loop(6, 10, norm, 0)

    gw[...] = jnp.zeros_like(gw)
    osum[...] = jnp.zeros_like(osum)
    nsum[...] = jnp.zeros_like(nsum)

    def mlp_pair(f, p):
        units = pl.ds(pl.multiple_of(f * 256, 256), 256)
        q = 7 - p
        normed = jnp.concatenate([nb[p], nb[q]], axis=1)
        upper = jnp.concatenate([gout[p], gout[q]], axis=1)
        hidden = jnp.dot(winT[units, :], normed, preferred_element_type=F32) + both(both(bias[units, :]))
        value, slope = gelu_parts(hidden)
        act = value.astype(BF16)
        gh = (jnp.dot(wout[units, :], upper, preferred_element_type=F32) * slope).astype(BF16)
        out = jnp.dot(woutT[:, units], act, preferred_element_type=F32)
        osum[p] += out[:, 0:256]
        osum[q] += out[:, 256:512]
        out = jnp.dot(w_in[:, units], gh, preferred_element_type=F32)
        nsum[p] += out[:, 0:256]
        nsum[q] += out[:, 256:512]
        gw[0, f] += lax.dot_general(normed, gh, NT, preferred_element_type=F32)
        gw[1, f] += lax.dot_general(upper, act, NT, preferred_element_type=F32)

    def mlp_inner(k, _):
        mlp_pair(k, 3)
        return 0

    lax.fori_loop(0, 3, mlp_inner, 0)

    @pl.when(has_up)
    def _():
        to_down.wait_recv()

    @pl.when(t == 0)
    def _():
        fx[0:3] = jnp.zeros((3, 192, 256), BF16)

    @pl.when(has_down)
    def _():
        to_up.wait_recv()

    @pl.when(t == 31)
    def _():
        fx[11:14] = jnp.zeros((3, 192, 256), BF16)

    def conv_halo(g, _):
        for r, slot in HALO_SLOTS:
            spread(fx[r, rows16(g), :], slot, g, xh)
        v = jnp.dot(taps_h[g], xh[g], preferred_element_type=F32)
        for i in (0, 1, 2, 5, 6, 7):
            zf[i, rows16(g), :] += v[i * 16 : i * 16 + 16, :]
        return 0

    lax.fori_loop(0, 12, conv_halo, 0)

    lax.fori_loop(0, 6, norm, 0)
    lax.fori_loop(10, 16, norm, 0)

    def buffers(f):
        return (gkr, rk, rk2, fk) if f == 3 else (pa.at[f], ra.at[f], rb.at[f], fc.at[f])

    def spread_copies(f):
        own, got, _, _ = buffers(f)
        return [
            remote(own.at[p], got.at[e], ar_send.at[f, e], ar_recv.at[f, e], *in_plane(p)) for e, p in enumerate(plane_peers)
        ]

    def pillar_copies(f):
        part = buffers(f)[2].at[pillar]
        return [
            remote(part, part, ar_send.at[f, 15 + e], ar_recv.at[f, 15 + e], *in_pillar(q)) for e, q in enumerate(pillar_peers)
        ]

    def back_copies(f):
        part = buffers(f)[3].at[plane]
        return [
            remote(part, part, ar_send.at[f, 22 + e], ar_recv.at[f, 22 + e], *in_plane(p)) for e, p in enumerate(plane_peers)
        ]

    def full_out(f):
        return pltpu.make_async_copy(fc.at[f], out_full.at[f], out_sem.at[2 + f])

    def stage_a(f):
        if f < 3:
            for j in range(16):
                at, ln = j % 8 * 24, j // 8 * 128
                part = [gw[m, f, at : at + 24, ln : ln + 128] for m in range(2)]
                pa[f, j] = jnp.concatenate(part, axis=0).astype(BF16)
        for c in spread_copies(f):
            c.start()

    def stage_b(f):
        for c in spread_copies(f):
            c.wait()
        own, got, mine, _ = buffers(f)
        total = own[plane].astype(F32)
        for e in range(15):
            total = total + got[e].astype(F32)
        mine[pillar] = total
        for c in pillar_copies(f):
            c.start()

    def stage_c(f):
        for c in pillar_copies(f):
            c.wait()
        _, _, mine, result = buffers(f)
        total = ((mine[0] + mine[1]) + (mine[2] + mine[3])) + ((mine[4] + mine[5]) + (mine[6] + mine[7]))
        result[plane] = total.astype(result.dtype)
        for c in back_copies(f):
            c.start()

    def stage_d(f):
        for c in back_copies(f):
            c.wait()
        if f < 3:
            full_out(f).start()

    after = {2: [(stage_a, 0)], 5: [(stage_a, 1)], 8: [(stage_a, 2), (stage_b, 0)]}

    def mlp(k, _):
        mlp_pair(k // 3, k % 3)
        for at, steps in after.items():

            @pl.when(k == at)
            def _():
                for step, chunk in steps:
                    step(chunk)

        return 0

    lax.fori_loop(0, 9, mlp, 0)

    def finish(n, _):
        i = n // 2
        ln = pl.ds(pl.multiple_of(n % 2 * 128, 128), 128)
        gn = nsum[i, :, ln] * par[1, 0:192, :]
        u = zf[i, :, ln]
        m1 = jnp.sum(gn, axis=0, keepdims=True) * (1.0 / 192)
        m2 = jnp.sum(gn * u, axis=0, keepdims=True) * (1.0 / 192)
        gzs[i, :, ln] = (rinv[i, 0:1, ln] * (gn - m1 - u * m2)).astype(BF16)
        return 0

    def finish_out(n, _):
        i = n // 2
        ln = pl.ds(pl.multiple_of(n % 2 * 128, 128), 128)
        branch = osum[i, :, ln] + par[3, 0:192, :]
        outs[i, :, ln] = (fx[i + 3, :, ln].astype(F32) + par[4, 0:192, :] * branch).astype(BF16)
        return 0

    lax.fori_loop(0, 16, finish, 0)

    gz_up = [remote(gzs.at[n], halo.at[1, n], halo_send.at[2 + n], halo_recv.at[2 + n], s, up) for n in range(3)]
    gz_down = [remote(gzs.at[7 - n], halo.at[0, 2 - n], halo_send.at[5 + n], halo_recv.at[5 + n], s, down) for n in range(3)]

    def send_row(n):
        @pl.when(has_up)
        def _():
            gz_up[n].start()

        @pl.when(has_down)
        def _():
            gz_down[n].start()

    send_row(0)

    lane = lax.broadcasted_iota(jnp.int32, (8, 128), 1)
    sub = lax.broadcasted_iota(jnp.int32, (8, 128), 0)

    def taps_grad(g, _):
        mine = jnp.concatenate([gzs[i, rows16(g), :] for i in range(8)], axis=0)
        for b in range(7):
            rows = pl.ds(b * 128, 128)
            pairs = lax.dot_general(mine, jnp.concatenate([xs[g, rows, :], xh[g, rows, :]], axis=0), NT, preferred_element_type=F32)
            at_own, at_halo = pairs[:, 0:128], pairs[:, 128:256]
            total = jnp.zeros((8, 128), F32)
            for i in range(8):
                use_own, use_halo = valid(i, lane)
                v = jnp.zeros((8, 128), F32)
                for h in range(2):
                    at = i * 16 + h * 8
                    same = lane % 16 == sub + h * 8
                    v = jnp.where(same & use_own, at_own[at : at + 8], v)
                    if not 3 <= i < 5:
                        v = jnp.where(same & use_halo, at_halo[at : at + 8], v)
                total = total + (pltpu.roll(v, (3 - i) * 16 % 128, 1) if i != 3 else v)
            gkr[g, b : b + 1, :] = jnp.sum(total, axis=0, keepdims=True)
        return 0

    gkr[...] = jnp.zeros_like(gkr)
    def taps_step(g, _):
        taps_grad(g, 0)

        @pl.when(g == 5)
        def _():
            send_row(1)
            stage_b(1)
            stage_c(0)

        return 0

    lax.fori_loop(0, 12, taps_step, 0)

    stage_a(3)
    stage_b(2)
    send_row(2)
    lax.fori_loop(0, 16, finish_out, 0)
    block_out = pltpu.make_async_copy(outs, out_block.at[0, 0], out_sem.at[0])
    block_out.start()
    stage_c(1)
    stage_d(0)
    build_taps(dwk, flat, back, back_h, True)

    def back_own(g, _):
        for i in range(8):
            spread(gzs[i, rows16(g), :], i, g, gs)
        v = jnp.dot(back[g], gs[g], preferred_element_type=F32)
        for i in range(8):
            zf[i, rows16(g), :] = ct[i, rows16(g), :].astype(F32) + v[i * 16 : i * 16 + 16, :]
        return 0

    def back_own_step(g, _):
        back_own(g, 0)

        @pl.when(g == 4)
        def _():
            stage_c(2)

        return 0

    lax.fori_loop(0, 12, back_own_step, 0)
    stage_b(3)
    stage_d(1)

    @pl.when(has_up)
    def _():
        for c in gz_down:
            c.wait_recv()

    @pl.when(t == 0)
    def _():
        halo[0] = jnp.zeros((3, 192, 256), BF16)

    @pl.when(has_down)
    def _():
        for c in gz_up:
            c.wait_recv()

    @pl.when(t == 31)
    def _():
        halo[1] = jnp.zeros((3, 192, 256), BF16)

    def back_halo(g, _):
        for r, slot in HALO_SLOTS:
            spread(halo[r // 8, r % 11, rows16(g), :], slot, g, gh_)
        v = jnp.dot(back_h[g], gh_[g], preferred_element_type=F32)
        for i in range(8):
            fx[i, rows16(g), :] = (zf[i, rows16(g), :] + v[i * 16 : i * 16 + 16, :]).astype(BF16)
        return 0

    def back_step(g, _):
        back_halo(g, 0)

        @pl.when(g == 5)
        def _():
            stage_c(3)

        return 0

    lax.fori_loop(0, 12, back_step, 0)
    gin_out = pltpu.make_async_copy(fx.at[pl.ds(0, 8)], out_gin.at[0, 0], out_sem.at[1])
    gin_out.start()
    stage_d(2)
    stage_d(3)
    for a in range(7):
        for tile, width in ((0, 128), (128, 64)):
            base = jnp.zeros((8, 128), F32)
            for g in range(tile // 16, (tile + width) // 16):
                at = g % 8 * 16
                v = pltpu.roll(fk[g], (at - a * 16) % 128, 1)
                base = jnp.where((lane >= at) & (lane < at + 16), v, base)
            out_gk[a, :, tile : tile + width] = base[0:7, 0:width] * PIXEL_SCALE

    @pl.when(has_up)
    def _():
        to_up.wait_send()
        for c in gz_up:
            c.wait_send()

    @pl.when(has_down)
    def _():
        to_down.wait_send()
        for c in gz_down:
            c.wait_send()

    block_out.wait()
    gin_out.wait()
    for f in range(3):
        full_out(f).wait()


def hand_over_kernel(
    block, gin, full, gk, out_block, out_gin, out_gk, out_gwi, out_gwoT, h_block, h_gin, h_gk, h_full, h_gwi, h_gwoT, sems
):
    plain = ((block, h_block, out_block), (gin, h_gin, out_gin), (gk, h_gk, out_gk))
    load = pltpu.make_async_copy(full, h_full, sems.at[0, 3])
    load.start()
    loads = [pltpu.make_async_copy(i, h, sems.at[0, n]) for n, (i, h, o) in enumerate(plain)]
    stores = [pltpu.make_async_copy(h, o, sems.at[1, n]) for n, (i, h, o) in enumerate(plain)]
    for c in loads:
        c.start()
    load.wait()
    for f in range(3):
        for j in range(16):
            part = h_full[f, j].astype(F32) * PIXEL_SCALE
            at, ln = j % 8 * 24, f * 256 + j // 8 * 128
            h_gwi[at : at + 24, ln : ln + 128] = part[0:24]
            h_gwoT[at : at + 24, ln : ln + 128] = part[24:48]
    for m, (held, out) in enumerate(((h_gwi, out_gwi), (h_gwoT, out_gwoT))):
        stores.append(pltpu.make_async_copy(held, out, sems.at[1, 3 + m]))
        stores[-1].start()
    for c, store in zip(loads, stores):
        c.wait()
        store.start()
    for c in stores:
        c.wait()


def hand_over(block, gin, full, gk):
    like = lambda v: jax.ShapeDtypeStruct(v.shape, v.dtype)
    weights = jax.ShapeDtypeStruct((192, 768), F32)
    shapes = (like(block), like(gin), like(gk), weights, weights)
    return pl.pallas_call(
        hand_over_kernel,
        out_shape=shapes,
        in_specs=[pl.BlockSpec(memory_space=pl.ANY)] * 4,
        out_specs=(pl.BlockSpec(memory_space=pl.ANY),) * 5,
        scratch_shapes=[pltpu.VMEM(v.shape, v.dtype) for v in (block, gin, gk, full, weights, weights)]
        + [pltpu.SemaphoreType.DMA((2, 5))],
    )(block, gin, full, gk)


def on_device(features, dw_kernel, dw_bias, ln_gain, ln_bias, w_in, b_in, w_out, b_out, layer_scale, cotangent):
    row = lambda v: v.reshape(1, -1)
    turn = lambda v: jnp.swapaxes(v, 3, 4)
    any_, vmem = pl.BlockSpec(memory_space=pl.ANY), pl.BlockSpec(memory_space=pltpu.VMEM)
    V, DMA = pltpu.VMEM, pltpu.SemaphoreType.DMA
    groups = V((12, 896, 256), BF16)
    tables = V((12, 128, 896), BF16)
    scratch = [
        V((14, 192, 256), BF16), V((8, 192, 256), BF16), groups, groups, groups, groups, tables, tables, tables, tables,
        V((19, 8, 256), F32), V((8, 192, 256), F32), V((5, 256, 128), F32), V((768, 128), F32), V((768, 192), BF16),
        V((768, 192), BF16), V((8, 192, 256), BF16),
        V((8, 192, 256), BF16), V((8, 8, 256), F32), V((8, 192, 256), F32), V((8, 192, 256), F32), V((8, 192, 256), BF16),
        V((8, 192, 256), BF16), V((2, 3, 192, 256), F32), V((16, 8, 128), F32), V((2, 3, 192, 256), BF16),
        V((3, 16, 48, 128), BF16), V((3, 15, 48, 128), BF16), V((3, 8, 48, 128), F32), V((3, 16, 48, 128), BF16),
        V((15, 8, 128), F32), V((8, 8, 128), F32), V((16, 8, 128), F32),
        DMA((2,)), DMA((5,)), DMA((8,)), DMA((8,)), DMA((4, 37)), DMA((4, 37)),
    ]
    values = pl.pallas_call(
        kernel,
        out_shape=(
            jax.ShapeDtypeStruct((1, 1, 8, 192, 256), BF16), jax.ShapeDtypeStruct((1, 1, 8, 192, 256), BF16),
            jax.ShapeDtypeStruct((3, 16, 48, 128), BF16), jax.ShapeDtypeStruct((7, 7, 192), F32),
        ),
        in_specs=[any_, any_] + [vmem] * 9,
        out_specs=(any_, any_, any_, vmem),
        scratch_shapes=scratch,
        compiler_params=pltpu.CompilerParams(collective_id=0, has_side_effects=True, vmem_limit_bytes=60 << 20),
    )(
        turn(features), turn(cotangent), dw_kernel, row(dw_bias), row(ln_gain), row(ln_bias), w_in, b_in, w_out.T, row(b_out),
        row(layer_scale),
    )
    block, gin, gk, gwi, gwoT = hand_over(*values)
    return turn(block), turn(gin), gwi, gwoT.T, gk


def solution(mesh):
    split, whole = P("slide", "space", None, None, None), P()
    return jax.shard_map(
        on_device,
        mesh=mesh,
        in_specs=(split,) + (whole,) * 9 + (split,),
        out_specs=(split, split, whole, whole, whole),
        check_vma=False,
    )
```

```python
import jax
import jax.numpy as jnp
from jax import lax
from jax.experimental import pallas as pl
from jax.experimental.pallas import tpu as pltpu
from jax.sharding import PartitionSpec as P

EPSILON = 1e-06
F32 = jnp.float32
BF16 = jnp.bfloat16
MESH = pl.DeviceIdType.MESH
PIXEL_SCALE = float(262144) ** (-0.5)
NT = (((1,), (1,)), ((), ()))


def remote(src, dst, send, recv, slide, space):
    return pltpu.make_async_remote_copy(
        src_ref=src, dst_ref=dst, send_sem=send, recv_sem=recv,
        device_id={"slide": slide, "space": space}, device_id_type=MESH,
    )


def gelu_parts(h):
    r = h * 0.7071067811865476
    cdf = 0.5 + 0.5 * lax.erf(r)
    density = jnp.exp2(r * r * -1.4426950408889634)
    return h * cdf, cdf + (h * 0.3989422804014327) * density


def spread(value, slot, group, dst):
    lane = lax.broadcasted_iota(jnp.int32, (16, 128), 1)
    left, right = value[:, 0:128], value[:, 128:256]
    none = jnp.zeros_like(left)
    for b in range(7):
        d = b - 3
        first, second = left, right
        if d:
            first, second = pltpu.roll(left, -d % 128, 1), pltpu.roll(right, -d % 128, 1)
            if d > 0:
                first, second = jnp.where(lane < 128 - d, first, second), jnp.where(lane < 128 - d, second, none)
            else:
                first, second = jnp.where(lane < -d, none, first), jnp.where(lane < -d, first, second)
        at = b * 128 + slot * 16
        dst[group, at : at + 16, 0:128] = first
        dst[group, at : at + 16, 128:256] = second


def valid(i, lane):
    slot = lane // 16
    own = (slot >= i - 3) & (slot <= i + 3)
    halo = jnp.zeros_like(own)
    if i < 3:
        halo = slot >= i + 5
    if i >= 5:
        halo = slot <= i - 5
    return own, halo


def build_taps(dwk, flat, own, halo, flip):
    lane8 = lax.broadcasted_iota(jnp.int32, (8, 128), 1)
    for a in range(7):
        flat[a, 0:7, 0:192] = jnp.concatenate(
            [dwk[6 - a if flip else a, (6 - b if flip else b) : (6 - b if flip else b) + 1, :] for b in range(7)], axis=0
        )
    for g in range(12):
        base = jnp.zeros((8, 128), F32)
        tile, at = g // 8 * 128, g % 8 * 16
        for a in range(7):
            v = flat[a, :, tile : tile + 128]
            v = pltpu.roll(v, (a * 16 - at) % 128, 1)
            base = jnp.where((lane8 >= a * 16) & (lane8 < a * 16 + 16), v, base)
        flat[7 + g, :, 0:128] = base
    lane = lax.broadcasted_iota(jnp.int32, (16, 128), 1)
    same = lane % 16 == lax.broadcasted_iota(jnp.int32, (16, 128), 0)

    def group(g, _):
        base = flat[7 + g, :, 0:128]
        for i in range(8):
            moved = pltpu.roll(base, (i - 3) * 16 % 128, 1)
            for keep, dst in zip(valid(i, lane8), (own, halo)):
                if dst is halo and 3 <= i < 5:
                    dst[g, i * 16 : i * 16 + 16, :] = jnp.zeros((16, 896), BF16)
                    continue
                v = jnp.where(keep, moved, 0.0)
                for b in range(7):
                    row = jnp.broadcast_to(v[b : b + 1, :], (16, 128))
                    dst[g, i * 16 : i * 16 + 16, b * 128 : b * 128 + 128] = jnp.where(same, row, 0.0).astype(BF16)
        return 0

    lax.fori_loop(0, 12, group, 0)


def both(v):
    return jnp.concatenate([v, v], axis=1)


def rows16(g):
    return pl.ds(pl.multiple_of(g * 16, 16), 16)


HALO_SLOTS = ((0, 5), (1, 6), (2, 7), (11, 0), (12, 1), (13, 2))


def kernel(
    feat, cot, dwk, dwb, gain, lbias, w_in, b_in, woutT, b_out, lscale,
    out_block, out_gin, out_full, out_gk,
    fx, ct, xs, xh, gs, gh_, taps, taps_h, back, back_h, flat, zf, par, bias, winT, wout, gout,
    nb, rinv, osum, nsum, outs, gzs, gw, gkr, halo,
    pa, ra, rb, fc, rk, rk2, fk,
    in_sem, out_sem, halo_send, halo_recv, ar_send, ar_recv,
):
    s, t = lax.axis_index("slide"), lax.axis_index("space")
    z_hi, core = s // 2, s % 2
    z_lo = t % 2
    z = z_hi * 2 + z_lo
    plane, pillar = t // 2, z * 2 + core
    plane_peers = [((plane + e) % 16) for e in range(1, 16)]
    pillar_peers = [((pillar + e) % 8) for e in range(1, 8)]

    def in_plane(p):
        return s, p * 2 + z_lo

    def in_pillar(q):
        return q // 4 * 2 + q % 2, plane * 2 + q // 2 % 2

    has_up, has_down = t > 0, t < 31
    up, down = jnp.maximum(t - 1, 0), jnp.minimum(t + 1, 31)

    own_in = pltpu.make_async_copy(feat.at[0, 0], fx.at[pl.ds(3, 8)], in_sem.at[0])
    own_in.start()
    cot_in = pltpu.make_async_copy(cot.at[0, 0], ct, in_sem.at[1])
    cot_in.start()

    barrier = pltpu.get_barrier_semaphore()
    for ps, pt in [in_plane(p) for p in plane_peers] + [in_pillar(q) for q in pillar_peers]:
        pl.semaphore_signal(barrier, inc=1, device_id={"slide": ps, "space": pt}, device_id_type=MESH)

    @pl.when(has_up)
    def _():
        pl.semaphore_signal(barrier, inc=1, device_id={"slide": s, "space": up}, device_id_type=MESH)

    @pl.when(has_down)
    def _():
        pl.semaphore_signal(barrier, inc=1, device_id={"slide": s, "space": down}, device_id_type=MESH)

    pl.semaphore_wait(barrier, 22 + jnp.minimum(t, 1) + jnp.minimum(31 - t, 1))

    to_up = remote(feat.at[0, 0, pl.ds(0, 3)], fx.at[pl.ds(11, 3)], halo_send.at[0], halo_recv.at[0], s, up)
    to_down = remote(feat.at[0, 0, pl.ds(5, 3)], fx.at[pl.ds(0, 3)], halo_send.at[1], halo_recv.at[1], s, down)

    @pl.when(has_up)
    def _():
        to_up.start()

    @pl.when(has_down)
    def _():
        to_down.start()

    for n, ref in enumerate((dwb, gain, lbias, b_out, lscale)):
        par[n, 0:128, :] = jnp.broadcast_to(ref[:, 0:128], (128, 128)).T
        par[n, 128:256, :] = jnp.broadcast_to(both(ref[:, 128:192]), (128, 128)).T
    for n in range(6):
        bias[n * 128 : n * 128 + 128, :] = jnp.broadcast_to(b_in[n * 128 : n * 128 + 128].reshape(1, 128), (128, 128)).T
    winT[...] = w_in[...].T
    wout[...] = woutT[...].T
    build_taps(dwk, flat, taps, taps_h, False)

    def clear(g, _):
        none = jnp.zeros((32, 256), BF16)
        for b in range(7):
            xh[g, b * 128 + 48 : b * 128 + 80, :] = none
            gh_[g, b * 128 + 48 : b * 128 + 80, :] = none
        return 0

    lax.fori_loop(0, 12, clear, 0)
    own_in.wait()

    def conv_own(g, _):
        for i in range(8):
            spread(fx[i + 3, rows16(g), :], i, g, xs)
        v = jnp.dot(taps[g], xs[g], preferred_element_type=F32)
        for i in range(8):
            zf[i, rows16(g), :] = v[i * 16 : i * 16 + 16, :] + both(par[0, rows16(g), :])
        return 0

    lax.fori_loop(0, 12, conv_own, 0)
    cot_in.wait()

    def scale_row(i, _):
        gout[i] = (both(par[4, 0:192, :]) * ct[i].astype(F32)).astype(BF16)
        return 0

    lax.fori_loop(0, 8, scale_row, 0)

    def norm(n, _):
        i = n // 2
        ln = pl.ds(pl.multiple_of(n % 2 * 128, 128), 128)
        v = zf[i, :, ln]
        v = v - jnp.sum(v, axis=0, keepdims=True) * (1.0 / 192)
        var = jnp.sum(v * v, axis=0, keepdims=True) * (1.0 / 192)
        r = lax.rsqrt(var + EPSILON)
        v = v * r
        zf[i, :, ln] = v
        rinv[i, :, ln] = jnp.broadcast_to(r, (8, 128))
        nb[i, :, ln] = (v * par[1, 0:192, :] + par[2, 0:192, :]).astype(BF16)
        return 0

    lax.fori_loop(6, 10, norm, 0)

    gw[...] = jnp.zeros_like(gw)
    osum[...] = jnp.zeros_like(osum)
    nsum[...] = jnp.zeros_like(nsum)

    def mlp_pair(f, p):
        units = pl.ds(pl.multiple_of(f * 256, 256), 256)
        q = 7 - p
        normed = jnp.concatenate([nb[p], nb[q]], axis=1)
        upper = jnp.concatenate([gout[p], gout[q]], axis=1)
        hidden = jnp.dot(winT[units, :], normed, preferred_element_type=F32) + both(both(bias[units, :]))
        value, slope = gelu_parts(hidden)
        act = value.astype(BF16)
        gh = (jnp.dot(wout[units, :], upper, preferred_element_type=F32) * slope).astype(BF16)
        out = jnp.dot(woutT[:, units], act, preferred_element_type=F32)
        osum[p] += out[:, 0:256]
        osum[q] += out[:, 256:512]
        out = jnp.dot(w_in[:, units], gh, preferred_element_type=F32)
        nsum[p] += out[:, 0:256]
        nsum[q] += out[:, 256:512]
        gw[0, f] += lax.dot_general(normed, gh, NT, preferred_element_type=F32)
        gw[1, f] += lax.dot_general(upper, act, NT, preferred_element_type=F32)

    def mlp_inner(k, _):
        mlp_pair(k, 3)
        return 0

    lax.fori_loop(0, 3, mlp_inner, 0)

    @pl.when(has_up)
    def _():
        to_down.wait_recv()

    @pl.when(t == 0)
    def _():
        fx[0:3] = jnp.zeros((3, 192, 256), BF16)

    @pl.when(has_down)
    def _():
        to_up.wait_recv()

    @pl.when(t == 31)
    def _():
        fx[11:14] = jnp.zeros((3, 192, 256), BF16)

    def conv_halo(g, _):
        for r, slot in HALO_SLOTS:
            spread(fx[r, rows16(g), :], slot, g, xh)
        v = jnp.dot(taps_h[g], xh[g], preferred_element_type=F32)
        for i in (0, 1, 2, 5, 6, 7):
            zf[i, rows16(g), :] += v[i * 16 : i * 16 + 16, :]
        return 0

    lax.fori_loop(0, 12, conv_halo, 0)

    lax.fori_loop(0, 6, norm, 0)
    lax.fori_loop(10, 16, norm, 0)

    def buffers(f):
        return (gkr, rk, rk2, fk) if f == 3 else (pa.at[f], ra.at[f], rb.at[f], fc.at[f])

    def spread_copies(f):
        own, got, _, _ = buffers(f)
        return [
            remote(own.at[p], got.at[e], ar_send.at[f, e], ar_recv.at[f, e], *in_plane(p)) for e, p in enumerate(plane_peers)
        ]

    def pillar_copies(f):
        part = buffers(f)[2].at[pillar]
        return [
            remote(part, part, ar_send.at[f, 15 + e], ar_recv.at[f, 15 + e], *in_pillar(q)) for e, q in enumerate(pillar_peers)
        ]

    def back_copies(f):
        part = buffers(f)[3].at[plane]
        return [
            remote(part, part, ar_send.at[f, 22 + e], ar_recv.at[f, 22 + e], *in_plane(p)) for e, p in enumerate(plane_peers)
        ]

    def full_out(f):
        return pltpu.make_async_copy(fc.at[f], out_full.at[f], out_sem.at[2 + f])

    def stage_a(f):
        if f < 3:
            for j in range(16):
                at, ln = j % 8 * 24, j // 8 * 128
                part = [gw[m, f, at : at + 24, ln : ln + 128] for m in range(2)]
                pa[f, j] = jnp.concatenate(part, axis=0).astype(BF16)
        for c in spread_copies(f):
            c.start()

    def stage_b(f):
        for c in spread_copies(f):
            c.wait()
        own, got, mine, _ = buffers(f)
        total = own[plane].astype(F32)
        for e in range(15):
            total = total + got[e].astype(F32)
        mine[pillar] = total.astype(mine.dtype)
        for c in pillar_copies(f):
            c.start()

    def stage_c(f):
        for c in pillar_copies(f):
            c.wait()
        _, _, mine, result = buffers(f)
        total = mine[0].astype(F32)
        for q in range(1, 8):
            total = total + mine[q].astype(F32)
        result[plane] = total.astype(result.dtype)
        for c in back_copies(f):
            c.start()

    def stage_d(f):
        for c in back_copies(f):
            c.wait()
        if f < 3:
            full_out(f).start()

    def finish(n, _):
        i = n // 2
        ln = pl.ds(pl.multiple_of(n % 2 * 128, 128), 128)
        gn = nsum[i, :, ln] * par[1, 0:192, :]
        u = zf[i, :, ln]
        m1 = jnp.sum(gn, axis=0, keepdims=True) * (1.0 / 192)
        m2 = jnp.sum(gn * u, axis=0, keepdims=True) * (1.0 / 192)
        gzs[i, :, ln] = (rinv[i, 0:1, ln] * (gn - m1 - u * m2)).astype(BF16)
        return 0

    def finish_out(n, _):
        i = n // 2
        ln = pl.ds(pl.multiple_of(n % 2 * 128, 128), 128)
        branch = osum[i, :, ln] + par[3, 0:192, :]
        outs[i, :, ln] = (fx[i + 3, :, ln].astype(F32) + par[4, 0:192, :] * branch).astype(BF16)
        return 0

    gz_up = [remote(gzs.at[n], halo.at[1, n], halo_send.at[2 + n], halo_recv.at[2 + n], s, up) for n in range(3)]
    gz_down = [remote(gzs.at[7 - n], halo.at[0, 2 - n], halo_send.at[5 + n], halo_recv.at[5 + n], s, down) for n in range(3)]

    def send_row(n):
        @pl.when(has_up)
        def _():
            gz_up[n].start()

        @pl.when(has_down)
        def _():
            gz_down[n].start()


    def mlp_outer(k, _):
        mlp_pair(k, 0)
        return 0

    lax.fori_loop(0, 3, mlp_outer, 0)
    lax.fori_loop(0, 2, finish, 0)
    lax.fori_loop(14, 16, finish, 0)
    send_row(0)
    after = {1: [(stage_a, 0)], 3: [(stage_a, 1)], 5: [(stage_a, 2)]}

    def mlp(k, _):
        mlp_pair(k // 2, 1 + k % 2)
        for at, steps in after.items():

            @pl.when(k == at)
            def _():
                for step, chunk in steps:
                    step(chunk)

        return 0

    lax.fori_loop(0, 6, mlp, 0)
    lax.fori_loop(2, 14, finish, 0)
    stage_b(0)
    send_row(1)

    lane = lax.broadcasted_iota(jnp.int32, (8, 128), 1)
    sub = lax.broadcasted_iota(jnp.int32, (8, 128), 0)

    def taps_grad(g, _):
        mine = jnp.concatenate([gzs[i, rows16(g), :] for i in range(8)], axis=0)
        for b in range(7):
            rows = pl.ds(b * 128, 128)
            pairs = lax.dot_general(mine, jnp.concatenate([xs[g, rows, :], xh[g, rows, :]], axis=0), NT, preferred_element_type=F32)
            at_own, at_halo = pairs[:, 0:128], pairs[:, 128:256]
            total = jnp.zeros((8, 128), F32)
            for i in range(8):
                use_own, use_halo = valid(i, lane)
                v = jnp.zeros((8, 128), F32)
                for h in range(2):
                    at = i * 16 + h * 8
                    same = lane % 16 == sub + h * 8
                    v = jnp.where(same & use_own, at_own[at : at + 8], v)
                    if not 3 <= i < 5:
                        v = jnp.where(same & use_halo, at_halo[at : at + 8], v)
                total = total + (pltpu.roll(v, (3 - i) * 16 % 128, 1) if i != 3 else v)
            gkr[g, b : b + 1, :] = jnp.sum(total, axis=0, keepdims=True)
        return 0

    gkr[...] = jnp.zeros_like(gkr)
    def taps_step(g, _):
        taps_grad(g, 0)

        @pl.when(g == 5)
        def _():
            stage_b(1)
            send_row(2)

        @pl.when(g == 8)
        def _():
            stage_c(0)

        return 0

    lax.fori_loop(0, 12, taps_step, 0)

    stage_a(3)
    stage_b(2)
    lax.fori_loop(0, 16, finish_out, 0)
    block_out = pltpu.make_async_copy(outs, out_block.at[0, 0], out_sem.at[0])
    block_out.start()
    stage_c(1)
    stage_d(0)
    build_taps(dwk, flat, back, back_h, True)

    def back_own(g, _):
        for i in range(8):
            spread(gzs[i, rows16(g), :], i, g, gs)
        v = jnp.dot(back[g], gs[g], preferred_element_type=F32)
        for i in range(8):
            zf[i, rows16(g), :] = ct[i, rows16(g), :].astype(F32) + v[i * 16 : i * 16 + 16, :]
        return 0

    def back_own_step(g, _):
        back_own(g, 0)

        @pl.when(g == 4)
        def _():
            stage_c(2)

        return 0

    lax.fori_loop(0, 12, back_own_step, 0)
    stage_b(3)
    stage_d(1)

    @pl.when(has_up)
    def _():
        for c in gz_down:
            c.wait_recv()

    @pl.when(t == 0)
    def _():
        halo[0] = jnp.zeros((3, 192, 256), BF16)

    @pl.when(has_down)
    def _():
        for c in gz_up:
            c.wait_recv()

    @pl.when(t == 31)
    def _():
        halo[1] = jnp.zeros((3, 192, 256), BF16)

    def back_halo(g, _):
        for r, slot in HALO_SLOTS:
            spread(halo[r // 8, r % 11, rows16(g), :], slot, g, gh_)
        v = jnp.dot(back_h[g], gh_[g], preferred_element_type=F32)
        for i in range(8):
            fx[i, rows16(g), :] = (zf[i, rows16(g), :] + v[i * 16 : i * 16 + 16, :]).astype(BF16)
        return 0

    def back_step(g, _):
        back_halo(g, 0)

        @pl.when(g == 5)
        def _():
            stage_c(3)

        return 0

    lax.fori_loop(0, 12, back_step, 0)
    gin_out = pltpu.make_async_copy(fx.at[pl.ds(0, 8)], out_gin.at[0, 0], out_sem.at[1])
    gin_out.start()
    stage_d(2)
    stage_d(3)
    for a in range(7):
        for tile, width in ((0, 128), (128, 64)):
            base = jnp.zeros((8, 128), F32)
            for g in range(tile // 16, (tile + width) // 16):
                at = g % 8 * 16
                v = pltpu.roll(fk[g], (at - a * 16) % 128, 1)
                base = jnp.where((lane >= at) & (lane < at + 16), v, base)
            out_gk[a, :, tile : tile + width] = base[0:7, 0:width] * PIXEL_SCALE

    @pl.when(has_up)
    def _():
        to_up.wait_send()
        for c in gz_up:
            c.wait_send()

    @pl.when(has_down)
    def _():
        to_down.wait_send()
        for c in gz_down:
            c.wait_send()

    block_out.wait()
    gin_out.wait()
    for f in range(3):
        full_out(f).wait()


def hand_over_kernel(
    block, gin, full, gk, out_block, out_gin, out_gk, out_gwi, out_gwoT, h_block, h_gin, h_gk, h_full, h_gwi, h_gwoT, sems
):
    plain = ((block, h_block, out_block), (gin, h_gin, out_gin), (gk, h_gk, out_gk))
    load = pltpu.make_async_copy(full, h_full, sems.at[0, 3])
    load.start()
    loads = [pltpu.make_async_copy(i, h, sems.at[0, n]) for n, (i, h, o) in enumerate(plain)]
    stores = [pltpu.make_async_copy(h, o, sems.at[1, n]) for n, (i, h, o) in enumerate(plain)]
    for c in loads:
        c.start()
    load.wait()
    for f in range(3):
        for j in range(16):
            part = h_full[f, j].astype(F32) * PIXEL_SCALE
            at, ln = j % 8 * 24, f * 256 + j // 8 * 128
            h_gwi[at : at + 24, ln : ln + 128] = part[0:24]
            h_gwoT[at : at + 24, ln : ln + 128] = part[24:48]
    for m, (held, out) in enumerate(((h_gwi, out_gwi), (h_gwoT, out_gwoT))):
        stores.append(pltpu.make_async_copy(held, out, sems.at[1, 3 + m]))
        stores[-1].start()
    for c, store in zip(loads, stores):
        c.wait()
        store.start()
    for c in stores:
        c.wait()


def hand_over(block, gin, full, gk):
    like = lambda v: jax.ShapeDtypeStruct(v.shape, v.dtype)
    weights = jax.ShapeDtypeStruct((192, 768), F32)
    shapes = (like(block), like(gin), like(gk), weights, weights)
    return pl.pallas_call(
        hand_over_kernel,
        out_shape=shapes,
        in_specs=[pl.BlockSpec(memory_space=pl.ANY)] * 4,
        out_specs=(pl.BlockSpec(memory_space=pl.ANY),) * 5,
        scratch_shapes=[pltpu.VMEM(v.shape, v.dtype) for v in (block, gin, gk, full, weights, weights)]
        + [pltpu.SemaphoreType.DMA((2, 5))],
    )(block, gin, full, gk)


def on_device(features, dw_kernel, dw_bias, ln_gain, ln_bias, w_in, b_in, w_out, b_out, layer_scale, cotangent):
    row = lambda v: v.reshape(1, -1)
    turn = lambda v: jnp.swapaxes(v, 3, 4)
    any_, vmem = pl.BlockSpec(memory_space=pl.ANY), pl.BlockSpec(memory_space=pltpu.VMEM)
    V, DMA = pltpu.VMEM, pltpu.SemaphoreType.DMA
    groups = V((12, 896, 256), BF16)
    tables = V((12, 128, 896), BF16)
    scratch = [
        V((14, 192, 256), BF16), V((8, 192, 256), BF16), groups, groups, groups, groups, tables, tables, tables, tables,
        V((19, 8, 256), F32), V((8, 192, 256), F32), V((5, 256, 128), F32), V((768, 128), F32), V((768, 192), BF16),
        V((768, 192), BF16), V((8, 192, 256), BF16),
        V((8, 192, 256), BF16), V((8, 8, 256), F32), V((8, 192, 256), F32), V((8, 192, 256), F32), V((8, 192, 256), BF16),
        V((8, 192, 256), BF16), V((2, 3, 192, 256), F32), V((16, 8, 128), F32), V((2, 3, 192, 256), BF16),
        V((3, 16, 48, 128), BF16), V((3, 15, 48, 128), BF16), V((3, 8, 48, 128), BF16), V((3, 16, 48, 128), BF16),
        V((15, 8, 128), F32), V((8, 8, 128), F32), V((16, 8, 128), F32),
        DMA((2,)), DMA((5,)), DMA((8,)), DMA((8,)), DMA((4, 37)), DMA((4, 37)),
    ]
    values = pl.pallas_call(
        kernel,
        out_shape=(
            jax.ShapeDtypeStruct((1, 1, 8, 192, 256), BF16), jax.ShapeDtypeStruct((1, 1, 8, 192, 256), BF16),
            jax.ShapeDtypeStruct((3, 16, 48, 128), BF16), jax.ShapeDtypeStruct((7, 7, 192), F32),
        ),
        in_specs=[any_, any_] + [vmem] * 9,
        out_specs=(any_, any_, any_, vmem),
        scratch_shapes=scratch,
        compiler_params=pltpu.CompilerParams(collective_id=0, has_side_effects=True, vmem_limit_bytes=60 << 20),
    )(
        turn(features), turn(cotangent), dw_kernel, row(dw_bias), row(ln_gain), row(ln_bias), w_in, b_in, w_out.T, row(b_out),
        row(layer_scale),
    )
    block, gin, gk, gwi, gwoT = hand_over(*values)
    return turn(block), turn(gin), gwi, gwoT.T, gk


def solution(mesh):
    split, whole = P("slide", "space", None, None, None), P()
    return jax.shard_map(
        on_device,
        mesh=mesh,
        in_specs=(split,) + (whole,) * 9 + (split,),
        out_specs=(split, split, whole, whole, whole),
        check_vma=False,
    )
```

```python
import jax
import jax.numpy as jnp
from jax import lax
from jax.experimental import pallas as pl
from jax.experimental.pallas import tpu as pltpu
from jax.sharding import PartitionSpec as P

EPSILON = 1e-06
F32 = jnp.float32
BF16 = jnp.bfloat16
MESH = pl.DeviceIdType.MESH
PIXEL_SCALE = float(262144) ** (-0.5)
NT = (((1,), (1,)), ((), ()))


def remote(src, dst, send, recv, slide, space):
    return pltpu.make_async_remote_copy(
        src_ref=src, dst_ref=dst, send_sem=send, recv_sem=recv,
        device_id={"slide": slide, "space": space}, device_id_type=MESH,
    )


def gelu_parts(h):
    r = h * 0.7071067811865476
    cdf = 0.5 + 0.5 * lax.erf(r)
    density = jnp.exp2(r * r * -1.4426950408889634)
    return h * cdf, cdf + (h * 0.3989422804014327) * density


def spread(value, slot, group, dst):
    lane = lax.broadcasted_iota(jnp.int32, (16, 128), 1)
    left, right = value[:, 0:128], value[:, 128:256]
    none = jnp.zeros_like(left)
    for b in range(7):
        d = b - 3
        first, second = left, right
        if d:
            first, second = pltpu.roll(left, -d % 128, 1), pltpu.roll(right, -d % 128, 1)
            if d > 0:
                first, second = jnp.where(lane < 128 - d, first, second), jnp.where(lane < 128 - d, second, none)
            else:
                first, second = jnp.where(lane < -d, none, first), jnp.where(lane < -d, first, second)
        at = b * 128 + slot * 16
        dst[group, at : at + 16, 0:128] = first
        dst[group, at : at + 16, 128:256] = second


def valid(i, lane):
    slot = lane // 16
    own = (slot >= i - 3) & (slot <= i + 3)
    halo = jnp.zeros_like(own)
    if i < 3:
        halo = slot >= i + 5
    if i >= 5:
        halo = slot <= i - 5
    return own, halo


def build_taps(dwk, flat, own, halo, flip):
    lane8 = lax.broadcasted_iota(jnp.int32, (8, 128), 1)
    for a in range(7):
        flat[a, 0:7, 0:192] = jnp.concatenate(
            [dwk[6 - a if flip else a, (6 - b if flip else b) : (6 - b if flip else b) + 1, :] for b in range(7)], axis=0
        )
    for g in range(12):
        base = jnp.zeros((8, 128), F32)
        tile, at = g // 8 * 128, g % 8 * 16
        for a in range(7):
            v = flat[a, :, tile : tile + 128]
            v = pltpu.roll(v, (a * 16 - at) % 128, 1)
            base = jnp.where((lane8 >= a * 16) & (lane8 < a * 16 + 16), v, base)
        flat[7 + g, :, 0:128] = base
    lane = lax.broadcasted_iota(jnp.int32, (16, 128), 1)
    same = lane % 16 == lax.broadcasted_iota(jnp.int32, (16, 128), 0)

    def group(g, _):
        base = flat[7 + g, :, 0:128]
        for i in range(8):
            moved = pltpu.roll(base, (i - 3) * 16 % 128, 1)
            for keep, dst in zip(valid(i, lane8), (own, halo)):
                if dst is halo and 3 <= i < 5:
                    dst[g, i * 16 : i * 16 + 16, :] = jnp.zeros((16, 896), BF16)
                    continue
                v = jnp.where(keep, moved, 0.0)
                for b in range(7):
                    row = jnp.broadcast_to(v[b : b + 1, :], (16, 128))
                    dst[g, i * 16 : i * 16 + 16, b * 128 : b * 128 + 128] = jnp.where(same, row, 0.0).astype(BF16)
        return 0

    lax.fori_loop(0, 12, group, 0)


def both(v):
    return jnp.concatenate([v, v], axis=1)


def rows16(g):
    return pl.ds(pl.multiple_of(g * 16, 16), 16)


HALO_SLOTS = ((0, 5), (1, 6), (2, 7), (11, 0), (12, 1), (13, 2))


def kernel(
    feat, cot, dwk, dwb, gain, lbias, w_in, b_in, woutT, b_out, lscale,
    out_block, out_gin, out_full, out_gk,
    fx, ct, xs, xh, gs, gh_, taps, taps_h, back, back_h, flat, zf, par, bias, winT, wout, gout,
    nb, rinv, osum, nsum, outs, gzs, gw, gkr, halo,
    pay, r0, s1f, s1b, r1, s2, r2, rz, fa, full, k0, kx, ky, kz, kfull,
    in_sem, out_sem, halo_send, halo_recv, ar_send, ar_recv, k_send, k_recv,
):
    s, t = lax.axis_index("slide"), lax.axis_index("space")
    z_hi, core = s // 2, s % 2
    z_lo, x, y = t % 2, (t // 2) % 4, t // 8
    z = z_hi * 2 + z_lo
    partner = z_hi * 2 + (1 - core)
    x_peers = [(s, (y * 4 + (x + d) % 4) * 2 + z_lo) for d in (1, 2, 3)]
    y_peers = [(s, (((y + d) % 4) * 4 + x) * 2 + z_lo) for d in (1, 2, 3)]
    z_peers = [(((z + d) % 4) // 2 * 2 + core, (y * 4 + x) * 2 + ((z + d) % 4) % 2) for d in (1, 2, 3)]
    has_up, has_down = t > 0, t < 31
    up, down = jnp.maximum(t - 1, 0), jnp.minimum(t + 1, 31)

    own_in = pltpu.make_async_copy(feat.at[0, 0], fx.at[pl.ds(3, 8)], in_sem.at[0])
    own_in.start()
    cot_in = pltpu.make_async_copy(cot.at[0, 0], ct, in_sem.at[1])
    cot_in.start()

    barrier = pltpu.get_barrier_semaphore()
    for ps, pt in [(partner, t)] + x_peers + y_peers + z_peers:
        pl.semaphore_signal(barrier, inc=1, device_id={"slide": ps, "space": pt}, device_id_type=MESH)

    @pl.when(has_up)
    def _():
        pl.semaphore_signal(barrier, inc=1, device_id={"slide": s, "space": up}, device_id_type=MESH)

    @pl.when(has_down)
    def _():
        pl.semaphore_signal(barrier, inc=1, device_id={"slide": s, "space": down}, device_id_type=MESH)

    pl.semaphore_wait(barrier, 10 + jnp.minimum(t, 1) + jnp.minimum(31 - t, 1))

    to_up = remote(feat.at[0, 0, pl.ds(0, 3)], fx.at[pl.ds(11, 3)], halo_send.at[0], halo_recv.at[0], s, up)
    to_down = remote(feat.at[0, 0, pl.ds(5, 3)], fx.at[pl.ds(0, 3)], halo_send.at[1], halo_recv.at[1], s, down)

    @pl.when(has_up)
    def _():
        to_up.start()

    @pl.when(has_down)
    def _():
        to_down.start()

    for n, ref in enumerate((dwb, gain, lbias, b_out, lscale)):
        par[n, 0:128, :] = jnp.broadcast_to(ref[:, 0:128], (128, 128)).T
        par[n, 128:256, :] = jnp.broadcast_to(both(ref[:, 128:192]), (128, 128)).T
    for n in range(6):
        bias[n * 128 : n * 128 + 128, :] = jnp.broadcast_to(b_in[n * 128 : n * 128 + 128].reshape(1, 128), (128, 128)).T
    winT[...] = w_in[...].T
    wout[...] = woutT[...].T
    build_taps(dwk, flat, taps, taps_h, False)

    def clear(g, _):
        none = jnp.zeros((32, 256), BF16)
        for b in range(7):
            xh[g, b * 128 + 48 : b * 128 + 80, :] = none
            gh_[g, b * 128 + 48 : b * 128 + 80, :] = none
        return 0

    lax.fori_loop(0, 12, clear, 0)
    own_in.wait()

    def conv_own(g, _):
        for i in range(8):
            spread(fx[i + 3, rows16(g), :], i, g, xs)
        v = jnp.dot(taps[g], xs[g], preferred_element_type=F32)
        for i in range(8):
            zf[i, rows16(g), :] = v[i * 16 : i * 16 + 16, :] + both(par[0, rows16(g), :])
        return 0

    lax.fori_loop(0, 12, conv_own, 0)
    cot_in.wait()

    def scale_row(i, _):
        gout[i] = (both(par[4, 0:192, :]) * ct[i].astype(F32)).astype(BF16)
        return 0

    lax.fori_loop(0, 8, scale_row, 0)

    def norm(n, _):
        i = n // 2
        ln = pl.ds(pl.multiple_of(n % 2 * 128, 128), 128)
        v = zf[i, :, ln]
        v = v - jnp.sum(v, axis=0, keepdims=True) * (1.0 / 192)
        var = jnp.sum(v * v, axis=0, keepdims=True) * (1.0 / 192)
        r = lax.rsqrt(var + EPSILON)
        v = v * r
        zf[i, :, ln] = v
        rinv[i, :, ln] = jnp.broadcast_to(r, (8, 128))
        nb[i, :, ln] = (v * par[1, 0:192, :] + par[2, 0:192, :]).astype(BF16)
        return 0

    lax.fori_loop(6, 10, norm, 0)

    gw[...] = jnp.zeros_like(gw)
    osum[...] = jnp.zeros_like(osum)
    nsum[...] = jnp.zeros_like(nsum)

    def mlp_pair(f, p):
        units = pl.ds(pl.multiple_of(f * 256, 256), 256)
        q = 7 - p
        normed = jnp.concatenate([nb[p], nb[q]], axis=1)
        upper = jnp.concatenate([gout[p], gout[q]], axis=1)
        hidden = jnp.dot(winT[units, :], normed, preferred_element_type=F32) + both(both(bias[units, :]))
        value, slope = gelu_parts(hidden)
        act = value.astype(BF16)
        gh = (jnp.dot(wout[units, :], upper, preferred_element_type=F32) * slope).astype(BF16)
        out = jnp.dot(woutT[:, units], act, preferred_element_type=F32)
        osum[p] += out[:, 0:256]
        osum[q] += out[:, 256:512]
        out = jnp.dot(w_in[:, units], gh, preferred_element_type=F32)
        nsum[p] += out[:, 0:256]
        nsum[q] += out[:, 256:512]
        gw[0, f] += lax.dot_general(normed, gh, NT, preferred_element_type=F32)
        gw[1, f] += lax.dot_general(upper, act, NT, preferred_element_type=F32)

    def mlp_inner(k, _):
        mlp_pair(k, 3)
        return 0

    lax.fori_loop(0, 3, mlp_inner, 0)

    @pl.when(has_up)
    def _():
        to_down.wait_recv()

    @pl.when(t == 0)
    def _():
        fx[0:3] = jnp.zeros((3, 192, 256), BF16)

    @pl.when(has_down)
    def _():
        to_up.wait_recv()

    @pl.when(t == 31)
    def _():
        fx[11:14] = jnp.zeros((3, 192, 256), BF16)

    def conv_halo(g, _):
        for r, slot in HALO_SLOTS:
            spread(fx[r, rows16(g), :], slot, g, xh)
        v = jnp.dot(taps_h[g], xh[g], preferred_element_type=F32)
        for i in (0, 1, 2, 5, 6, 7):
            zf[i, rows16(g), :] += v[i * 16 : i * 16 + 16, :]
        return 0

    lax.fori_loop(0, 12, conv_halo, 0)

    lax.fori_loop(0, 6, norm, 0)
    lax.fori_loop(10, 16, norm, 0)

    def stage0(f):
        pay[f] = gw[1 - core, f].astype(BF16)
        core_copy(f).start()

    def core_copy(f):
        return remote(pay.at[f], r0.at[f], ar_send.at[f, 0], ar_recv.at[f, 0], partner, t)

    def y_copies(f):
        return [
            remote(s1b.at[f, pl.ds(((y + d + 1) % 4) * 48, 48)], r1.at[f, d], ar_send.at[f, 1 + d], ar_recv.at[f, 1 + d], *y_peers[d])
            for d in range(3)
        ]

    def x_copies(f):
        return [
            remote(s2.at[f, (x + d + 1) % 4], r2.at[f, d], ar_send.at[f, 4 + d], ar_recv.at[f, 4 + d], *x_peers[d]) for d in range(3)
        ]

    def z_copies(f):
        return [remote(rz.at[f, z], rz.at[f, z], ar_send.at[f, 7 + d], ar_recv.at[f, 7 + d], *z_peers[d]) for d in range(3)]

    def x_back(f):
        return [remote(fa.at[f, x], fa.at[f, x], ar_send.at[f, 10 + d], ar_recv.at[f, 10 + d], *x_peers[d]) for d in range(3)]

    def y_back(f):
        mine = full.at[f, core, pl.ds(y * 48, 48)]
        return [remote(mine, mine, ar_send.at[f, 13 + d], ar_recv.at[f, 13 + d], *y_peers[d]) for d in range(3)]

    def core_back(f):
        return remote(full.at[f, core], full.at[f, core], ar_send.at[f, 16], ar_recv.at[f, 16], partner, t)

    def stage1(f):
        core_copy(f).wait()
        total = gw[core, f] + r0[f].astype(F32)
        s1f[f] = total
        s1b[f] = total.astype(BF16)
        for c in y_copies(f):
            c.start()

    def stage2(f):
        for c in y_copies(f):
            c.wait()
        total = s1f[f, pl.ds(y * 48, 48), :]
        for d in range(3):
            total = total + r1[f, d].astype(F32)
        for part in range(4):
            at, ln = part % 2 * 24, part // 2 * 128
            s2[f, part] = total[at : at + 24, ln : ln + 128]
        for c in x_copies(f):
            c.start()

    def stage3(f):
        for c in x_copies(f):
            c.wait()
        rz[f, z] = (s2[f, x] + r2[f, 0]) + (r2[f, 1] + r2[f, 2])
        for c in z_copies(f):
            c.start()

    def stage4(f):
        for c in z_copies(f):
            c.wait()
        fa[f, x] = (rz[f, 0] + rz[f, 1]) + (rz[f, 2] + rz[f, 3])
        for c in x_back(f):
            c.start()

    def stage5(f):
        for c in x_back(f):
            c.wait()
        rows = [jnp.concatenate([fa[f, part], fa[f, part + 2]], axis=1) for part in range(2)]
        full[f, core, pl.ds(pl.multiple_of(y * 48, 16), 48), :] = jnp.concatenate(rows, axis=0).astype(BF16)
        for c in y_back(f):
            c.start()

    def stage6(f):
        for c in y_back(f):
            c.wait()
        core_back(f).start()

    def stage7(f):
        core_back(f).wait()
        full_out(f).start()

    def full_out(f):
        return pltpu.make_async_copy(full.at[f], out_full.at[f], out_sem.at[2 + f])

    def finish(n, _):
        i = n // 2
        ln = pl.ds(pl.multiple_of(n % 2 * 128, 128), 128)
        gn = nsum[i, :, ln] * par[1, 0:192, :]
        u = zf[i, :, ln]
        m1 = jnp.sum(gn, axis=0, keepdims=True) * (1.0 / 192)
        m2 = jnp.sum(gn * u, axis=0, keepdims=True) * (1.0 / 192)
        gzs[i, :, ln] = (rinv[i, 0:1, ln] * (gn - m1 - u * m2)).astype(BF16)
        return 0

    def finish_out(n, _):
        i = n // 2
        ln = pl.ds(pl.multiple_of(n % 2 * 128, 128), 128)
        branch = osum[i, :, ln] + par[3, 0:192, :]
        outs[i, :, ln] = (fx[i + 3, :, ln].astype(F32) + par[4, 0:192, :] * branch).astype(BF16)
        return 0

    gz_up = [remote(gzs.at[n], halo.at[1, n], halo_send.at[2 + n], halo_recv.at[2 + n], s, up) for n in range(3)]
    gz_down = [remote(gzs.at[7 - n], halo.at[0, 2 - n], halo_send.at[5 + n], halo_recv.at[5 + n], s, down) for n in range(3)]

    def send_row(n):
        @pl.when(has_up)
        def _():
            gz_up[n].start()

        @pl.when(has_down)
        def _():
            gz_down[n].start()

    def mlp_outer(k, _):
        mlp_pair(k, 0)
        return 0

    lax.fori_loop(0, 3, mlp_outer, 0)
    lax.fori_loop(0, 2, finish, 0)
    lax.fori_loop(14, 16, finish, 0)
    send_row(0)
    after = {1: [(stage0, 0)], 3: [(stage0, 1), (stage1, 0)], 5: [(stage0, 2), (stage1, 1)]}

    def mlp(k, _):
        mlp_pair(k // 2, 1 + k % 2)
        for at, steps in after.items():

            @pl.when(k == at)
            def _():
                for step, chunk in steps:
                    step(chunk)

        return 0

    lax.fori_loop(0, 6, mlp, 0)
    lax.fori_loop(2, 14, finish, 0)
    stage1(2)
    stage2(0)
    send_row(1)

    lane = lax.broadcasted_iota(jnp.int32, (8, 128), 1)
    sub = lax.broadcasted_iota(jnp.int32, (8, 128), 0)

    def taps_grad(g, _):
        mine = jnp.concatenate([gzs[i, rows16(g), :] for i in range(8)], axis=0)
        for b in range(7):
            rows = pl.ds(b * 128, 128)
            pairs = lax.dot_general(mine, jnp.concatenate([xs[g, rows, :], xh[g, rows, :]], axis=0), NT, preferred_element_type=F32)
            at_own, at_halo = pairs[:, 0:128], pairs[:, 128:256]
            total = jnp.zeros((8, 128), F32)
            for i in range(8):
                use_own, use_halo = valid(i, lane)
                v = jnp.zeros((8, 128), F32)
                for h in range(2):
                    at = i * 16 + h * 8
                    same = lane % 16 == sub + h * 8
                    v = jnp.where(same & use_own, at_own[at : at + 8], v)
                    if not 3 <= i < 5:
                        v = jnp.where(same & use_halo, at_halo[at : at + 8], v)
                total = total + (pltpu.roll(v, (3 - i) * 16 % 128, 1) if i != 3 else v)
            gkr[pl.ds(g * 8 + b, 1), :] = jnp.sum(total, axis=0, keepdims=True)
        return 0

    gkr[...] = jnp.zeros_like(gkr)
    def taps_step(g, _):
        taps_grad(g, 0)

        @pl.when(g == 4)
        def _():
            stage2(1)
            stage3(0)
            send_row(2)

        @pl.when(g == 8)
        def _():
            stage2(2)
            stage3(1)

        return 0

    lax.fori_loop(0, 12, taps_step, 0)

    other = pl.ds((1 - core) * 48, 48)
    own_half = pl.ds(core * 48, 48)
    k_core = remote(gkr.at[other], k0, k_send.at[0], k_recv.at[0], partner, t)
    k_core.start()
    stage3(2)
    stage4(0)
    lax.fori_loop(0, 16, finish_out, 0)
    block_out = pltpu.make_async_copy(outs, out_block.at[0, 0], out_sem.at[0])
    block_out.start()

    def back_own(g, _):
        for i in range(8):
            spread(gzs[i, rows16(g), :], i, g, gs)
        v = jnp.dot(back[g], gs[g], preferred_element_type=F32)
        for i in range(8):
            zf[i, rows16(g), :] = ct[i, rows16(g), :].astype(F32) + v[i * 16 : i * 16 + 16, :]
        return 0

    k_core.wait()
    ky[y] = gkr[own_half, :] + k0[...]
    ky_copies = [remote(ky.at[y], ky.at[y], k_send.at[1 + d], k_recv.at[1 + d], *y_peers[d]) for d in range(3)]
    for c in ky_copies:
        c.start()
    build_taps(dwk, flat, back, back_h, True)
    stage4(1)
    stage5(0)
    stage4(2)
    lax.fori_loop(0, 4, back_own, 0)
    for c in ky_copies:
        c.wait()
    kx[x] = (ky[0] + ky[1]) + (ky[2] + ky[3])
    kx_copies = [remote(kx.at[x], kx.at[x], k_send.at[4 + d], k_recv.at[4 + d], *x_peers[d]) for d in range(3)]
    for c in kx_copies:
        c.start()
    stage5(1)
    stage5(2)
    stage6(0)
    lax.fori_loop(4, 12, back_own, 0)
    for c in kx_copies:
        c.wait()
    kz[z] = (kx[0] + kx[1]) + (kx[2] + kx[3])
    kz_copies = [remote(kz.at[z], kz.at[z], k_send.at[7 + d], k_recv.at[7 + d], *z_peers[d]) for d in range(3)]
    for c in kz_copies:
        c.start()
    stage6(1)
    stage6(2)
    stage7(0)
    stage7(1)

    @pl.when(has_up)
    def _():
        for c in gz_down:
            c.wait_recv()

    @pl.when(t == 0)
    def _():
        halo[0] = jnp.zeros((3, 192, 256), BF16)

    @pl.when(has_down)
    def _():
        for c in gz_up:
            c.wait_recv()

    @pl.when(t == 31)
    def _():
        halo[1] = jnp.zeros((3, 192, 256), BF16)

    def back_halo(g, _):
        for r, slot in HALO_SLOTS:
            spread(halo[r // 8, r % 11, rows16(g), :], slot, g, gh_)
        v = jnp.dot(back_h[g], gh_[g], preferred_element_type=F32)
        for i in range(8):
            fx[i, rows16(g), :] = (zf[i, rows16(g), :] + v[i * 16 : i * 16 + 16, :]).astype(BF16)
        return 0

    def back_step(g, _):
        back_halo(g, 0)

        @pl.when(g == 5)
        def _():
            for c in kz_copies:
                c.wait()
            kfull[own_half, :] = (kz[0] + kz[1]) + (kz[2] + kz[3])
            k_back.start()

        return 0

    k_back = remote(kfull.at[own_half], kfull.at[own_half], k_send.at[10], k_recv.at[10], partner, t)
    lax.fori_loop(0, 12, back_step, 0)
    gin_out = pltpu.make_async_copy(fx.at[pl.ds(0, 8)], out_gin.at[0, 0], out_sem.at[1])
    gin_out.start()
    stage7(2)
    k_back.wait()
    for a in range(7):
        for tile, width in ((0, 128), (128, 64)):
            base = jnp.zeros((8, 128), F32)
            for g in range(tile // 16, (tile + width) // 16):
                at = g % 8 * 16
                v = pltpu.roll(kfull[g * 8 : g * 8 + 8, :], (at - a * 16) % 128, 1)
                base = jnp.where((lane >= at) & (lane < at + 16), v, base)
            out_gk[a, :, tile : tile + width] = base[0:7, 0:width] * PIXEL_SCALE

    @pl.when(has_up)
    def _():
        to_up.wait_send()
        for c in gz_up:
            c.wait_send()

    @pl.when(has_down)
    def _():
        to_down.wait_send()
        for c in gz_down:
            c.wait_send()

    block_out.wait()
    gin_out.wait()
    for f in range(3):
        full_out(f).wait()


def hand_over_kernel(
    block, gin, full, gk, out_block, out_gin, out_gk, out_gwi, out_gwoT, h_block, h_gin, h_gk, h_full, h_gwi, h_gwoT, sems
):
    plain = ((block, h_block, out_block), (gin, h_gin, out_gin), (gk, h_gk, out_gk))
    load = pltpu.make_async_copy(full, h_full, sems.at[0, 3])
    load.start()
    loads = [pltpu.make_async_copy(i, h, sems.at[0, n]) for n, (i, h, o) in enumerate(plain)]
    stores = [pltpu.make_async_copy(h, o, sems.at[1, n]) for n, (i, h, o) in enumerate(plain)]
    for c in loads:
        c.start()
    load.wait()
    for m, (held, out) in enumerate(((h_gwi, out_gwi), (h_gwoT, out_gwoT))):
        for f in range(3):
            held[:, f * 256 : f * 256 + 256] = h_full[f, m].astype(F32) * PIXEL_SCALE
        stores.append(pltpu.make_async_copy(held, out, sems.at[1, 3 + m]))
        stores[-1].start()
    for c, store in zip(loads, stores):
        c.wait()
        store.start()
    for c in stores:
        c.wait()


def hand_over(block, gin, full, gk):
    like = lambda v: jax.ShapeDtypeStruct(v.shape, v.dtype)
    weights = jax.ShapeDtypeStruct((192, 768), F32)
    shapes = (like(block), like(gin), like(gk), weights, weights)
    return pl.pallas_call(
        hand_over_kernel,
        out_shape=shapes,
        in_specs=[pl.BlockSpec(memory_space=pl.ANY)] * 4,
        out_specs=(pl.BlockSpec(memory_space=pl.ANY),) * 5,
        scratch_shapes=[pltpu.VMEM(v.shape, v.dtype) for v in (block, gin, gk, full, weights, weights)]
        + [pltpu.SemaphoreType.DMA((2, 5))],
    )(block, gin, full, gk)


def on_device(features, dw_kernel, dw_bias, ln_gain, ln_bias, w_in, b_in, w_out, b_out, layer_scale, cotangent):
    row = lambda v: v.reshape(1, -1)
    turn = lambda v: jnp.swapaxes(v, 3, 4)
    any_, vmem = pl.BlockSpec(memory_space=pl.ANY), pl.BlockSpec(memory_space=pltpu.VMEM)
    V, DMA = pltpu.VMEM, pltpu.SemaphoreType.DMA
    groups = V((12, 896, 256), BF16)
    tables = V((12, 128, 896), BF16)
    scratch = [
        V((14, 192, 256), BF16), V((8, 192, 256), BF16), groups, groups, groups, groups, tables, tables, tables, tables,
        V((19, 8, 256), F32), V((8, 192, 256), F32), V((5, 256, 128), F32), V((768, 128), F32), V((768, 192), BF16),
        V((768, 192), BF16), V((8, 192, 256), BF16),
        V((8, 192, 256), BF16), V((8, 8, 256), F32), V((8, 192, 256), F32), V((8, 192, 256), F32), V((8, 192, 256), BF16),
        V((8, 192, 256), BF16), V((2, 3, 192, 256), F32), V((96, 128), F32), V((2, 3, 192, 256), BF16),
        V((3, 192, 256), BF16), V((3, 192, 256), BF16), V((3, 192, 256), F32), V((3, 192, 256), BF16), V((3, 3, 48, 256), BF16),
        V((3, 4, 24, 128), F32), V((3, 3, 24, 128), F32), V((3, 4, 24, 128), F32), V((3, 4, 24, 128), F32), V((3, 2, 192, 256), BF16),
        V((48, 128), F32), V((4, 48, 128), F32), V((4, 48, 128), F32), V((4, 48, 128), F32), V((96, 128), F32),
        DMA((2,)), DMA((5,)), DMA((8,)), DMA((8,)), DMA((3, 17)), DMA((3, 17)), DMA((11,)), DMA((11,)),
    ]
    values = pl.pallas_call(
        kernel,
        out_shape=(
            jax.ShapeDtypeStruct((1, 1, 8, 192, 256), BF16), jax.ShapeDtypeStruct((1, 1, 8, 192, 256), BF16),
            jax.ShapeDtypeStruct((3, 2, 192, 256), BF16), jax.ShapeDtypeStruct((7, 7, 192), F32),
        ),
        in_specs=[any_, any_] + [vmem] * 9,
        out_specs=(any_, any_, any_, vmem),
        scratch_shapes=scratch,
        compiler_params=pltpu.CompilerParams(collective_id=0, has_side_effects=True, vmem_limit_bytes=60 << 20),
    )(
        turn(features), turn(cotangent), dw_kernel, row(dw_bias), row(ln_gain), row(ln_bias), w_in, b_in, w_out.T, row(b_out),
        row(layer_scale),
    )
    block, gin, gk, gwi, gwoT = hand_over(*values)
    return turn(block), turn(gin), gwi, gwoT.T, gk


def solution(mesh):
    split, whole = P("slide", "space", None, None, None), P()
    return jax.shard_map(
        on_device,
        mesh=mesh,
        in_specs=(split,) + (whole,) * 9 + (split,),
        out_specs=(split, split, whole, whole, whole),
        check_vma=False,
    )
```

```python
import jax
import jax.numpy as jnp
from jax import lax
from jax.experimental import pallas as pl
from jax.experimental.pallas import tpu as pltpu
from jax.sharding import PartitionSpec as P

EPSILON = 1e-06
F32 = jnp.float32
BF16 = jnp.bfloat16
MESH = pl.DeviceIdType.MESH
PIXEL_SCALE = float(262144) ** (-0.5)
NT = (((1,), (1,)), ((), ()))


def remote(src, dst, send, recv, slide, space):
    return pltpu.make_async_remote_copy(
        src_ref=src, dst_ref=dst, send_sem=send, recv_sem=recv,
        device_id={"slide": slide, "space": space}, device_id_type=MESH,
    )


def gelu_parts(h):
    r = h * 0.7071067811865476
    cdf = 0.5 + 0.5 * lax.erf(r)
    density = jnp.exp2(r * r * -1.4426950408889634)
    return h * cdf, cdf + (h * 0.3989422804014327) * density


def spread(value, slot, group, dst):
    lane = lax.broadcasted_iota(jnp.int32, (16, 128), 1)
    left, right = value[:, 0:128], value[:, 128:256]
    none = jnp.zeros_like(left)
    for b in range(7):
        d = b - 3
        first, second = left, right
        if d:
            first, second = pltpu.roll(left, -d % 128, 1), pltpu.roll(right, -d % 128, 1)
            if d > 0:
                first, second = jnp.where(lane < 128 - d, first, second), jnp.where(lane < 128 - d, second, none)
            else:
                first, second = jnp.where(lane < -d, none, first), jnp.where(lane < -d, first, second)
        at = b * 128 + slot * 16
        dst[group, at : at + 16, 0:128] = first
        dst[group, at : at + 16, 128:256] = second


def valid(i, lane):
    slot = lane // 16
    own = (slot >= i - 3) & (slot <= i + 3)
    halo = jnp.zeros_like(own)
    if i < 3:
        halo = slot >= i + 5
    if i >= 5:
        halo = slot <= i - 5
    return own, halo


def build_taps(dwk, flat, own, halo, flip):
    lane8 = lax.broadcasted_iota(jnp.int32, (8, 128), 1)
    for a in range(7):
        flat[a, 0:7, 0:192] = jnp.concatenate(
            [dwk[6 - a if flip else a, (6 - b if flip else b) : (6 - b if flip else b) + 1, :] for b in range(7)], axis=0
        )
    for g in range(12):
        base = jnp.zeros((8, 128), F32)
        tile, at = g // 8 * 128, g % 8 * 16
        for a in range(7):
            v = flat[a, :, tile : tile + 128]
            v = pltpu.roll(v, (a * 16 - at) % 128, 1)
            base = jnp.where((lane8 >= a * 16) & (lane8 < a * 16 + 16), v, base)
        flat[7 + g, :, 0:128] = base
    lane = lax.broadcasted_iota(jnp.int32, (16, 128), 1)
    same = lane % 16 == lax.broadcasted_iota(jnp.int32, (16, 128), 0)

    def group(g, _):
        base = flat[7 + g, :, 0:128]
        for i in range(8):
            moved = pltpu.roll(base, (i - 3) * 16 % 128, 1)
            for keep, dst in zip(valid(i, lane8), (own, halo)):
                if dst is halo and 3 <= i < 5:
                    dst[g, i * 16 : i * 16 + 16, :] = jnp.zeros((16, 896), BF16)
                    continue
                v = jnp.where(keep, moved, 0.0)
                for b in range(7):
                    row = jnp.broadcast_to(v[b : b + 1, :], (16, 128))
                    dst[g, i * 16 : i * 16 + 16, b * 128 : b * 128 + 128] = jnp.where(same, row, 0.0).astype(BF16)
        return 0

    lax.fori_loop(0, 12, group, 0)


def both(v):
    return jnp.concatenate([v, v], axis=1)


def rows16(g):
    return pl.ds(pl.multiple_of(g * 16, 16), 16)


HALO_SLOTS = ((0, 5), (1, 6), (2, 7), (11, 0), (12, 1), (13, 2))


def kernel(
    feat, cot, dwk, dwb, gain, lbias, w_in, b_in, woutT, b_out, lscale,
    out_block, out_gin, out_full, out_gk,
    fx, ct, xs, xh, gs, gh_, taps, taps_h, back, back_h, flat, zf, par, bias, winT, wout, gout,
    nb, rinv, osum, nsum, outs, gzs, gw, gkr, halo,
    pay, r0, s1f, s1b, r1, s2, r2, rz, fa, full, k0, kx, ky, kz, kfull,
    in_sem, out_sem, halo_send, halo_recv, ar_send, ar_recv, k_send, k_recv,
):
    s, t = lax.axis_index("slide"), lax.axis_index("space")
    z_hi, core = s // 2, s % 2
    z_lo, x, y = t % 2, (t // 2) % 4, t // 8
    z = z_hi * 2 + z_lo
    partner = z_hi * 2 + (1 - core)
    x_peers = [(s, (y * 4 + (x + d) % 4) * 2 + z_lo) for d in (1, 2, 3)]
    y_peers = [(s, (((y + d) % 4) * 4 + x) * 2 + z_lo) for d in (1, 2, 3)]
    z_peers = [(((z + d) % 4) // 2 * 2 + core, (y * 4 + x) * 2 + ((z + d) % 4) % 2) for d in (1, 2, 3)]
    has_up, has_down = t > 0, t < 31
    up, down = jnp.maximum(t - 1, 0), jnp.minimum(t + 1, 31)

    own_in = pltpu.make_async_copy(feat.at[0, 0], fx.at[pl.ds(3, 8)], in_sem.at[0])
    own_in.start()
    cot_in = pltpu.make_async_copy(cot.at[0, 0], ct, in_sem.at[1])
    cot_in.start()

    barrier = pltpu.get_barrier_semaphore()
    for ps, pt in [(partner, t)] + x_peers + y_peers + z_peers:
        pl.semaphore_signal(barrier, inc=1, device_id={"slide": ps, "space": pt}, device_id_type=MESH)

    @pl.when(has_up)
    def _():
        pl.semaphore_signal(barrier, inc=1, device_id={"slide": s, "space": up}, device_id_type=MESH)

    @pl.when(has_down)
    def _():
        pl.semaphore_signal(barrier, inc=1, device_id={"slide": s, "space": down}, device_id_type=MESH)

    pl.semaphore_wait(barrier, 10 + jnp.minimum(t, 1) + jnp.minimum(31 - t, 1))

    to_up = remote(feat.at[0, 0, pl.ds(0, 3)], fx.at[pl.ds(11, 3)], halo_send.at[0], halo_recv.at[0], s, up)
    to_down = remote(feat.at[0, 0, pl.ds(5, 3)], fx.at[pl.ds(0, 3)], halo_send.at[1], halo_recv.at[1], s, down)

    @pl.when(has_up)
    def _():
        to_up.start()

    @pl.when(has_down)
    def _():
        to_down.start()

    for n, ref in enumerate((dwb, gain, lbias, b_out, lscale)):
        par[n, 0:128, :] = jnp.broadcast_to(ref[:, 0:128], (128, 128)).T
        par[n, 128:256, :] = jnp.broadcast_to(both(ref[:, 128:192]), (128, 128)).T
    for n in range(6):
        bias[n * 128 : n * 128 + 128, :] = jnp.broadcast_to(b_in[n * 128 : n * 128 + 128].reshape(1, 128), (128, 128)).T
    winT[...] = w_in[...].T
    wout[...] = woutT[...].T
    build_taps(dwk, flat, taps, taps_h, False)

    def clear(g, _):
        none = jnp.zeros((32, 256), BF16)
        for b in range(7):
            xh[g, b * 128 + 48 : b * 128 + 80, :] = none
            gh_[g, b * 128 + 48 : b * 128 + 80, :] = none
        return 0

    lax.fori_loop(0, 12, clear, 0)
    own_in.wait()

    def conv_own(g, _):
        for i in range(8):
            spread(fx[i + 3, rows16(g), :], i, g, xs)
        v = jnp.dot(taps[g], xs[g], preferred_element_type=F32)
        for i in range(8):
            zf[i, rows16(g), :] = v[i * 16 : i * 16 + 16, :] + both(par[0, rows16(g), :])
        return 0

    lax.fori_loop(0, 12, conv_own, 0)
    cot_in.wait()

    def scale_row(i, _):
        gout[i] = (both(par[4, 0:192, :]) * ct[i].astype(F32)).astype(BF16)
        return 0

    lax.fori_loop(0, 8, scale_row, 0)

    def norm(n, _):
        i = n // 2
        ln = pl.ds(pl.multiple_of(n % 2 * 128, 128), 128)
        v = zf[i, :, ln]
        v = v - jnp.sum(v, axis=0, keepdims=True) * (1.0 / 192)
        var = jnp.sum(v * v, axis=0, keepdims=True) * (1.0 / 192)
        r = lax.rsqrt(var + EPSILON)
        v = v * r
        zf[i, :, ln] = v
        rinv[i, :, ln] = jnp.broadcast_to(r, (8, 128))
        nb[i, :, ln] = (v * par[1, 0:192, :] + par[2, 0:192, :]).astype(BF16)
        return 0

    lax.fori_loop(6, 10, norm, 0)

    gw[...] = jnp.zeros_like(gw)
    osum[...] = jnp.zeros_like(osum)
    nsum[...] = jnp.zeros_like(nsum)

    def mlp_pair(f, p):
        units = pl.ds(pl.multiple_of(f * 256, 256), 256)
        q = 7 - p
        normed = jnp.concatenate([nb[p], nb[q]], axis=1)
        upper = jnp.concatenate([gout[p], gout[q]], axis=1)
        hidden = jnp.dot(winT[units, :], normed, preferred_element_type=F32) + both(both(bias[units, :]))
        value, slope = gelu_parts(hidden)
        act = value.astype(BF16)
        gh = (jnp.dot(wout[units, :], upper, preferred_element_type=F32) * slope).astype(BF16)
        out = jnp.dot(woutT[:, units], act, preferred_element_type=F32)
        osum[p] += out[:, 0:256]
        osum[q] += out[:, 256:512]
        out = jnp.dot(w_in[:, units], gh, preferred_element_type=F32)
        nsum[p] += out[:, 0:256]
        nsum[q] += out[:, 256:512]
        gw[0, f] += lax.dot_general(normed, gh, NT, preferred_element_type=F32)
        gw[1, f] += lax.dot_general(upper, act, NT, preferred_element_type=F32)

    def mlp_inner(k, _):
        mlp_pair(k, 3)
        return 0

    lax.fori_loop(0, 3, mlp_inner, 0)

    @pl.when(has_up)
    def _():
        to_down.wait_recv()

    @pl.when(t == 0)
    def _():
        fx[0:3] = jnp.zeros((3, 192, 256), BF16)

    @pl.when(has_down)
    def _():
        to_up.wait_recv()

    @pl.when(t == 31)
    def _():
        fx[11:14] = jnp.zeros((3, 192, 256), BF16)

    def conv_halo(g, _):
        for r, slot in HALO_SLOTS:
            spread(fx[r, rows16(g), :], slot, g, xh)
        v = jnp.dot(taps_h[g], xh[g], preferred_element_type=F32)
        for i in (0, 1, 2, 5, 6, 7):
            zf[i, rows16(g), :] += v[i * 16 : i * 16 + 16, :]
        return 0

    lax.fori_loop(0, 12, conv_halo, 0)

    lax.fori_loop(0, 6, norm, 0)
    lax.fori_loop(10, 16, norm, 0)

    def stage0(f):
        pay[f] = gw[1 - core, f].astype(BF16)
        core_copy(f).start()

    def core_copy(f):
        return remote(pay.at[f], r0.at[f], ar_send.at[f, 0], ar_recv.at[f, 0], partner, t)

    def y_copies(f):
        return [
            remote(s1b.at[f, pl.ds(((y + d + 1) % 4) * 48, 48)], r1.at[f, d], ar_send.at[f, 1 + d], ar_recv.at[f, 1 + d], *y_peers[d])
            for d in range(3)
        ]

    def x_copies(f):
        return [
            remote(s2.at[f, (x + d + 1) % 4], r2.at[f, d], ar_send.at[f, 4 + d], ar_recv.at[f, 4 + d], *x_peers[d]) for d in range(3)
        ]

    def z_copies(f):
        return [remote(rz.at[f, z], rz.at[f, z], ar_send.at[f, 7 + d], ar_recv.at[f, 7 + d], *z_peers[d]) for d in range(3)]

    def x_back(f):
        return [remote(fa.at[f, x], fa.at[f, x], ar_send.at[f, 10 + d], ar_recv.at[f, 10 + d], *x_peers[d]) for d in range(3)]

    def y_back(f):
        mine = full.at[f, core, pl.ds(y * 48, 48)]
        return [remote(mine, mine, ar_send.at[f, 13 + d], ar_recv.at[f, 13 + d], *y_peers[d]) for d in range(3)]

    def core_back(f):
        return remote(full.at[f, core], full.at[f, core], ar_send.at[f, 16], ar_recv.at[f, 16], partner, t)

    def stage1(f):
        core_copy(f).wait()
        total = gw[core, f] + r0[f].astype(F32)
        s1f[f] = total
        s1b[f] = total.astype(BF16)
        for c in y_copies(f):
            c.start()

    def stage2(f):
        for c in y_copies(f):
            c.wait()
        total = s1f[f, pl.ds(y * 48, 48), :]
        for d in range(3):
            total = total + r1[f, d].astype(F32)
        for part in range(4):
            at, ln = part % 2 * 24, part // 2 * 128
            s2[f, part] = total[at : at + 24, ln : ln + 128]
        for c in x_copies(f):
            c.start()

    def stage3(f):
        for c in x_copies(f):
            c.wait()
        rz[f, z] = (s2[f, x] + r2[f, 0]) + (r2[f, 1] + r2[f, 2])
        for c in z_copies(f):
            c.start()

    def stage4(f):
        for c in z_copies(f):
            c.wait()
        fa[f, x] = (rz[f, 0] + rz[f, 1]) + (rz[f, 2] + rz[f, 3])
        for c in x_back(f):
            c.start()

    def stage5(f):
        for c in x_back(f):
            c.wait()
        rows = [jnp.concatenate([fa[f, part], fa[f, part + 2]], axis=1) for part in range(2)]
        full[f, core, pl.ds(pl.multiple_of(y * 48, 16), 48), :] = jnp.concatenate(rows, axis=0).astype(BF16)
        for c in y_back(f):
            c.start()

    def stage6(f):
        for c in y_back(f):
            c.wait()
        core_back(f).start()

    def stage7(f):
        core_back(f).wait()
        full_out(f).start()

    def full_out(f):
        return pltpu.make_async_copy(full.at[f], out_full.at[f], out_sem.at[2 + f])

    def finish(n, _):
        i = n // 2
        ln = pl.ds(pl.multiple_of(n % 2 * 128, 128), 128)
        gn = nsum[i, :, ln] * par[1, 0:192, :]
        u = zf[i, :, ln]
        m1 = jnp.sum(gn, axis=0, keepdims=True) * (1.0 / 192)
        m2 = jnp.sum(gn * u, axis=0, keepdims=True) * (1.0 / 192)
        gzs[i, :, ln] = (rinv[i, 0:1, ln] * (gn - m1 - u * m2)).astype(BF16)
        return 0

    def finish_out(n, _):
        i = n // 2
        ln = pl.ds(pl.multiple_of(n % 2 * 128, 128), 128)
        branch = osum[i, :, ln] + par[3, 0:192, :]
        outs[i, :, ln] = (fx[i + 3, :, ln].astype(F32) + par[4, 0:192, :] * branch).astype(BF16)
        return 0

    gz_up = [remote(gzs.at[n], halo.at[1, n], halo_send.at[2 + n], halo_recv.at[2 + n], s, up) for n in range(3)]
    gz_down = [remote(gzs.at[7 - n], halo.at[0, 2 - n], halo_send.at[5 + n], halo_recv.at[5 + n], s, down) for n in range(3)]

    def send_row(n):
        @pl.when(has_up)
        def _():
            gz_up[n].start()

        @pl.when(has_down)
        def _():
            gz_down[n].start()

    def mlp_outer(k, _):
        mlp_pair(k, 0)
        return 0

    lax.fori_loop(0, 3, mlp_outer, 0)
    lax.fori_loop(0, 2, finish, 0)
    lax.fori_loop(14, 16, finish, 0)
    send_row(0)
    after = {1: [(stage0, 0)], 3: [(stage0, 1), (stage1, 0)], 5: [(stage0, 2), (stage1, 1)]}

    def mlp(k, _):
        mlp_pair(k // 2, 1 + k % 2)
        for at, steps in after.items():

            @pl.when(k == at)
            def _():
                for step, chunk in steps:
                    step(chunk)

        return 0

    lax.fori_loop(0, 6, mlp, 0)
    lax.fori_loop(2, 4, finish, 0)
    lax.fori_loop(12, 14, finish, 0)
    stage1(2)
    stage2(0)
    send_row(1)
    lax.fori_loop(4, 12, finish, 0)

    lane = lax.broadcasted_iota(jnp.int32, (8, 128), 1)
    sub = lax.broadcasted_iota(jnp.int32, (8, 128), 0)

    def taps_grad(g, _):
        mine = jnp.concatenate([gzs[i, rows16(g), :] for i in range(8)], axis=0)
        for b in range(7):
            rows = pl.ds(b * 128, 128)
            pairs = lax.dot_general(mine, jnp.concatenate([xs[g, rows, :], xh[g, rows, :]], axis=0), NT, preferred_element_type=F32)
            at_own, at_halo = pairs[:, 0:128], pairs[:, 128:256]
            total = jnp.zeros((8, 128), F32)
            for i in range(8):
                use_own, use_halo = valid(i, lane)
                v = jnp.zeros((8, 128), F32)
                for h in range(2):
                    at = i * 16 + h * 8
                    same = lane % 16 == sub + h * 8
                    v = jnp.where(same & use_own, at_own[at : at + 8], v)
                    if not 3 <= i < 5:
                        v = jnp.where(same & use_halo, at_halo[at : at + 8], v)
                total = total + (pltpu.roll(v, (3 - i) * 16 % 128, 1) if i != 3 else v)
            gkr[pl.ds(g * 8 + b, 1), :] = jnp.sum(total, axis=0, keepdims=True)
        return 0

    gkr[...] = jnp.zeros_like(gkr)
    def taps_step(g, _):
        taps_grad(g, 0)

        @pl.when(g == 4)
        def _():
            stage2(1)
            stage3(0)
            send_row(2)

        @pl.when(g == 8)
        def _():
            stage2(2)
            stage3(1)

        return 0

    lax.fori_loop(0, 12, taps_step, 0)

    other = pl.ds((1 - core) * 48, 48)
    own_half = pl.ds(core * 48, 48)
    k_core = remote(gkr.at[other], k0, k_send.at[0], k_recv.at[0], partner, t)
    k_core.start()
    stage3(2)
    stage4(0)
    lax.fori_loop(0, 16, finish_out, 0)
    block_out = pltpu.make_async_copy(outs, out_block.at[0, 0], out_sem.at[0])
    block_out.start()

    def back_own(g, _):
        for i in range(8):
            spread(gzs[i, rows16(g), :], i, g, gs)
        v = jnp.dot(back[g], gs[g], preferred_element_type=F32)
        for i in range(8):
            zf[i, rows16(g), :] = ct[i, rows16(g), :].astype(F32) + v[i * 16 : i * 16 + 16, :]
        return 0

    k_core.wait()
    ky[y] = gkr[own_half, :] + k0[...]
    ky_copies = [remote(ky.at[y], ky.at[y], k_send.at[1 + d], k_recv.at[1 + d], *y_peers[d]) for d in range(3)]
    for c in ky_copies:
        c.start()
    build_taps(dwk, flat, back, back_h, True)
    stage4(1)
    stage5(0)
    stage4(2)
    lax.fori_loop(0, 4, back_own, 0)
    for c in ky_copies:
        c.wait()
    kx[x] = (ky[0] + ky[1]) + (ky[2] + ky[3])
    kx_copies = [remote(kx.at[x], kx.at[x], k_send.at[4 + d], k_recv.at[4 + d], *x_peers[d]) for d in range(3)]
    for c in kx_copies:
        c.start()
    stage5(1)
    stage5(2)
    stage6(0)
    lax.fori_loop(4, 12, back_own, 0)
    for c in kx_copies:
        c.wait()
    kz[z] = (kx[0] + kx[1]) + (kx[2] + kx[3])
    kz_copies = [remote(kz.at[z], kz.at[z], k_send.at[7 + d], k_recv.at[7 + d], *z_peers[d]) for d in range(3)]
    for c in kz_copies:
        c.start()
    stage6(1)
    stage6(2)
    stage7(0)
    stage7(1)

    @pl.when(has_up)
    def _():
        for c in gz_down:
            c.wait_recv()

    @pl.when(t == 0)
    def _():
        halo[0] = jnp.zeros((3, 192, 256), BF16)

    @pl.when(has_down)
    def _():
        for c in gz_up:
            c.wait_recv()

    @pl.when(t == 31)
    def _():
        halo[1] = jnp.zeros((3, 192, 256), BF16)

    def back_halo(g, _):
        for r, slot in HALO_SLOTS:
            spread(halo[r // 8, r % 11, rows16(g), :], slot, g, gh_)
        v = jnp.dot(back_h[g], gh_[g], preferred_element_type=F32)
        for i in range(8):
            fx[i, rows16(g), :] = (zf[i, rows16(g), :] + v[i * 16 : i * 16 + 16, :]).astype(BF16)
        return 0

    def back_step(g, _):
        back_halo(g, 0)

        @pl.when(g == 5)
        def _():
            for c in kz_copies:
                c.wait()
            kfull[own_half, :] = (kz[0] + kz[1]) + (kz[2] + kz[3])
            k_back.start()

        return 0

    k_back = remote(kfull.at[own_half], kfull.at[own_half], k_send.at[10], k_recv.at[10], partner, t)
    lax.fori_loop(0, 12, back_step, 0)
    gin_out = pltpu.make_async_copy(fx.at[pl.ds(0, 8)], out_gin.at[0, 0], out_sem.at[1])
    gin_out.start()
    stage7(2)
    k_back.wait()
    for a in range(7):
        for tile, width in ((0, 128), (128, 64)):
            base = jnp.zeros((8, 128), F32)
            for g in range(tile // 16, (tile + width) // 16):
                at = g % 8 * 16
                v = pltpu.roll(kfull[g * 8 : g * 8 + 8, :], (at - a * 16) % 128, 1)
                base = jnp.where((lane >= at) & (lane < at + 16), v, base)
            out_gk[a, :, tile : tile + width] = base[0:7, 0:width] * PIXEL_SCALE

    @pl.when(has_up)
    def _():
        to_up.wait_send()
        for c in gz_up:
            c.wait_send()

    @pl.when(has_down)
    def _():
        to_down.wait_send()
        for c in gz_down:
            c.wait_send()

    block_out.wait()
    gin_out.wait()
    for f in range(3):
        full_out(f).wait()


def hand_over_kernel(
    block, gin, full, gk, out_block, out_gin, out_gk, out_gwi, out_gwoT, h_block, h_gin, h_gk, h_full, h_gwi, h_gwoT, sems
):
    plain = ((block, h_block, out_block), (gin, h_gin, out_gin), (gk, h_gk, out_gk))
    load = pltpu.make_async_copy(full, h_full, sems.at[0, 3])
    load.start()
    loads = [pltpu.make_async_copy(i, h, sems.at[0, n]) for n, (i, h, o) in enumerate(plain)]
    stores = [pltpu.make_async_copy(h, o, sems.at[1, n]) for n, (i, h, o) in enumerate(plain)]
    for c in loads:
        c.start()
    load.wait()
    for m, (held, out) in enumerate(((h_gwi, out_gwi), (h_gwoT, out_gwoT))):
        for f in range(3):
            held[:, f * 256 : f * 256 + 256] = h_full[f, m].astype(F32) * PIXEL_SCALE
        stores.append(pltpu.make_async_copy(held, out, sems.at[1, 3 + m]))
        stores[-1].start()
    for c, store in zip(loads, stores):
        c.wait()
        store.start()
    for c in stores:
        c.wait()


def hand_over(block, gin, full, gk):
    like = lambda v: jax.ShapeDtypeStruct(v.shape, v.dtype)
    weights = jax.ShapeDtypeStruct((192, 768), F32)
    shapes = (like(block), like(gin), like(gk), weights, weights)
    return pl.pallas_call(
        hand_over_kernel,
        out_shape=shapes,
        in_specs=[pl.BlockSpec(memory_space=pl.ANY)] * 4,
        out_specs=(pl.BlockSpec(memory_space=pl.ANY),) * 5,
        scratch_shapes=[pltpu.VMEM(v.shape, v.dtype) for v in (block, gin, gk, full, weights, weights)]
        + [pltpu.SemaphoreType.DMA((2, 5))],
    )(block, gin, full, gk)


def on_device(features, dw_kernel, dw_bias, ln_gain, ln_bias, w_in, b_in, w_out, b_out, layer_scale, cotangent):
    row = lambda v: v.reshape(1, -1)
    turn = lambda v: jnp.swapaxes(v, 3, 4)
    any_, vmem = pl.BlockSpec(memory_space=pl.ANY), pl.BlockSpec(memory_space=pltpu.VMEM)
    V, DMA = pltpu.VMEM, pltpu.SemaphoreType.DMA
    groups = V((12, 896, 256), BF16)
    tables = V((12, 128, 896), BF16)
    scratch = [
        V((14, 192, 256), BF16), V((8, 192, 256), BF16), groups, groups, groups, groups, tables, tables, tables, tables,
        V((19, 8, 256), F32), V((8, 192, 256), F32), V((5, 256, 128), F32), V((768, 128), F32), V((768, 192), BF16),
        V((768, 192), BF16), V((8, 192, 256), BF16),
        V((8, 192, 256), BF16), V((8, 8, 256), F32), V((8, 192, 256), F32), V((8, 192, 256), F32), V((8, 192, 256), BF16),
        V((8, 192, 256), BF16), V((2, 3, 192, 256), F32), V((96, 128), F32), V((2, 3, 192, 256), BF16),
        V((3, 192, 256), BF16), V((3, 192, 256), BF16), V((3, 192, 256), F32), V((3, 192, 256), BF16), V((3, 3, 48, 256), BF16),
        V((3, 4, 24, 128), F32), V((3, 3, 24, 128), F32), V((3, 4, 24, 128), F32), V((3, 4, 24, 128), F32), V((3, 2, 192, 256), BF16),
        V((48, 128), F32), V((4, 48, 128), F32), V((4, 48, 128), F32), V((4, 48, 128), F32), V((96, 128), F32),
        DMA((2,)), DMA((5,)), DMA((8,)), DMA((8,)), DMA((3, 17)), DMA((3, 17)), DMA((11,)), DMA((11,)),
    ]
    values = pl.pallas_call(
        kernel,
        out_shape=(
            jax.ShapeDtypeStruct((1, 1, 8, 192, 256), BF16), jax.ShapeDtypeStruct((1, 1, 8, 192, 256), BF16),
            jax.ShapeDtypeStruct((3, 2, 192, 256), BF16), jax.ShapeDtypeStruct((7, 7, 192), F32),
        ),
        in_specs=[any_, any_] + [vmem] * 9,
        out_specs=(any_, any_, any_, vmem),
        scratch_shapes=scratch,
        compiler_params=pltpu.CompilerParams(collective_id=0, has_side_effects=True, vmem_limit_bytes=60 << 20),
    )(
        turn(features), turn(cotangent), dw_kernel, row(dw_bias), row(ln_gain), row(ln_bias), w_in, b_in, w_out.T, row(b_out),
        row(layer_scale),
    )
    block, gin, gk, gwi, gwoT = hand_over(*values)
    return turn(block), turn(gin), gwi, gwoT.T, gk


def solution(mesh):
    split, whole = P("slide", "space", None, None, None), P()
    return jax.shard_map(
        on_device,
        mesh=mesh,
        in_specs=(split,) + (whole,) * 9 + (split,),
        out_specs=(split, split, whole, whole, whole),
        check_vma=False,
    )
```
